256 devices in a mesh: rows: 32 (over x, y, core), grp: 8 (over z).
Axes of the slice: x: 4, y: 4, z: 8, core: 2. Of those that a mesh axis runs over, the one named last changes fastest.
Arguments:
- pivot_columns: bfloat16 [128, 10240, 256], P('rows', 'grp'), may hold values from -6 to 6
- previous: bfloat16 [128, 10240, 512], P('rows', 'grp'), may hold values from -0.59765625 to 0.59765625
- pivots: int32 [256], replicated, may hold values from 0 to 1310719, as said below
- pivot_inverse: bfloat16 [256, 256], replicated, may hold values from -0.4 to 1.5
- orbitals: bfloat16 [10240, 1024], P('grp'), may hold values from -0.0625 to 0.0625
- slab_orbitals: bfloat16 [128, 1024], replicated, may hold values from -0.5 to 0.5
Outputs:
- new_vectors: bfloat16 [128, 10240, 256], P('rows', 'grp')
- mo_block: bfloat16 [256, 1024, 1024], P('rows', None, 'grp')
The draws below stay inside these ranges and needn't reach their ends.
Inputs may be any that keep to these rules, and one draw needn't show every extreme that they name: `pivots`: distinct entries.
All inputs are finite; a program needn't handle non-finite values.
Results may differ from the reference program's by a relative error of at most 0.0038.
The reference program's roundings to bfloat16 on the way (of `pivot_rows`, `residual_columns`, `upper` and `half`) count: a program that leaves them out, or rounds other values in their place, can miss the bound.
Values may be sent and summed in bfloat16 or wider, within the bound.
No kernel may reach another device: no remote copies, remote signals or barrier semaphores. Data moves between devices by JAX's collectives and lax.ppermute only.
A program may use at most 64 MiB of HBM per device.

```python
import jax
import jax.numpy as jnp

NBAS = 10240
NOCC = 1024
K_PREV = 512
NP = 256
MU = 128


def draw_pivots(key, part):
    chosen = jax.random.permutation(key, MU * NBAS)[:NP]
    return chosen.astype(jnp.int32)


def draw_pivot_inverse(key, part):
    first, second = jax.random.split(jax.random.fold_in(key, 17))
    spread = jax.random.normal(first, (NP, NP), jnp.float32) * NP ** (-0.5)
    spread = jnp.clip(spread, -0.39, 0.39)
    diagonal = jax.random.uniform(second, (NP,), jnp.float32, 0.5, 1.5)
    eye_mask = jnp.arange(NP)[:, None] == jnp.arange(NP)[None, :]
    return jnp.where(eye_mask, diagonal[None, :], spread).astype(jnp.bfloat16)


def shard_levels(key, dims, cuts, low, largest):
    loudness = 1.0
    for position, blocks in cuts:
        heights = jax.random.uniform(jax.random.fold_in(jax.random.fold_in(key, 6), position), (blocks,), jnp.float32, low / len(cuts), largest / len(cuts))
        loudness = loudness * jnp.repeat(jnp.exp(heights), dims[position] // blocks).reshape((-1,) + (1,) * (len(dims) - 1 - position))
    return loudness


def scatter_about(rng, dims, deviation, reach, shards=(), dtype=jnp.bfloat16):
    entries = deviation * jax.random.normal(rng, dims, jnp.float32)
    if shards:
        entries = entries * shard_levels(rng, dims, shards, -0.22, 0.18)
    return jnp.clip(entries, -reach, reach).astype(dtype)


def setup_inputs(seed: int = 0) -> dict:
    arg_keys = jax.random.split(jax.random.key(seed), 7)
    return {
        "pivot_columns": scatter_about(arg_keys[0], (MU, NBAS, NP), 1.0, 6.0, ((0, 32), (1, 8))),
        "previous": scatter_about(arg_keys[1], (MU, NBAS, K_PREV), 0.1, 0.59765625, ((0, 32), (1, 8))),
        "pivots": draw_pivots(jax.random.fold_in(arg_keys[6], 71), 0),
        "pivot_inverse": draw_pivot_inverse(jax.random.fold_in(arg_keys[6], 71), 0),
        "orbitals": scatter_about(arg_keys[4], (NBAS, NOCC), NBAS ** -0.5, 0.0625, ((0, 8),)),
        "slab_orbitals": scatter_about(arg_keys[5], (MU, NOCC), MU ** -0.5, 0.5),
    }


def reference(pivot_columns, previous, pivots, pivot_inverse, orbitals, slab_orbitals):
    prev_count = previous.shape[2]
    flat_prev = previous.reshape(MU * NBAS, prev_count)
    pivot_rows = jnp.take(flat_prev, pivots.astype(jnp.int32), axis=0)
    correction = jnp.dot(flat_prev, pivot_rows.T, preferred_element_type=jnp.float32)
    flat_columns = pivot_columns.reshape(MU * NBAS, NP)
    residual_columns = (flat_columns.astype(jnp.float32) - correction).astype(jnp.bfloat16)
    upper = jnp.triu(pivot_inverse)
    new_flat = jnp.dot(residual_columns, upper, preferred_element_type=jnp.float32).astype(jnp.bfloat16)
    new_vectors = new_flat.reshape(MU, NBAS, NP)
    by_second = jnp.transpose(new_vectors, (1, 0, 2)).reshape(NBAS, MU * NP)
    half = jnp.dot(orbitals.T, by_second, preferred_element_type=jnp.float32).astype(jnp.bfloat16)
    half = half.reshape(NOCC, MU, NP)
    by_first = jnp.transpose(half, (1, 0, 2)).reshape(MU, NOCC * NP)
    full = jnp.dot(slab_orbitals.T, by_first, preferred_element_type=jnp.float32).astype(jnp.bfloat16)
    mo_block = jnp.transpose(full.reshape(NOCC, NOCC, NP), (2, 0, 1))
    return new_vectors, mo_block
```

```python
import functools

import jax
import jax.numpy as jnp
from jax import lax
from jax.experimental import pallas as pl
from jax.experimental.pallas import tpu as pltpu
from jax.sharding import PartitionSpec as P

NBAS = 10240
F32 = jnp.float32
BF16 = jnp.bfloat16


def pick_kernel(base_ref, piv_ref, prev_ref, out_ref, acc_ref):
    m = pl.program_id(0)
    nu = prev_ref.shape[1]
    local = piv_ref[...] - (base_ref[0] + m * NBAS)
    hot = (local == lax.broadcasted_iota(jnp.int32, (local.shape[0], nu), 1)).astype(F32).astype(BF16)
    picked = jnp.dot(hot, prev_ref[0], preferred_element_type=F32)

    @pl.when(m == 0)
    def _():
        acc_ref[...] = picked

    @pl.when(m > 0)
    def _():
        acc_ref[...] += picked

    @pl.when(m == pl.num_programs(0) - 1)
    def _():
        out_ref[...] = acc_ref[...].astype(BF16)


def pick_rows(base, pivots, previous):
    mu, nu, k = previous.shape
    n = pivots.shape[0]
    return pl.pallas_call(
        pick_kernel,
        out_shape=jax.ShapeDtypeStruct((n, k), BF16),
        grid_spec=pltpu.PrefetchScalarGridSpec(
            num_scalar_prefetch=1,
            grid=(mu,),
            in_specs=[
                pl.BlockSpec((n, 1), lambda m, b: (0, 0)),
                pl.BlockSpec((1, nu, k), lambda m, b: (m, 0, 0)),
            ],
            out_specs=pl.BlockSpec((n, k), lambda m, b: (0, 0)),
            scratch_shapes=[pltpu.VMEM((n, k), F32)],
        ),
        cost_estimate=pl.CostEstimate(
            flops=2 * n * mu * nu * k, bytes_accessed=2 * mu * nu * k, transcendentals=0
        ),
        name="pick_rows",
    )(base, pivots.reshape(n, 1), previous)


def block_kernel(cols_ref, prev_ref, rows_ref, inv_ref, orb_ref, new_ref, part_ref):
    contract = (((1,), (1,)), ((), ()))
    correction = lax.dot_general(prev_ref[0], rows_ref[...], contract, preferred_element_type=F32)
    residual = (cols_ref[0].astype(F32) - correction).astype(BF16)
    inv = inv_ref[...]
    below = lax.broadcasted_iota(jnp.int32, inv.shape, 0) > lax.broadcasted_iota(jnp.int32, inv.shape, 1)
    upper = jnp.where(below, 0.0, inv.astype(F32)).astype(BF16)
    new = jnp.dot(residual, upper, preferred_element_type=F32).astype(BF16)
    new_ref[0] = new
    part = lax.dot_general(new, orb_ref[...], (((0,), (0,)), ((), ())), preferred_element_type=F32)
    owners, dests, _, keep, width = part_ref.shape
    for g in range(owners):
        part_ref[g, :, 0] = part[:, g * width : (g + 1) * width].reshape(dests, keep, width)


def block(pivot_columns, previous, rows, pivot_inverse, orbitals, owners, dests):
    mu, nu, k = previous.shape
    n = pivot_columns.shape[2]
    occ = orbitals.shape[1]
    part_shape = (owners, dests, mu, n // dests, occ // owners)
    return pl.pallas_call(
        block_kernel,
        grid=(mu,),
        out_shape=(
            jax.ShapeDtypeStruct((mu, nu, n), BF16),
            jax.ShapeDtypeStruct(part_shape, F32),
        ),
        in_specs=[
            pl.BlockSpec((1, nu, n), lambda m: (m, 0, 0)),
            pl.BlockSpec((1, nu, k), lambda m: (m, 0, 0)),
            pl.BlockSpec((n, k), lambda m: (0, 0)),
            pl.BlockSpec((n, n), lambda m: (0, 0)),
            pl.BlockSpec((nu, occ), lambda m: (0, 0)),
        ],
        out_specs=(
            pl.BlockSpec((1, nu, n), lambda m: (m, 0, 0)),
            pl.BlockSpec(part_shape[:2] + (1,) + part_shape[3:], lambda m: (0, 0, m, 0, 0)),
        ),
        compiler_params=pltpu.CompilerParams(vmem_limit_bytes=40 << 20),
        cost_estimate=pl.CostEstimate(
            flops=2 * mu * nu * n * (k + n + occ),
            bytes_accessed=2 * mu * nu * (k + 2 * n) + 4 * mu * n * occ,
            transcendentals=0,
        ),
        name="block",
    )(pivot_columns, previous, rows, pivot_inverse, orbitals)


def final_kernel(half_ref, slab_ref, out_ref, wide_ref):
    mu, keep, width = half_ref.shape
    wide_ref[...] = half_ref[...].astype(F32).reshape(mu * keep, width)
    slab_t = slab_ref[...].T
    for p in range(0, keep, 2):
        pair = [wide_ref[pl.ds(q, mu, stride=keep), :].astype(BF16) for q in (p, p + 1)]
        both = jnp.dot(slab_t, jnp.concatenate(pair, axis=1), preferred_element_type=F32)
        out_ref[p] = both[:, :width].astype(BF16)
        out_ref[p + 1] = both[:, width:].astype(BF16)


def final(half, slab):
    mu, keep, width = half.shape
    occ = slab.shape[1]
    return pl.pallas_call(
        final_kernel,
        out_shape=jax.ShapeDtypeStruct((keep, occ, width), BF16),
        scratch_shapes=[pltpu.VMEM((mu * keep, width), F32)],
        compiler_params=pltpu.CompilerParams(vmem_limit_bytes=32 << 20),
        cost_estimate=pl.CostEstimate(
            flops=2 * mu * keep * width * occ,
            bytes_accessed=2 * keep * width * (mu + occ),
            transcendentals=0,
        ),
        name="final",
    )(half, slab)


def exchange(x, axis):
    return lax.all_to_all(x, axis, split_axis=0, concat_axis=0, tiled=True)


def sum_rows(x):
    return jnp.sum(x.astype(F32), axis=0).astype(BF16)


def per_device(n_rows, n_grp, pivot_columns, previous, pivots, pivot_inverse, orbitals, slab_orbitals):
    mu, nu, k = previous.shape
    n = pivot_columns.shape[2]
    base = lax.axis_index("rows") * (mu * NBAS) + lax.axis_index("grp") * nu
    picked = pick_rows(base.reshape(1).astype(jnp.int32), pivots, previous)
    mine = sum_rows(exchange(picked.reshape(n_rows, n // n_rows, k), "rows"))
    mine = sum_rows(exchange(jnp.broadcast_to(mine, (n_grp,) + mine.shape), "grp"))
    rows = exchange(jnp.broadcast_to(mine, (n_rows,) + mine.shape), "rows").reshape(n, k)
    new_vectors, part = block(
        pivot_columns, previous, rows, pivot_inverse, orbitals, n_grp, n_rows
    )
    width = part.shape[-1]
    half = lax.psum_scatter(part.reshape(-1, width), "grp", scatter_dimension=0, tiled=True)
    half = half.astype(BF16).reshape(part.shape[1:])
    half = exchange(half, "rows").reshape(n_rows * mu, n // n_rows, width)
    return new_vectors, final(half, slab_orbitals)


def solution(mesh):
    in_specs = (P("rows", "grp", None), P("rows", "grp", None), P(), P(), P("grp", None), P())
    out_specs = (P("rows", "grp", None), P("rows", None, "grp"))
    body = functools.partial(per_device, mesh.shape["rows"], mesh.shape["grp"])
    return jax.shard_map(body, mesh=mesh, in_specs=in_specs, out_specs=out_specs, check_vma=False)
```

```python
import functools

import jax
import jax.numpy as jnp
from jax import lax
from jax.experimental import pallas as pl
from jax.experimental.pallas import tpu as pltpu
from jax.sharding import PartitionSpec as P

NBAS = 10240
F32 = jnp.float32
BF16 = jnp.bfloat16
STREAMS = 2


def pick_kernel(base_ref, piv_ref, prev_ref, out_ref, acc_ref, slots, sems, where_ref):
    mu, nu, _ = prev_ref.shape
    depth, group, _ = slots.shape
    n = acc_ref.shape[0]
    acc_ref[...] = jnp.zeros_like(acc_ref)
    offset = piv_ref[...] - base_ref[0]
    local = jnp.full_like(offset, -1)
    for m in range(mu):
        inside = offset - m * NBAS
        local = jnp.where((inside >= 0) & (inside < nu), inside + m * nu, local)
    order = lax.broadcasted_iota(jnp.int32, local.shape, 0) * local.shape[1] + lax.broadcasted_iota(
        jnp.int32, local.shape, 1
    )
    total = jnp.sum((local >= 0).astype(jnp.int32))

    def find(count, last):
        p = jnp.min(jnp.where((local >= 0) & (order > last), order, n))
        where_ref[0, count] = p
        where_ref[1, count] = jnp.max(jnp.where(order == p, local, -1))
        return p

    lax.fori_loop(0, total, find, jnp.int32(-1))

    def fetch(row, slot):
        m = jnp.int32(0)
        for step in range(1, mu):
            m += (row >= step * nu).astype(jnp.int32)
        start = pl.multiple_of((row - m * nu) // group * group, group)
        return pltpu.make_async_copy(
            prev_ref.at[m, pl.ds(start, group)], slots.at[slot], sems.at[slot]
        )

    def batch(b, _):
        first = b * depth
        size = jnp.minimum(total - first, depth)

        def begin(i, _):
            fetch(where_ref[1, first + i], i).start()
            return 0

        def end(i, _):
            row = where_ref[1, first + i]
            fetch(row, i).wait()
            rows = slots[i].astype(F32)
            keep = lax.broadcasted_iota(jnp.int32, rows.shape, 0) == row % group
            picked = jnp.sum(jnp.where(keep, rows, 0.0), axis=0, keepdims=True)
            acc_ref[pl.ds(where_ref[0, first + i], 1), :] = picked
            return 0

        lax.fori_loop(0, size, begin, 0)
        lax.fori_loop(0, size, end, 0)
        return 0

    lax.fori_loop(0, (total + depth - 1) // depth, batch, 0)
    out_ref[...] = acc_ref[...].astype(BF16)


def pick_rows(base, pivots, previous):
    mu, nu, k = previous.shape
    n = pivots.shape[0]
    lanes = 128
    return pl.pallas_call(
        pick_kernel,
        out_shape=jax.ShapeDtypeStruct((n, k), BF16),
        in_specs=[
            pl.BlockSpec(memory_space=pltpu.SMEM),
            pl.BlockSpec(memory_space=pltpu.VMEM),
            pl.BlockSpec(memory_space=pltpu.HBM),
        ],
        out_specs=pl.BlockSpec(memory_space=pltpu.VMEM),
        scratch_shapes=[
            pltpu.VMEM((n, k), F32),
            pltpu.VMEM((16, 16, k), BF16),
            pltpu.SemaphoreType.DMA((16,)),
            pltpu.SMEM((2, n), jnp.int32),
        ],
        compiler_params=pltpu.CompilerParams(vmem_limit_bytes=4 << 20),
        cost_estimate=pl.CostEstimate(flops=n * k, bytes_accessed=2 * n * k, transcendentals=0),
        name="pick_rows",
    )(base, pivots.reshape(n // lanes, lanes), previous)


def block_kernel(me_ref, cols_ref, prev_ref, rows_ref, inv_ref, orb_ref, *rest):
    new_ref, part_ref, right_ref, left_ref, turned_ref = rest[-5:]
    owners, dests, mus, keep, width = part_ref.shape
    n = dests * keep
    i = pl.program_id(0)

    @pl.when(i < mus)
    def _():
        contract = (((1,), (1,)), ((), ()))
        correction = lax.dot_general(
            prev_ref[0], rows_ref[...], contract, preferred_element_type=F32
        )
        residual = (cols_ref[0].astype(F32) - correction).astype(BF16)
        inv = inv_ref[...]
        row, column = (lax.broadcasted_iota(jnp.int32, inv.shape, d) for d in (0, 1))
        upper = jnp.where(row > column, 0.0, inv.astype(F32)).astype(BF16)
        new = jnp.dot(residual, upper, preferred_element_type=F32).astype(BF16)
        new_ref[0] = new
        turned_ref[pl.ds(pl.multiple_of(i * n, n), n), :] = new.T

    @pl.when(i >= mus)
    def _():
        part = jnp.dot(turned_ref[...], orb_ref[...], preferred_element_type=F32)
        for q in range(part.shape[1] // width):
            owner = (i - mus) * (part.shape[1] // width) + q
            ahead = lax.rem(owner - me_ref[0] + owners, owners)
            for m in range(mus):
                piece = part[m * n : (m + 1) * n, q * width : (q + 1) * width]
                piece = piece.reshape(dests, keep, width)
                part_ref[ahead, :, m] = piece

                @pl.when(ahead == owners // 2)
                def _():
                    right_ref[:, m] = piece[: dests // 2].astype(BF16)
                    left_ref[:, m] = piece[dests // 2 :].astype(BF16)


def block(me, first, mus, pivot_columns, previous, rows, pivot_inverse, orbitals, owners, dests, so_far):
    mu, nu, k = previous.shape
    n = pivot_columns.shape[2]
    occ = orbitals.shape[1]
    wide = 2 * occ // owners
    part_shape = (owners, dests, mus, n // dests, occ // owners)
    send_shape = (dests // 2,) + part_shape[2:]
    slab = lambda i, me: (first + jnp.minimum(i, mus - 1), 0, 0)
    whole = lambda i, me: (0, 0)
    in_specs = [
        pl.BlockSpec((1, nu, n), slab),
        pl.BlockSpec((1, nu, k), slab),
        pl.BlockSpec((n, k), whole),
        pl.BlockSpec((n, n), whole),
        pl.BlockSpec((nu, wide), lambda i, me: (0, jnp.maximum(i - mus, 0))),
    ]
    args = [pivot_columns, previous, rows, pivot_inverse, orbitals]
    aliases = {}
    if so_far is not None:
        in_specs.append(pl.BlockSpec(memory_space=pl.ANY))
        args.append(so_far)
        aliases = {len(args): 0}
    return pl.pallas_call(
        block_kernel,
        out_shape=(
            jax.ShapeDtypeStruct((mu, nu, n), BF16),
            jax.ShapeDtypeStruct(part_shape, F32),
            jax.ShapeDtypeStruct(send_shape, BF16),
            jax.ShapeDtypeStruct(send_shape, BF16),
        ),
        grid_spec=pltpu.PrefetchScalarGridSpec(
            num_scalar_prefetch=1,
            grid=(mus + occ // wide,),
            in_specs=in_specs,
            out_specs=(
                pl.BlockSpec((1, nu, n), slab),
                pl.BlockSpec(part_shape, lambda i, me: (0, 0, 0, 0, 0)),
                pl.BlockSpec(send_shape, lambda i, me: (0, 0, 0, 0)),
                pl.BlockSpec(send_shape, lambda i, me: (0, 0, 0, 0)),
            ),
            scratch_shapes=[pltpu.VMEM((mus * n, nu), BF16)],
        ),
        input_output_aliases=aliases,
        compiler_params=pltpu.CompilerParams(vmem_limit_bytes=28 << 20),
        cost_estimate=pl.CostEstimate(
            flops=2 * mus * nu * n * (k + n + occ),
            bytes_accessed=2 * mus * nu * (k + 2 * n) + 4 * mus * n * occ,
            transcendentals=0,
        ),
        name="block",
    )(me, *args)


def join_kernel(own_ref, came_ref, out_ref, *, second):
    half = came_ref.shape[0]
    mine, other = (slice(half, None), slice(0, half)) if second else (slice(0, half), slice(half, None))
    out_ref[mine] = (own_ref[0, mine] + came_ref[...].astype(F32)).astype(BF16)
    out_ref[other] = own_ref[0, other].astype(BF16)


def join(part, ahead, came, second):
    shape = part.shape[1:]
    return pl.pallas_call(
        functools.partial(join_kernel, second=second),
        grid=(1,),
        out_shape=jax.ShapeDtypeStruct(shape, BF16),
        in_specs=[
            pl.BlockSpec((1,) + shape, lambda i: (ahead, 0, 0, 0, 0)),
            pl.BlockSpec(came.shape, lambda i: (0, 0, 0, 0)),
        ],
        out_specs=pl.BlockSpec(shape, lambda i: (0, 0, 0, 0)),
        compiler_params=pltpu.CompilerParams(vmem_limit_bytes=6 << 20),
        cost_estimate=pl.CostEstimate(
            flops=came.size, bytes_accessed=12 * came.size, transcendentals=0
        ),
        name="join",
    )(part, came)


def reduce_to_owner(part, right, left):
    owners = part.shape[0]
    far = owners // 2

    def hop(x, way):
        return lax.ppermute(x, "grp", [(i, (i + way) % owners) for i in range(owners)])

    right, left = hop(right, 1), hop(left, -1)
    right, left = hop(join(part, far - 1, right, False), 1), hop(join(part, far + 1, left, True), -1)
    for ahead in range(far - 2, 0, -1):
        right, left = (
            hop((part[a].astype(F32) + x.astype(F32)).astype(BF16), way)
            for a, x, way in ((ahead, right, 1), (owners - ahead, left, -1))
        )
    return part, right, left


def finish_kernel(*refs):
    out_ref = refs[-1]
    mus = refs[0].shape[2]
    for s in range(len(refs) // 3):
        own, right, left = refs[3 * s : 3 * s + 3]
        total = own[0] + right[...].astype(F32) + left[...].astype(F32)
        out_ref[:, s * mus : (s + 1) * mus] = total


def finish(streams):
    dests, mus, keep, width = streams[0][0].shape[1:]
    out_shape = (dests, mus * len(streams), keep, width)
    zeros = lambda d: (lambda i: (0,) * d)
    own = pl.BlockSpec((1, dests, mus, keep, width), zeros(5))
    came = pl.BlockSpec((dests, mus, keep, width), zeros(4))
    return pl.pallas_call(
        finish_kernel,
        grid=(1,),
        out_shape=jax.ShapeDtypeStruct(out_shape, F32),
        in_specs=[own, came, came] * len(streams),
        out_specs=pl.BlockSpec(out_shape, zeros(4)),
        compiler_params=pltpu.CompilerParams(vmem_limit_bytes=10 << 20),
        cost_estimate=pl.CostEstimate(
            flops=2 * dests * mus * keep * width * len(streams),
            bytes_accessed=12 * dests * mus * keep * width * len(streams),
            transcendentals=0,
        ),
        name="finish",
    )(*[x for stream in streams for x in stream])


def final_kernel(half_ref, slab_ref, out_ref):
    rows, width = half_ref.shape
    mu = slab_ref.shape[0]
    keep = rows // mu
    slab_t = slab_ref[...].T
    slab_t = jnp.concatenate([slab_t, slab_t], axis=1)
    for p in range(0, keep, 2):
        pair = jnp.concatenate(
            [half_ref[pl.ds(q, mu, stride=keep), :] for q in (p, p + 1)], axis=1
        )
        high = pair.astype(BF16)
        low = (pair - high.astype(F32)).astype(BF16)
        both = jnp.dot(slab_t, jnp.concatenate([high, low], axis=0), preferred_element_type=F32)
        out_ref[p] = both[:, :width].astype(BF16)
        out_ref[p + 1] = both[:, width:].astype(BF16)


def final(half, slab):
    mu, occ = slab.shape
    rows, width = half.shape
    keep = rows // mu
    return pl.pallas_call(
        final_kernel,
        out_shape=jax.ShapeDtypeStruct((keep, occ, width), BF16),
        compiler_params=pltpu.CompilerParams(vmem_limit_bytes=16 << 20),
        cost_estimate=pl.CostEstimate(
            flops=4 * rows * width * occ,
            bytes_accessed=2 * keep * width * (2 * mu + occ),
            transcendentals=0,
        ),
        name="final",
    )(half, slab)


def exchange(x, axis):
    return lax.all_to_all(x, axis, split_axis=0, concat_axis=0, tiled=True)


def sum_rows(x):
    return jnp.sum(x.astype(F32), axis=0).astype(BF16)


def per_device(n_rows, n_grp, pivot_columns, previous, pivots, pivot_inverse, orbitals, slab_orbitals):
    mu, nu, k = previous.shape
    n = pivot_columns.shape[2]
    base = lax.axis_index("rows") * (mu * NBAS) + lax.axis_index("grp") * nu
    previous, orbitals = (
        pltpu.with_memory_space_constraint(x, pltpu.HBM) for x in (previous, orbitals)
    )
    picked = pick_rows(base.reshape(1).astype(jnp.int32), pivots, previous)
    mine = sum_rows(exchange(picked.reshape(n_rows, n // n_rows, k), "rows"))
    mine = sum_rows(exchange(jnp.broadcast_to(mine, (n_grp,) + mine.shape), "grp"))
    rows = exchange(jnp.broadcast_to(mine, (n_rows,) + mine.shape), "rows").reshape(n, k)
    me = lax.axis_index("grp").reshape(1).astype(jnp.int32)
    mus = mu // STREAMS
    new_vectors, streams = None, []
    for s in range(STREAMS):
        new_vectors, part, right, left = block(
            me, s * mus, mus, pivot_columns, previous, rows, pivot_inverse, orbitals,
            n_grp, n_rows, new_vectors,
        )
        streams.append(reduce_to_owner(part, right, left))
    half = exchange(finish(streams), "rows")
    return new_vectors, final(half.reshape(-1, half.shape[-1]), slab_orbitals)


def solution(mesh):
    in_specs = (P("rows", "grp", None), P("rows", "grp", None), P(), P(), P("grp", None), P())
    out_specs = (P("rows", "grp", None), P("rows", None, "grp"))
    body = functools.partial(per_device, mesh.shape["rows"], mesh.shape["grp"])
    return jax.shard_map(body, mesh=mesh, in_specs=in_specs, out_specs=out_specs, check_vma=False)
```

```python
import functools

import jax
import jax.numpy as jnp
from jax import lax
from jax.experimental import pallas as pl
from jax.experimental.pallas import tpu as pltpu
from jax.sharding import PartitionSpec as P

NBAS = 10240
F32 = jnp.float32
BF16 = jnp.bfloat16


def pick_kernel(base_ref, piv_ref, prev_ref, out_ref, acc_ref, slots, sems, where_ref):
    mu, nu, _ = prev_ref.shape
    depth, group, _ = slots.shape
    n = acc_ref.shape[0]
    acc_ref[...] = jnp.zeros_like(acc_ref)
    offset = piv_ref[...] - base_ref[0]
    local = jnp.full_like(offset, -1)
    for m in range(mu):
        inside = offset - m * NBAS
        local = jnp.where((inside >= 0) & (inside < nu), inside + m * nu, local)
    order = lax.broadcasted_iota(jnp.int32, local.shape, 0) * local.shape[1] + lax.broadcasted_iota(
        jnp.int32, local.shape, 1
    )
    total = jnp.sum((local >= 0).astype(jnp.int32))

    def find(count, last):
        p = jnp.min(jnp.where((local >= 0) & (order > last), order, n))
        where_ref[0, count] = p
        where_ref[1, count] = jnp.max(jnp.where(order == p, local, -1))
        return p

    lax.fori_loop(0, total, find, jnp.int32(-1))

    def fetch(row, slot):
        m = jnp.int32(0)
        for step in range(1, mu):
            m += (row >= step * nu).astype(jnp.int32)
        start = pl.multiple_of((row - m * nu) // group * group, group)
        return pltpu.make_async_copy(
            prev_ref.at[m, pl.ds(start, group)], slots.at[slot], sems.at[slot]
        )

    def batch(b, _):
        first = b * depth
        size = jnp.minimum(total - first, depth)

        def begin(i, _):
            fetch(where_ref[1, first + i], i).start()
            return 0

        def end(i, _):
            row = where_ref[1, first + i]
            fetch(row, i).wait()
            rows = slots[i].astype(F32)
            keep = lax.broadcasted_iota(jnp.int32, rows.shape, 0) == row % group
            picked = jnp.sum(jnp.where(keep, rows, 0.0), axis=0, keepdims=True)
            acc_ref[pl.ds(where_ref[0, first + i], 1), :] = picked
            return 0

        lax.fori_loop(0, size, begin, 0)
        lax.fori_loop(0, size, end, 0)
        return 0

    lax.fori_loop(0, (total + depth - 1) // depth, batch, 0)
    out_ref[...] = acc_ref[...].astype(BF16)


def pick_rows(base, pivots, previous):
    mu, nu, k = previous.shape
    n = pivots.shape[0]
    lanes = 128
    return pl.pallas_call(
        pick_kernel,
        out_shape=jax.ShapeDtypeStruct((n, k), BF16),
        in_specs=[
            pl.BlockSpec(memory_space=pltpu.SMEM),
            pl.BlockSpec(memory_space=pltpu.VMEM),
            pl.BlockSpec(memory_space=pltpu.HBM),
        ],
        out_specs=pl.BlockSpec(memory_space=pltpu.VMEM),
        scratch_shapes=[
            pltpu.VMEM((n, k), F32),
            pltpu.VMEM((16, 16, k), BF16),
            pltpu.SemaphoreType.DMA((16,)),
            pltpu.SMEM((2, n), jnp.int32),
        ],
        compiler_params=pltpu.CompilerParams(vmem_limit_bytes=4 << 20),
        cost_estimate=pl.CostEstimate(flops=n * k, bytes_accessed=2 * n * k, transcendentals=0),
        name="pick_rows",
    )(base, pivots.reshape(n // lanes, lanes), previous)


def vectors_kernel(cols_ref, prev_ref, rows_ref, inv_ref, new_ref, turned_ref):
    contract = (((1,), (1,)), ((), ()))
    correction = lax.dot_general(prev_ref[0], rows_ref[...], contract, preferred_element_type=F32)
    residual = (cols_ref[0].astype(F32) - correction).astype(BF16)
    inv = inv_ref[...]
    row, column = (lax.broadcasted_iota(jnp.int32, inv.shape, d) for d in (0, 1))
    upper = jnp.where(row > column, 0.0, inv.astype(F32)).astype(BF16)
    new = jnp.dot(residual, upper, preferred_element_type=F32).astype(BF16)
    new_ref[0] = new
    turned_ref[0] = new.T


def vectors(pivot_columns, previous, rows, pivot_inverse):
    mu, nu, k = previous.shape
    n = pivot_columns.shape[2]
    slab = lambda m: (m, 0, 0)
    whole = lambda m: (0, 0)
    return pl.pallas_call(
        vectors_kernel,
        grid=(mu,),
        out_shape=(
            jax.ShapeDtypeStruct((mu, nu, n), BF16),
            jax.ShapeDtypeStruct((mu, n, nu), BF16),
        ),
        in_specs=[
            pl.BlockSpec((1, nu, n), slab),
            pl.BlockSpec((1, nu, k), slab),
            pl.BlockSpec((n, k), whole),
            pl.BlockSpec((n, n), whole),
        ],
        out_specs=(pl.BlockSpec((1, nu, n), slab), pl.BlockSpec((1, n, nu), slab)),
        compiler_params=pltpu.CompilerParams(vmem_limit_bytes=20 << 20),
        cost_estimate=pl.CostEstimate(
            flops=2 * mu * nu * n * (k + n),
            bytes_accessed=2 * mu * nu * (k + 3 * n),
            transcendentals=0,
        ),
        name="vectors",
    )(pivot_columns, previous, rows, pivot_inverse)


def parts_kernel(me_ref, turned_ref, orb_ref, *out_refs, ahead, owners):
    mu, n, nu = turned_ref.shape
    width = orb_ref.shape[1] // owners
    keep, last = out_refs[0].shape[-2:]
    columns = []
    for a in ahead:
        start = pl.multiple_of(lax.rem(me_ref[0] + a, owners) * width, width)
        columns.append(orb_ref[:, pl.ds(start, width)])
    columns = columns[0] if len(columns) == 1 else jnp.concatenate(columns, axis=1)
    for m in range(mu):
        part = jnp.dot(turned_ref[m], columns, preferred_element_type=F32)
        if len(out_refs) == 2:
            half = n // 2
            for h, out_ref in enumerate(out_refs):
                piece = part[h * half : (h + 1) * half].reshape(half // keep, keep, last)
                out_ref[:, m] = piece.astype(out_ref.dtype)
        else:
            for q in range(len(ahead)):
                piece = part[:, q * width : (q + 1) * width].reshape(n // keep, keep, width)
                out_refs[0][q, :, m] = piece


def parts(me, turned, orbitals, ahead, owners, dests, send=False):
    mu, n, nu = turned.shape
    width = orbitals.shape[1] // owners
    if send:
        shape = (dests // 2, mu, n // dests, width)
        out_shape = (jax.ShapeDtypeStruct(shape, BF16),) * 2
    else:
        shape = (len(ahead), dests, mu, n // dests, width)
        out_shape = jax.ShapeDtypeStruct(shape, F32)
    vmem = pl.BlockSpec(memory_space=pltpu.VMEM)
    return pl.pallas_call(
        functools.partial(parts_kernel, ahead=ahead, owners=owners),
        out_shape=out_shape,
        in_specs=[pl.BlockSpec(memory_space=pltpu.SMEM), vmem, vmem],
        out_specs=(vmem, vmem) if send else vmem,
        compiler_params=pltpu.CompilerParams(vmem_limit_bytes=20 << 20),
        cost_estimate=pl.CostEstimate(
            flops=2 * mu * n * nu * width * len(ahead),
            bytes_accessed=2 * mu * n * nu,
            transcendentals=0,
        ),
        name="parts",
    )(me, turned, orbitals)


def join_kernel(own_ref, came_ref, out_ref, *, second):
    half = came_ref.shape[0]
    mine, other = (slice(half, None), slice(0, half)) if second else (slice(0, half), slice(half, None))
    out_ref[mine] = (own_ref[0, mine] + came_ref[...].astype(F32)).astype(BF16)
    out_ref[other] = own_ref[0, other].astype(BF16)


def join(part, which, came, second):
    shape = part.shape[1:]
    return pl.pallas_call(
        functools.partial(join_kernel, second=second),
        grid=(1,),
        out_shape=jax.ShapeDtypeStruct(shape, BF16),
        in_specs=[
            pl.BlockSpec((1,) + shape, lambda i: (which, 0, 0, 0, 0)),
            pl.BlockSpec(came.shape, lambda i: (0, 0, 0, 0)),
        ],
        out_specs=pl.BlockSpec(shape, lambda i: (0, 0, 0, 0)),
        compiler_params=pltpu.CompilerParams(vmem_limit_bytes=6 << 20),
        cost_estimate=pl.CostEstimate(
            flops=came.size, bytes_accessed=12 * came.size, transcendentals=0
        ),
        name="join",
    )(part, came)


def reduce_to_owner(me, turned, orbitals, owners, dests):
    far = owners // 2

    def hop(x, way):
        return lax.ppermute(x, "grp", [(i, (i + way) % owners) for i in range(owners)])

    def own(ahead, **more):
        return parts(me, turned, orbitals, ahead, owners, dests, **more)

    right, left = own((far,), send=True)
    right, left = hop(right, 1), hop(left, -1)
    near = own((far - 1, far + 1))
    right, left = hop(join(near, 0, right, False), 1), hop(join(near, 1, left, True), -1)
    for ahead in range(far - 2, 0, -1):
        near = own((ahead, owners - ahead))
        right, left = (
            hop((near[q] + x.astype(F32)).astype(BF16), way)
            for q, (x, way) in enumerate(((right, 1), (left, -1)))
        )
    return own((0,))[0] + right.astype(F32) + left.astype(F32)


def final_kernel(half_ref, slab_ref, out_ref):
    rows, width = half_ref.shape
    mu = slab_ref.shape[0]
    keep = rows // mu
    slab_t = slab_ref[...].T
    slab_t = jnp.concatenate([slab_t, slab_t], axis=1)
    for p in range(0, keep, 2):
        pair = jnp.concatenate(
            [half_ref[pl.ds(q, mu, stride=keep), :] for q in (p, p + 1)], axis=1
        )
        high = pair.astype(BF16)
        low = (pair - high.astype(F32)).astype(BF16)
        both = jnp.dot(slab_t, jnp.concatenate([high, low], axis=0), preferred_element_type=F32)
        out_ref[p] = both[:, :width].astype(BF16)
        out_ref[p + 1] = both[:, width:].astype(BF16)


def final(half, slab):
    mu, occ = slab.shape
    rows, width = half.shape
    keep = rows // mu
    return pl.pallas_call(
        final_kernel,
        out_shape=jax.ShapeDtypeStruct((keep, occ, width), BF16),
        compiler_params=pltpu.CompilerParams(vmem_limit_bytes=16 << 20),
        cost_estimate=pl.CostEstimate(
            flops=4 * rows * width * occ,
            bytes_accessed=2 * keep * width * (2 * mu + occ),
            transcendentals=0,
        ),
        name="final",
    )(half, slab)


def exchange(x, axis):
    return lax.all_to_all(x, axis, split_axis=0, concat_axis=0, tiled=True)


def sum_rows(x):
    return jnp.sum(x.astype(F32), axis=0).astype(BF16)


def per_device(n_rows, n_grp, pivot_columns, previous, pivots, pivot_inverse, orbitals, slab_orbitals):
    mu, nu, k = previous.shape
    n = pivot_columns.shape[2]
    base = lax.axis_index("rows") * (mu * NBAS) + lax.axis_index("grp") * nu
    previous = pltpu.with_memory_space_constraint(previous, pltpu.HBM)
    picked = pick_rows(base.reshape(1).astype(jnp.int32), pivots, previous)
    mine = sum_rows(exchange(picked.reshape(n_rows, n // n_rows, k), "rows"))
    mine = sum_rows(exchange(jnp.broadcast_to(mine, (n_grp,) + mine.shape), "grp"))
    rows = exchange(jnp.broadcast_to(mine, (n_rows,) + mine.shape), "rows").reshape(n, k)
    me = lax.axis_index("grp").reshape(1).astype(jnp.int32)
    new_vectors, turned = vectors(pivot_columns, previous, rows, pivot_inverse)
    half = exchange(reduce_to_owner(me, turned, orbitals, n_grp, n_rows), "rows")
    return new_vectors, final(half.reshape(-1, half.shape[-1]), slab_orbitals)


def solution(mesh):
    in_specs = (P("rows", "grp", None), P("rows", "grp", None), P(), P(), P("grp", None), P())
    out_specs = (P("rows", "grp", None), P("rows", None, "grp"))
    body = functools.partial(per_device, mesh.shape["rows"], mesh.shape["grp"])
    return jax.shard_map(body, mesh=mesh, in_specs=in_specs, out_specs=out_specs, check_vma=False)
```

```python
import functools

import jax
import jax.numpy as jnp
from jax import lax
from jax.experimental import pallas as pl
from jax.experimental.pallas import tpu as pltpu
from jax.sharding import PartitionSpec as P

NBAS = 10240
F32 = jnp.float32
BF16 = jnp.bfloat16
SLOTS = 24


def pick_kernel(where_from_ref, piv_ref, prev_ref, out_ref, acc_ref, held, sems, todo_ref):
    mu, nu, _ = prev_ref.shape
    depth, group, _ = held.shape
    line, base, round_index = (where_from_ref[i] for i in range(3))
    n = todo_ref.shape[1]
    slots = acc_ref.shape[0]
    acc_ref[...] = jnp.zeros_like(acc_ref)
    pivots = piv_ref[...]
    order = lax.broadcasted_iota(jnp.int32, pivots.shape, 0) * pivots.shape[1]
    order += lax.broadcasted_iota(jnp.int32, pivots.shape, 1)
    in_line = (pivots >= line) & (pivots < line + mu * NBAS)
    local = jnp.full_like(pivots, -1)
    for m in range(mu):
        inside = pivots - base - m * NBAS
        local = jnp.where((inside >= 0) & (inside < nu), inside + m * nu, local)
    owned = jnp.sum((local >= 0).astype(jnp.int32))

    def find(i, carry):
        last, count = carry
        p = jnp.min(jnp.where((local >= 0) & (order > last), order, n))
        rank = jnp.sum((in_line & (order < p)).astype(jnp.int32))
        slot = rank - round_index * slots
        todo_ref[0, count] = slot
        todo_ref[1, count] = jnp.max(jnp.where(order == p, local, -1))
        return p, count + ((slot >= 0) & (slot < slots)).astype(jnp.int32)

    _, total = lax.fori_loop(0, owned, find, (jnp.int32(-1), jnp.int32(0)))

    def fetch(row, i):
        m = jnp.int32(0)
        for step in range(1, mu):
            m += (row >= step * nu).astype(jnp.int32)
        start = pl.multiple_of((row - m * nu) // group * group, group)
        return pltpu.make_async_copy(prev_ref.at[m, pl.ds(start, group)], held.at[i], sems.at[i])

    def batch(b, _):
        first = b * depth
        size = jnp.minimum(total - first, depth)

        def begin(i, _):
            fetch(todo_ref[1, first + i], i).start()
            return 0

        def end(i, _):
            row = todo_ref[1, first + i]
            fetch(row, i).wait()
            rows = held[i].astype(F32)
            keep = lax.broadcasted_iota(jnp.int32, rows.shape, 0) == row % group
            picked = jnp.sum(jnp.where(keep, rows, 0.0), axis=0, keepdims=True)
            acc_ref[pl.ds(todo_ref[0, first + i], 1), :] = picked
            return 0

        lax.fori_loop(0, size, begin, 0)
        lax.fori_loop(0, size, end, 0)
        return 0

    lax.fori_loop(0, (total + depth - 1) // depth, batch, 0)
    out_ref[...] = acc_ref[...].astype(BF16)


def pick_rows(where_from, pivots, previous):
    mu, nu, k = previous.shape
    n = pivots.shape[0]
    lanes = 128
    return pl.pallas_call(
        pick_kernel,
        out_shape=jax.ShapeDtypeStruct((SLOTS, k), BF16),
        in_specs=[
            pl.BlockSpec(memory_space=pltpu.SMEM),
            pl.BlockSpec(memory_space=pltpu.VMEM),
            pl.BlockSpec(memory_space=pltpu.HBM),
        ],
        out_specs=pl.BlockSpec(memory_space=pltpu.VMEM),
        scratch_shapes=[
            pltpu.VMEM((SLOTS, k), F32),
            pltpu.VMEM((16, 16, k), BF16),
            pltpu.SemaphoreType.DMA((16,)),
            pltpu.SMEM((2, n + 1), jnp.int32),
        ],
        compiler_params=pltpu.CompilerParams(vmem_limit_bytes=4 << 20),
        cost_estimate=pl.CostEstimate(flops=n * k, bytes_accessed=2 * n * k, transcendentals=0),
        name="pick_rows",
    )(where_from, pivots.reshape(n // lanes, lanes), previous)


def select_kernel(round_ref, piv_ref, slots_ref, so_far_ref, out_ref, *, per_line):
    total, _ = slots_ref.shape
    n = piv_ref.shape[1]
    along = jnp.broadcast_to(piv_ref[...].astype(F32), (n, n))
    lines_along = jnp.floor((along + 0.5) * (1.0 / per_line))
    lines = lines_along.T
    earlier = lax.broadcasted_iota(jnp.int32, (n, n), 1) < lax.broadcasted_iota(jnp.int32, (n, n), 0)
    same = jnp.where((lines_along == lines) & earlier, 1.0, 0.0)
    rank = jnp.sum(same, axis=1, keepdims=True) - (round_ref[0] * SLOTS).astype(F32)
    mine = (rank >= 0.0) & (rank < SLOTS)
    index = jnp.where(mine, lines[:, :1] * SLOTS + rank, -1.0).astype(jnp.int32)
    hot = index == lax.broadcasted_iota(jnp.int32, (n, total), 1)
    hot = jnp.where(hot, 1.0, 0.0).astype(BF16)
    picked = jnp.dot(hot, slots_ref[...], preferred_element_type=F32)
    out_ref[...] = (picked + so_far_ref[...].astype(F32)).astype(BF16)


def select_rows(round_index, pivots, slots, so_far, per_line):
    total, width = slots.shape
    n = pivots.shape[0]
    vmem = pl.BlockSpec(memory_space=pltpu.VMEM)
    return pl.pallas_call(
        functools.partial(select_kernel, per_line=per_line),
        out_shape=jax.ShapeDtypeStruct((n, width), BF16),
        in_specs=[pl.BlockSpec(memory_space=pltpu.SMEM), vmem, vmem, vmem],
        out_specs=vmem,
        compiler_params=pltpu.CompilerParams(vmem_limit_bytes=8 << 20),
        cost_estimate=pl.CostEstimate(
            flops=2 * n * total * width, bytes_accessed=2 * total * width, transcendentals=0
        ),
        name="select_rows",
    )(round_index, pivots.reshape(1, n), slots, so_far)


def vectors_kernel(
    core_ref, cols_ref, prev_ref, mine_ref, other_ref, inv_ref, new_ref, turned_ref, came, load
):
    m = pl.program_id(0)

    def load_of(m):
        return pltpu.make_async_copy(prev_ref.at[m], came.at[m], load.at[m])

    @pl.when(m == 0)
    def _():
        for other_m in range(came.shape[0]):
            load_of(other_m).start()

    load_of(m).wait()
    mine, other = mine_ref[...].astype(F32), other_ref[...].astype(F32)
    first = core_ref[0] == 0
    rows = jnp.concatenate(
        [jnp.where(first, mine, other), jnp.where(first, other, mine)], axis=1
    ).astype(BF16)
    contract = (((1,), (1,)), ((), ()))
    correction = lax.dot_general(came[m], rows, contract, preferred_element_type=F32)
    residual = (cols_ref[0].astype(F32) - correction).astype(BF16)
    inv = inv_ref[...]
    row, column = (lax.broadcasted_iota(jnp.int32, inv.shape, d) for d in (0, 1))
    upper = jnp.where(row > column, 0.0, inv.astype(F32)).astype(BF16)
    new = jnp.dot(residual, upper, preferred_element_type=F32).astype(BF16)
    new_ref[0] = new
    turned_ref[0] = new.T


def vectors(core, pivot_columns, previous, mine, other, pivot_inverse):
    mu, nu, k = previous.shape
    n = pivot_columns.shape[2]
    slab = lambda m: (m, 0, 0)
    whole = lambda m: (0, 0)
    return pl.pallas_call(
        vectors_kernel,
        grid=(mu,),
        out_shape=(
            jax.ShapeDtypeStruct((mu, nu, n), BF16),
            jax.ShapeDtypeStruct((mu, n, nu), BF16),
        ),
        in_specs=[
            pl.BlockSpec(memory_space=pltpu.SMEM),
            pl.BlockSpec((1, nu, n), slab),
            pl.BlockSpec(memory_space=pltpu.HBM),
            pl.BlockSpec((n, k // 2), whole),
            pl.BlockSpec((n, k // 2), whole),
            pl.BlockSpec((n, n), whole),
        ],
        out_specs=(pl.BlockSpec((1, nu, n), slab), pl.BlockSpec((1, n, nu), slab)),
        scratch_shapes=[pltpu.VMEM((mu, nu, k), BF16), pltpu.SemaphoreType.DMA((mu,))],
        compiler_params=pltpu.CompilerParams(vmem_limit_bytes=24 << 20),
        cost_estimate=pl.CostEstimate(
            flops=2 * mu * nu * n * (k + n),
            bytes_accessed=2 * mu * nu * (k + 3 * n),
            transcendentals=0,
        ),
        name="vectors",
    )(core, pivot_columns, previous, mine, other, pivot_inverse)


def parts_kernel(me_ref, turned_ref, orb_ref, *out_refs, ahead, owners):
    mu, n, nu = turned_ref.shape
    width = orb_ref.shape[1] // owners
    keep, last = out_refs[0].shape[-2:]
    columns = []
    for a in ahead:
        start = pl.multiple_of(lax.rem(me_ref[0] + a, owners) * width, width)
        columns.append(orb_ref[:, pl.ds(start, width)])
    columns = columns[0] if len(columns) == 1 else jnp.concatenate(columns, axis=1)
    for m in range(mu):
        part = jnp.dot(turned_ref[m], columns, preferred_element_type=F32)
        if len(out_refs) == 2:
            half = n // 2
            for h, out_ref in enumerate(out_refs):
                piece = part[h * half : (h + 1) * half].reshape(half // keep, keep, last)
                out_ref[:, m] = piece.astype(out_ref.dtype)
        else:
            for q in range(len(ahead)):
                piece = part[:, q * width : (q + 1) * width].reshape(n // keep, keep, width)
                out_refs[0][q, :, m] = piece


def parts(me, turned, orbitals, ahead, owners, dests, send=False):
    mu, n, nu = turned.shape
    width = orbitals.shape[1] // owners
    if send:
        shape = (dests // 2, mu, n // dests, width)
        out_shape = (jax.ShapeDtypeStruct(shape, BF16),) * 2
    else:
        shape = (len(ahead), dests, mu, n // dests, width)
        out_shape = jax.ShapeDtypeStruct(shape, F32)
    vmem = pl.BlockSpec(memory_space=pltpu.VMEM)
    return pl.pallas_call(
        functools.partial(parts_kernel, ahead=ahead, owners=owners),
        out_shape=out_shape,
        in_specs=[pl.BlockSpec(memory_space=pltpu.SMEM), vmem, vmem],
        out_specs=(vmem, vmem) if send else vmem,
        compiler_params=pltpu.CompilerParams(vmem_limit_bytes=20 << 20),
        cost_estimate=pl.CostEstimate(
            flops=2 * mu * n * nu * width * len(ahead),
            bytes_accessed=2 * mu * n * nu,
            transcendentals=0,
        ),
        name="parts",
    )(me, turned, orbitals)


def join_kernel(own_ref, came_ref, out_ref, *, second):
    half = came_ref.shape[0]
    mine, other = (slice(half, None), slice(0, half)) if second else (slice(0, half), slice(half, None))
    out_ref[mine] = (own_ref[0, mine] + came_ref[...].astype(F32)).astype(BF16)
    out_ref[other] = own_ref[0, other].astype(BF16)


def join(part, which, came, second):
    shape = part.shape[1:]
    return pl.pallas_call(
        functools.partial(join_kernel, second=second),
        grid=(1,),
        out_shape=jax.ShapeDtypeStruct(shape, BF16),
        in_specs=[
            pl.BlockSpec((1,) + shape, lambda i: (which, 0, 0, 0, 0)),
            pl.BlockSpec(came.shape, lambda i: (0, 0, 0, 0)),
        ],
        out_specs=pl.BlockSpec(shape, lambda i: (0, 0, 0, 0)),
        compiler_params=pltpu.CompilerParams(vmem_limit_bytes=6 << 20),
        cost_estimate=pl.CostEstimate(
            flops=came.size, bytes_accessed=12 * came.size, transcendentals=0
        ),
        name="join",
    )(part, came)


def reduce_to_owner(me, turned, orbitals, owners, dests):
    far = owners // 2

    def hop(x, way):
        return lax.ppermute(x, "grp", [(i, (i + way) % owners) for i in range(owners)])

    def own(ahead, **more):
        return parts(me, turned, orbitals, ahead, owners, dests, **more)

    right, left = own((far,), send=True)
    right, left = hop(right, 1), hop(left, -1)
    near = own((far - 1, far + 1))
    right, left = hop(join(near, 0, right, False), 1), hop(join(near, 1, left, True), -1)
    for ahead in range(far - 2, 0, -1):
        near = own((ahead, owners - ahead))
        right, left = (
            hop((near[q] + x.astype(F32)).astype(BF16), way)
            for q, (x, way) in enumerate(((right, 1), (left, -1)))
        )
    return own((0,))[0] + right.astype(F32) + left.astype(F32)


def final_kernel(half_ref, slab_ref, out_ref):
    rows, width = half_ref.shape
    mu = slab_ref.shape[0]
    keep = rows // mu
    slab_t = slab_ref[...].T
    slab_t = jnp.concatenate([slab_t, slab_t], axis=1)
    for p in range(0, keep, 2):
        pair = jnp.concatenate(
            [half_ref[pl.ds(q, mu, stride=keep), :] for q in (p, p + 1)], axis=1
        )
        high = pair.astype(BF16)
        low = (pair - high.astype(F32)).astype(BF16)
        both = jnp.dot(slab_t, jnp.concatenate([high, low], axis=0), preferred_element_type=F32)
        out_ref[p] = both[:, :width].astype(BF16)
        out_ref[p + 1] = both[:, width:].astype(BF16)


def final(half, slab):
    mu, occ = slab.shape
    rows, width = half.shape
    keep = rows // mu
    return pl.pallas_call(
        final_kernel,
        out_shape=jax.ShapeDtypeStruct((keep, occ, width), BF16),
        compiler_params=pltpu.CompilerParams(vmem_limit_bytes=16 << 20),
        cost_estimate=pl.CostEstimate(
            flops=4 * rows * width * occ,
            bytes_accessed=2 * keep * width * (2 * mu + occ),
            transcendentals=0,
        ),
        name="final",
    )(half, slab)


def exchange(x, axis):
    return lax.all_to_all(x, axis, split_axis=0, concat_axis=0, tiled=True)


def sum_rows(x):
    return jnp.sum(x.astype(F32), axis=0).astype(BF16)


def pivot_halves(n_rows, n_grp, pivots, previous):
    mu, nu, k = previous.shape
    n = pivots.shape[0]
    half = k // 2
    per_line = mu * NBAS
    line = lax.axis_index("rows") * per_line
    base = line + lax.axis_index("grp") * nu
    line, base = line.astype(jnp.int32), base.astype(jnp.int32)

    def one_round(index, so_far):
        index = jnp.asarray(index, jnp.int32)
        picked = pick_rows(jnp.stack([line, base, index]), pivots, previous)
        line_slots = sum_rows(exchange(jnp.broadcast_to(picked, (n_grp,) + picked.shape), "grp"))
        both = jnp.stack([line_slots[:, :half], line_slots[:, half:]])
        copies = jnp.broadcast_to(both, (n_rows // 2,) + both.shape)
        slots = exchange(copies.reshape(n_rows, SLOTS, half), "rows")
        return select_rows(
            index.reshape(1), pivots, slots.reshape(n_rows * SLOTS, half), so_far, per_line
        )

    lines = pivots // per_line
    most = jnp.max(jnp.sum(lines[:, None] == jnp.arange(n_rows)[None, :], axis=0))
    rounds = (most + SLOTS - 1) // SLOTS
    mine = one_round(0, jnp.zeros((n, half), BF16))
    mine = lax.fori_loop(1, rounds, one_round, mine)
    other = lax.ppermute(mine, "rows", [(i, i ^ 1) for i in range(n_rows)])
    return mine, other


def per_device(n_rows, n_grp, pivot_columns, previous, pivots, pivot_inverse, orbitals, slab_orbitals):
    previous = pltpu.with_memory_space_constraint(previous, pltpu.HBM)
    mine, other = pivot_halves(n_rows, n_grp, pivots, previous)
    core = (lax.axis_index("rows") % 2).reshape(1).astype(jnp.int32)
    me = lax.axis_index("grp").reshape(1).astype(jnp.int32)
    new_vectors, turned = vectors(core, pivot_columns, previous, mine, other, pivot_inverse)
    half = exchange(reduce_to_owner(me, turned, orbitals, n_grp, n_rows), "rows")
    return new_vectors, final(half.reshape(-1, half.shape[-1]), slab_orbitals)


def solution(mesh):
    in_specs = (P("rows", "grp", None), P("rows", "grp", None), P(), P(), P("grp", None), P())
    out_specs = (P("rows", "grp", None), P("rows", None, "grp"))
    body = functools.partial(per_device, mesh.shape["rows"], mesh.shape["grp"])
    return jax.shard_map(body, mesh=mesh, in_specs=in_specs, out_specs=out_specs, check_vma=False)
```

```python
import functools

import jax
import jax.numpy as jnp
from jax import lax
from jax.experimental import pallas as pl
from jax.experimental.pallas import tpu as pltpu
from jax.sharding import PartitionSpec as P

NBAS = 10240
F32 = jnp.float32
BF16 = jnp.bfloat16
SLOTS = 24


def pick_kernel(where_from_ref, piv_ref, prev_ref, out_ref, acc_ref, held, sems, todo_ref):
    mu, nu, _ = prev_ref.shape
    depth, group, _ = held.shape
    line, base, round_index = (where_from_ref[i] for i in range(3))
    n = todo_ref.shape[1]
    slots = acc_ref.shape[0]
    acc_ref[...] = jnp.zeros_like(acc_ref)
    pivots = piv_ref[...]
    order = lax.broadcasted_iota(jnp.int32, pivots.shape, 0) * pivots.shape[1]
    order += lax.broadcasted_iota(jnp.int32, pivots.shape, 1)
    in_line = (pivots >= line) & (pivots < line + mu * NBAS)
    local = jnp.full_like(pivots, -1)
    for m in range(mu):
        inside = pivots - base - m * NBAS
        local = jnp.where((inside >= 0) & (inside < nu), inside + m * nu, local)
    owned = jnp.sum((local >= 0).astype(jnp.int32))

    def find(i, carry):
        last, count = carry
        p = jnp.min(jnp.where((local >= 0) & (order > last), order, n))
        rank = jnp.sum((in_line & (order < p)).astype(jnp.int32))
        slot = rank - round_index * slots
        todo_ref[0, count] = slot
        todo_ref[1, count] = jnp.max(jnp.where(order == p, local, -1))
        return p, count + ((slot >= 0) & (slot < slots)).astype(jnp.int32)

    _, total = lax.fori_loop(0, owned, find, (jnp.int32(-1), jnp.int32(0)))

    def fetch(row, i):
        m = jnp.int32(0)
        for step in range(1, mu):
            m += (row >= step * nu).astype(jnp.int32)
        start = pl.multiple_of((row - m * nu) // group * group, group)
        return pltpu.make_async_copy(prev_ref.at[m, pl.ds(start, group)], held.at[i], sems.at[i])

    def batch(b, _):
        first = b * depth
        size = jnp.minimum(total - first, depth)

        def begin(i, _):
            fetch(todo_ref[1, first + i], i).start()
            return 0

        def end(i, _):
            row = todo_ref[1, first + i]
            fetch(row, i).wait()
            rows = held[i].astype(F32)
            keep = lax.broadcasted_iota(jnp.int32, rows.shape, 0) == row % group
            picked = jnp.sum(jnp.where(keep, rows, 0.0), axis=0, keepdims=True)
            acc_ref[pl.ds(todo_ref[0, first + i], 1), :] = picked
            return 0

        lax.fori_loop(0, size, begin, 0)
        lax.fori_loop(0, size, end, 0)
        return 0

    lax.fori_loop(0, (total + depth - 1) // depth, batch, 0)
    out_ref[...] = acc_ref[...].astype(BF16)


def pick_rows(where_from, pivots, previous):
    mu, nu, k = previous.shape
    n = pivots.shape[0]
    lanes = 128
    return pl.pallas_call(
        pick_kernel,
        out_shape=jax.ShapeDtypeStruct((SLOTS, k), BF16),
        in_specs=[
            pl.BlockSpec(memory_space=pltpu.SMEM),
            pl.BlockSpec(memory_space=pltpu.VMEM),
            pl.BlockSpec(memory_space=pltpu.HBM),
        ],
        out_specs=pl.BlockSpec(memory_space=pltpu.VMEM),
        scratch_shapes=[
            pltpu.VMEM((SLOTS, k), F32),
            pltpu.VMEM((16, 16, k), BF16),
            pltpu.SemaphoreType.DMA((16,)),
            pltpu.SMEM((2, n + 1), jnp.int32),
        ],
        compiler_params=pltpu.CompilerParams(vmem_limit_bytes=4 << 20),
        cost_estimate=pl.CostEstimate(flops=n * k, bytes_accessed=2 * n * k, transcendentals=0),
        name="pick_rows",
    )(where_from, pivots.reshape(n // lanes, lanes), previous)


def select_kernel(round_ref, piv_ref, slots_ref, so_far_ref, out_ref, rounds_ref, *, per_line):
    total, _ = slots_ref.shape
    n = piv_ref.shape[1]
    along = jnp.broadcast_to(piv_ref[...].astype(F32), (n, n))
    lines_along = jnp.floor((along + 0.5) * (1.0 / per_line))
    lines = lines_along.T
    earlier = lax.broadcasted_iota(jnp.int32, (n, n), 1) < lax.broadcasted_iota(jnp.int32, (n, n), 0)
    same = jnp.where((lines_along == lines) & earlier, 1.0, 0.0)
    rank = jnp.sum(same, axis=1, keepdims=True)
    rounds_ref[0] = jnp.max(rank).astype(jnp.int32) // SLOTS + 1
    rank = rank - (round_ref[0] * SLOTS).astype(F32)
    mine = (rank >= 0.0) & (rank < SLOTS)
    index = jnp.where(mine, lines[:, :1] * SLOTS + rank, -1.0).astype(jnp.int32)
    hot = index == lax.broadcasted_iota(jnp.int32, (n, total), 1)
    hot = jnp.where(hot, 1.0, 0.0).astype(BF16)
    picked = jnp.dot(hot, slots_ref[...], preferred_element_type=F32)
    out_ref[...] = (picked + so_far_ref[...].astype(F32)).astype(BF16)


def select_rows(round_index, pivots, slots, so_far, per_line):
    total, width = slots.shape
    n = pivots.shape[0]
    vmem = pl.BlockSpec(memory_space=pltpu.VMEM)
    return pl.pallas_call(
        functools.partial(select_kernel, per_line=per_line),
        out_shape=(
            jax.ShapeDtypeStruct((n, width), BF16),
            jax.ShapeDtypeStruct((1,), jnp.int32),
        ),
        in_specs=[pl.BlockSpec(memory_space=pltpu.SMEM), vmem, vmem, vmem],
        out_specs=(vmem, pl.BlockSpec(memory_space=pltpu.SMEM)),
        compiler_params=pltpu.CompilerParams(vmem_limit_bytes=8 << 20),
        cost_estimate=pl.CostEstimate(
            flops=2 * n * total * width, bytes_accessed=2 * total * width, transcendentals=0
        ),
        name="select_rows",
    )(round_index, pivots.reshape(1, n), slots, so_far)


def spread_kernel(came_ref, out_ref):
    total = jnp.sum(came_ref[...].astype(F32), axis=0).astype(BF16)
    half = out_ref.shape[2]
    for c in range(2):
        piece = total[:, c * half : (c + 1) * half]

        @pl.loop(0, out_ref.shape[0] // 2)
        def _(chip):
            out_ref[2 * chip + c] = piece


def spread(came, n_rows):
    n_grp, slots, k = came.shape
    vmem = pl.BlockSpec(memory_space=pltpu.VMEM)
    return pl.pallas_call(
        spread_kernel,
        out_shape=jax.ShapeDtypeStruct((n_rows, slots, k // 2), BF16),
        in_specs=[vmem],
        out_specs=vmem,
        compiler_params=pltpu.CompilerParams(vmem_limit_bytes=4 << 20),
        cost_estimate=pl.CostEstimate(
            flops=n_grp * slots * k, bytes_accessed=n_rows * slots * k, transcendentals=0
        ),
        name="spread",
    )(came)


def vectors_kernel(
    core_ref, cols_ref, prev_ref, mine_ref, other_ref, inv_ref, new_ref, turned_ref, came, made, load, store
):
    mu = came.shape[0]

    def load_of(m):
        return pltpu.make_async_copy(prev_ref.at[m], came.at[m], load.at[m])

    def store_of(m):
        return pltpu.make_async_copy(made.at[m], new_ref.at[m], store.at[m])

    for m in range(mu):
        load_of(m).start()

    @pl.loop(0, mu)
    def _(m):
        load_of(m).wait()
        mine, other = mine_ref[...].astype(F32), other_ref[...].astype(F32)
        first = core_ref[0] == 0
        rows = jnp.concatenate(
            [jnp.where(first, mine, other), jnp.where(first, other, mine)], axis=1
        ).astype(BF16)
        contract = (((1,), (1,)), ((), ()))
        correction = lax.dot_general(came[m], rows, contract, preferred_element_type=F32)
        residual = (cols_ref[m].astype(F32) - correction).astype(BF16)
        inv = inv_ref[...]
        row, column = (lax.broadcasted_iota(jnp.int32, inv.shape, d) for d in (0, 1))
        upper = jnp.where(row > column, 0.0, inv.astype(F32)).astype(BF16)
        new = jnp.dot(residual, upper, preferred_element_type=F32).astype(BF16)
        made[m] = new
        store_of(m).start()
        turned_ref[m] = new.T

    for m in range(mu):
        store_of(m).wait()


def vectors(core, pivot_columns, previous, mine, other, pivot_inverse):
    mu, nu, k = previous.shape
    n = pivot_columns.shape[2]
    vmem = pl.BlockSpec(memory_space=pltpu.VMEM)
    return pl.pallas_call(
        vectors_kernel,
        out_shape=(
            jax.ShapeDtypeStruct((mu, nu, n), BF16),
            jax.ShapeDtypeStruct((mu, n, nu), BF16),
        ),
        in_specs=[
            pl.BlockSpec(memory_space=pltpu.SMEM),
            vmem,
            pl.BlockSpec(memory_space=pltpu.HBM),
            vmem,
            vmem,
            vmem,
        ],
        out_specs=(pl.BlockSpec(memory_space=pl.ANY), vmem),
        scratch_shapes=[
            pltpu.VMEM((mu, nu, k), BF16),
            pltpu.VMEM((mu, nu, n), BF16),
            pltpu.SemaphoreType.DMA((mu,)),
            pltpu.SemaphoreType.DMA((mu,)),
        ],
        compiler_params=pltpu.CompilerParams(vmem_limit_bytes=24 << 20),
        cost_estimate=pl.CostEstimate(
            flops=2 * mu * nu * n * (k + n),
            bytes_accessed=2 * mu * nu * (k + 3 * n),
            transcendentals=0,
        ),
        name="vectors",
    )(core, pivot_columns, previous, mine, other, pivot_inverse)


def parts_kernel(me_ref, turned_ref, orb_ref, *out_refs, ahead, owners):
    mu, n, nu = turned_ref.shape
    width = orb_ref.shape[1] // owners
    keep, last = out_refs[0].shape[-2:]
    columns = []
    for a in ahead:
        start = pl.multiple_of(lax.rem(me_ref[0] + a, owners) * width, width)
        columns.append(orb_ref[:, pl.ds(start, width)])
    columns = columns[0] if len(columns) == 1 else jnp.concatenate(columns, axis=1)
    for m in range(mu):
        part = jnp.dot(turned_ref[m], columns, preferred_element_type=F32)
        if len(out_refs) == 2:
            half = n // 2
            for h, out_ref in enumerate(out_refs):
                piece = part[h * half : (h + 1) * half].reshape(half // keep, keep, last)
                out_ref[:, m] = piece.astype(out_ref.dtype)
        else:
            for q in range(len(ahead)):
                piece = part[:, q * width : (q + 1) * width].reshape(n // keep, keep, width)
                out_refs[0][q, :, m] = piece


def parts(me, turned, orbitals, ahead, owners, dests, send=False):
    mu, n, nu = turned.shape
    width = orbitals.shape[1] // owners
    if send:
        shape = (dests // 2, mu, n // dests, width)
        out_shape = (jax.ShapeDtypeStruct(shape, BF16),) * 2
    else:
        shape = (len(ahead), dests, mu, n // dests, width)
        out_shape = jax.ShapeDtypeStruct(shape, F32)
    vmem = pl.BlockSpec(memory_space=pltpu.VMEM)
    return pl.pallas_call(
        functools.partial(parts_kernel, ahead=ahead, owners=owners),
        out_shape=out_shape,
        in_specs=[pl.BlockSpec(memory_space=pltpu.SMEM), vmem, vmem],
        out_specs=(vmem, vmem) if send else vmem,
        compiler_params=pltpu.CompilerParams(vmem_limit_bytes=20 << 20),
        cost_estimate=pl.CostEstimate(
            flops=2 * mu * n * nu * width * len(ahead),
            bytes_accessed=2 * mu * n * nu,
            transcendentals=0,
        ),
        name="parts",
    )(me, turned, orbitals)


def join_kernel(own_ref, came_ref, out_ref, *, second):
    half = came_ref.shape[0]
    mine, other = (slice(half, None), slice(0, half)) if second else (slice(0, half), slice(half, None))
    out_ref[mine] = (own_ref[0, mine] + came_ref[...].astype(F32)).astype(BF16)
    out_ref[other] = own_ref[0, other].astype(BF16)


def join(part, which, came, second):
    shape = part.shape[1:]
    return pl.pallas_call(
        functools.partial(join_kernel, second=second),
        grid=(1,),
        out_shape=jax.ShapeDtypeStruct(shape, BF16),
        in_specs=[
            pl.BlockSpec((1,) + shape, lambda i: (which, 0, 0, 0, 0)),
            pl.BlockSpec(came.shape, lambda i: (0, 0, 0, 0)),
        ],
        out_specs=pl.BlockSpec(shape, lambda i: (0, 0, 0, 0)),
        compiler_params=pltpu.CompilerParams(vmem_limit_bytes=6 << 20),
        cost_estimate=pl.CostEstimate(
            flops=came.size, bytes_accessed=12 * came.size, transcendentals=0
        ),
        name="join",
    )(part, came)


def reduce_to_owner(me, turned, orbitals, owners, dests):
    far = owners // 2

    def hop(x, way):
        return lax.ppermute(x, "grp", [(i, (i + way) % owners) for i in range(owners)])

    def own(ahead, **more):
        return parts(me, turned, orbitals, ahead, owners, dests, **more)

    right, left = own((far,), send=True)
    right, left = hop(right, 1), hop(left, -1)
    near = own((far - 1, far + 1))
    right, left = hop(join(near, 0, right, False), 1), hop(join(near, 1, left, True), -1)
    for ahead in range(far - 2, 0, -1):
        near = own((ahead, owners - ahead))
        right, left = (
            hop((near[q] + x.astype(F32)).astype(BF16), way)
            for q, (x, way) in enumerate(((right, 1), (left, -1)))
        )
    return own((0,))[0] + right.astype(F32) + left.astype(F32)


def final_kernel(half_ref, slab_ref, out_ref, turned_ref):
    rows, width = half_ref.shape
    mu = slab_ref.shape[0]
    keep = rows // mu

    @pl.when(pl.program_id(0) == 0)
    def _():
        slab_t = slab_ref[...].T
        turned_ref[...] = jnp.concatenate([slab_t, slab_t], axis=1)

    first = pl.program_id(0) * 2
    pair = jnp.concatenate(
        [half_ref[pl.ds(first + q, mu, stride=keep), :] for q in (0, 1)], axis=1
    )
    high = pair.astype(BF16)
    low = (pair - high.astype(F32)).astype(BF16)
    both = jnp.dot(
        turned_ref[...], jnp.concatenate([high, low], axis=0), preferred_element_type=F32
    )
    out_ref[0] = both[:, :width].astype(BF16)
    out_ref[1] = both[:, width:].astype(BF16)


def final(half, slab):
    mu, occ = slab.shape
    rows, width = half.shape
    keep = rows // mu
    whole = lambda i: (0, 0)
    return pl.pallas_call(
        final_kernel,
        grid=(keep // 2,),
        out_shape=jax.ShapeDtypeStruct((keep, occ, width), BF16),
        in_specs=[pl.BlockSpec((rows, width), whole), pl.BlockSpec((mu, occ), whole)],
        out_specs=pl.BlockSpec((2, occ, width), lambda i: (i, 0, 0)),
        scratch_shapes=[pltpu.VMEM((occ, 2 * mu), BF16)],
        compiler_params=pltpu.CompilerParams(vmem_limit_bytes=16 << 20),
        cost_estimate=pl.CostEstimate(
            flops=4 * rows * width * occ,
            bytes_accessed=2 * keep * width * (2 * mu + occ),
            transcendentals=0,
        ),
        name="final",
    )(half, slab)


def exchange(x, axis):
    return lax.all_to_all(x, axis, split_axis=0, concat_axis=0, tiled=True)


def pivot_halves(n_rows, n_grp, pivots, previous):
    mu, nu, k = previous.shape
    n = pivots.shape[0]
    half = k // 2
    per_line = mu * NBAS
    line = lax.axis_index("rows") * per_line
    base = line + lax.axis_index("grp") * nu
    line, base = line.astype(jnp.int32), base.astype(jnp.int32)

    def one_round(index, so_far):
        index = jnp.asarray(index, jnp.int32)
        picked = pick_rows(jnp.stack([line, base, index]), pivots, previous)
        came = exchange(jnp.broadcast_to(picked, (n_grp,) + picked.shape), "grp")
        slots = exchange(spread(came, n_rows), "rows")
        return select_rows(
            index.reshape(1), pivots, slots.reshape(n_rows * SLOTS, half), so_far, per_line
        )

    mine, rounds = one_round(0, jnp.zeros((n, half), BF16))
    start, mine, rounds = lax.optimization_barrier((jnp.int32(1), mine, rounds))
    mine = lax.fori_loop(start, rounds[0], lambda i, rows: one_round(i, rows)[0], mine)
    other = lax.ppermute(mine, "rows", [(i, i ^ 1) for i in range(n_rows)])
    return mine, other


def per_device(n_rows, n_grp, pivot_columns, previous, pivots, pivot_inverse, orbitals, slab_orbitals):
    previous = pltpu.with_memory_space_constraint(previous, pltpu.HBM)
    mine, other = pivot_halves(n_rows, n_grp, pivots, previous)
    core = (lax.axis_index("rows") % 2).reshape(1).astype(jnp.int32)
    me = lax.axis_index("grp").reshape(1).astype(jnp.int32)
    new_vectors, turned = vectors(core, pivot_columns, previous, mine, other, pivot_inverse)
    half = exchange(reduce_to_owner(me, turned, orbitals, n_grp, n_rows), "rows")
    return new_vectors, final(half.reshape(-1, half.shape[-1]), slab_orbitals)


def solution(mesh):
    in_specs = (P("rows", "grp", None), P("rows", "grp", None), P(), P(), P("grp", None), P())
    out_specs = (P("rows", "grp", None), P("rows", None, "grp"))
    body = functools.partial(per_device, mesh.shape["rows"], mesh.shape["grp"])
    return jax.shard_map(body, mesh=mesh, in_specs=in_specs, out_specs=out_specs, check_vma=False)
```

```python
import functools

import jax
import jax.numpy as jnp
from jax import lax
from jax.experimental import pallas as pl
from jax.experimental.pallas import tpu as pltpu
from jax.sharding import PartitionSpec as P

NBAS = 10240
F32 = jnp.float32
BF16 = jnp.bfloat16
SLOTS = 24


def pick_kernel(where_from_ref, piv_ref, prev_ref, out_ref, acc_ref, held, sems, todo_ref):
    mu, nu, _ = prev_ref.shape
    depth, group, _ = held.shape
    line, base, round_index = (where_from_ref[i] for i in range(3))
    n = todo_ref.shape[1]
    slots = acc_ref.shape[0]
    acc_ref[...] = jnp.zeros_like(acc_ref)
    pivots = piv_ref[...]
    order = lax.broadcasted_iota(jnp.int32, pivots.shape, 0) * pivots.shape[1]
    order += lax.broadcasted_iota(jnp.int32, pivots.shape, 1)
    in_line = (pivots >= line) & (pivots < line + mu * NBAS)
    local = jnp.full_like(pivots, -1)
    for m in range(mu):
        inside = pivots - base - m * NBAS
        local = jnp.where((inside >= 0) & (inside < nu), inside + m * nu, local)
    owned = jnp.sum((local >= 0).astype(jnp.int32))

    def find(i, carry):
        last, count = carry
        p = jnp.min(jnp.where((local >= 0) & (order > last), order, n))
        rank = jnp.sum((in_line & (order < p)).astype(jnp.int32))
        slot = rank - round_index * slots
        todo_ref[0, count] = slot
        todo_ref[1, count] = jnp.max(jnp.where(order == p, local, -1))
        return p, count + ((slot >= 0) & (slot < slots)).astype(jnp.int32)

    _, total = lax.fori_loop(0, owned, find, (jnp.int32(-1), jnp.int32(0)))

    def fetch(row, i):
        m = jnp.int32(0)
        for step in range(1, mu):
            m += (row >= step * nu).astype(jnp.int32)
        start = pl.multiple_of((row - m * nu) // group * group, group)
        return pltpu.make_async_copy(prev_ref.at[m, pl.ds(start, group)], held.at[i], sems.at[i])

    def batch(b, _):
        first = b * depth
        size = jnp.minimum(total - first, depth)

        def begin(i, _):
            fetch(todo_ref[1, first + i], i).start()
            return 0

        def end(i, _):
            row = todo_ref[1, first + i]
            fetch(row, i).wait()
            rows = held[i].astype(F32)
            keep = lax.broadcasted_iota(jnp.int32, rows.shape, 0) == row % group
            picked = jnp.sum(jnp.where(keep, rows, 0.0), axis=0, keepdims=True)
            acc_ref[pl.ds(todo_ref[0, first + i], 1), :] = picked
            return 0

        lax.fori_loop(0, size, begin, 0)
        lax.fori_loop(0, size, end, 0)
        return 0

    lax.fori_loop(0, (total + depth - 1) // depth, batch, 0)
    out_ref[...] = acc_ref[...].astype(BF16)


def pick_rows(where_from, pivots, previous):
    mu, nu, k = previous.shape
    n = pivots.shape[0]
    lanes = 128
    return pl.pallas_call(
        pick_kernel,
        out_shape=jax.ShapeDtypeStruct((SLOTS, k), BF16),
        in_specs=[
            pl.BlockSpec(memory_space=pltpu.SMEM),
            pl.BlockSpec(memory_space=pltpu.VMEM),
            pl.BlockSpec(memory_space=pltpu.HBM),
        ],
        out_specs=pl.BlockSpec(memory_space=pltpu.VMEM),
        scratch_shapes=[
            pltpu.VMEM((SLOTS, k), F32),
            pltpu.VMEM((16, 16, k), BF16),
            pltpu.SemaphoreType.DMA((16,)),
            pltpu.SMEM((2, n + 1), jnp.int32),
        ],
        compiler_params=pltpu.CompilerParams(vmem_limit_bytes=4 << 20),
        cost_estimate=pl.CostEstimate(flops=n * k, bytes_accessed=2 * n * k, transcendentals=0),
        name="pick_rows",
    )(where_from, pivots.reshape(n // lanes, lanes), previous)


def select_kernel(round_ref, piv_ref, slots_ref, so_far_ref, out_ref, rounds_ref, *, per_line):
    total, _ = slots_ref.shape
    n = piv_ref.shape[1]
    along = jnp.broadcast_to(piv_ref[...].astype(F32), (n, n))
    lines_along = jnp.floor((along + 0.5) * (1.0 / per_line))
    lines = lines_along.T
    earlier = lax.broadcasted_iota(jnp.int32, (n, n), 1) < lax.broadcasted_iota(jnp.int32, (n, n), 0)
    same = jnp.where((lines_along == lines) & earlier, 1.0, 0.0)
    rank = jnp.sum(same, axis=1, keepdims=True)
    rounds_ref[0] = jnp.max(rank).astype(jnp.int32) // SLOTS + 1
    rank = rank - (round_ref[0] * SLOTS).astype(F32)
    mine = (rank >= 0.0) & (rank < SLOTS)
    index = jnp.where(mine, lines[:, :1] * SLOTS + rank, -1.0).astype(jnp.int32)
    hot = index == lax.broadcasted_iota(jnp.int32, (n, total), 1)
    hot = jnp.where(hot, 1.0, 0.0).astype(BF16)
    picked = jnp.dot(hot, slots_ref[...], preferred_element_type=F32)
    out_ref[...] = (picked + so_far_ref[...].astype(F32)).astype(BF16)


def select_rows(round_index, pivots, slots, so_far, per_line):
    total, width = slots.shape
    n = pivots.shape[0]
    vmem = pl.BlockSpec(memory_space=pltpu.VMEM)
    return pl.pallas_call(
        functools.partial(select_kernel, per_line=per_line),
        out_shape=(
            jax.ShapeDtypeStruct((n, width), BF16),
            jax.ShapeDtypeStruct((1,), jnp.int32),
        ),
        in_specs=[pl.BlockSpec(memory_space=pltpu.SMEM), vmem, vmem, vmem],
        out_specs=(vmem, pl.BlockSpec(memory_space=pltpu.SMEM)),
        compiler_params=pltpu.CompilerParams(vmem_limit_bytes=8 << 20),
        cost_estimate=pl.CostEstimate(
            flops=2 * n * total * width, bytes_accessed=2 * total * width, transcendentals=0
        ),
        name="select_rows",
    )(round_index, pivots.reshape(1, n), slots, so_far)


def spread_kernel(came_ref, out_ref):
    total = jnp.sum(came_ref[...].astype(F32), axis=0).astype(BF16)
    half = out_ref.shape[2]
    for c in range(2):
        piece = total[:, c * half : (c + 1) * half]

        @pl.loop(0, out_ref.shape[0] // 2)
        def _(chip):
            out_ref[2 * chip + c] = piece


def spread(came, n_rows):
    n_grp, slots, k = came.shape
    vmem = pl.BlockSpec(memory_space=pltpu.VMEM)
    return pl.pallas_call(
        spread_kernel,
        out_shape=jax.ShapeDtypeStruct((n_rows, slots, k // 2), BF16),
        in_specs=[vmem],
        out_specs=vmem,
        compiler_params=pltpu.CompilerParams(vmem_limit_bytes=4 << 20),
        cost_estimate=pl.CostEstimate(
            flops=n_grp * slots * k, bytes_accessed=n_rows * slots * k, transcendentals=0
        ),
        name="spread",
    )(came)


def preload_kernel(prev_ref, after_ref, out_ref, sems):
    copies = [
        pltpu.make_async_copy(prev_ref.at[m], out_ref.at[m], sems.at[m])
        for m in range(prev_ref.shape[0])
    ]
    for copy in copies:
        copy.start()
    for copy in copies:
        copy.wait()


def preload(previous, after):
    return pl.pallas_call(
        preload_kernel,
        out_shape=jax.ShapeDtypeStruct(previous.shape, previous.dtype),
        in_specs=[pl.BlockSpec(memory_space=pltpu.HBM), pl.BlockSpec(memory_space=pl.ANY)],
        out_specs=pl.BlockSpec(memory_space=pltpu.VMEM),
        scratch_shapes=[pltpu.SemaphoreType.DMA((previous.shape[0],))],
        compiler_params=pltpu.CompilerParams(vmem_limit_bytes=8 << 20),
        cost_estimate=pl.CostEstimate(
            flops=0, bytes_accessed=2 * previous.size, transcendentals=0
        ),
        name="preload",
    )(previous, after)


def vectors_kernel(
    core_ref, cols_ref, prev_ref, mine_ref, other_ref, inv_ref, new_ref, turned_ref, made, store
):
    mu = prev_ref.shape[0]

    def store_of(m):
        return pltpu.make_async_copy(made.at[m], new_ref.at[m], store.at[m])

    @pl.loop(0, mu)
    def _(m):
        mine, other = mine_ref[...].astype(F32), other_ref[...].astype(F32)
        first = core_ref[0] == 0
        rows = jnp.concatenate(
            [jnp.where(first, mine, other), jnp.where(first, other, mine)], axis=1
        ).astype(BF16)
        contract = (((1,), (1,)), ((), ()))
        correction = lax.dot_general(prev_ref[m], rows, contract, preferred_element_type=F32)
        residual = (cols_ref[m].astype(F32) - correction).astype(BF16)
        inv = inv_ref[...]
        row, column = (lax.broadcasted_iota(jnp.int32, inv.shape, d) for d in (0, 1))
        upper = jnp.where(row > column, 0.0, inv.astype(F32)).astype(BF16)
        new = jnp.dot(residual, upper, preferred_element_type=F32).astype(BF16)
        made[m] = new
        store_of(m).start()
        turned_ref[m] = new.T

    for m in range(mu):
        store_of(m).wait()


def vectors(core, pivot_columns, previous, mine, other, pivot_inverse):
    mu, nu, k = previous.shape
    n = pivot_columns.shape[2]
    vmem = pl.BlockSpec(memory_space=pltpu.VMEM)
    return pl.pallas_call(
        vectors_kernel,
        out_shape=(
            jax.ShapeDtypeStruct((mu, nu, n), BF16),
            jax.ShapeDtypeStruct((mu, n, nu), BF16),
        ),
        in_specs=[pl.BlockSpec(memory_space=pltpu.SMEM), vmem, vmem, vmem, vmem, vmem],
        out_specs=(pl.BlockSpec(memory_space=pl.ANY), vmem),
        scratch_shapes=[pltpu.VMEM((mu, nu, n), BF16), pltpu.SemaphoreType.DMA((mu,))],
        compiler_params=pltpu.CompilerParams(vmem_limit_bytes=24 << 20),
        cost_estimate=pl.CostEstimate(
            flops=2 * mu * nu * n * (k + n),
            bytes_accessed=2 * mu * nu * (k + 3 * n),
            transcendentals=0,
        ),
        name="vectors",
    )(core, pivot_columns, previous, mine, other, pivot_inverse)


def parts_kernel(me_ref, turned_ref, orb_ref, *out_refs, ahead, owners):
    mu, n, nu = turned_ref.shape
    width = orb_ref.shape[1] // owners
    keep, last = out_refs[0].shape[-2:]
    columns = []
    for a in ahead:
        start = pl.multiple_of(lax.rem(me_ref[0] + a, owners) * width, width)
        columns.append(orb_ref[:, pl.ds(start, width)])
    columns = columns[0] if len(columns) == 1 else jnp.concatenate(columns, axis=1)
    for m in range(mu):
        part = jnp.dot(turned_ref[m], columns, preferred_element_type=F32)
        if len(out_refs) == 2:
            half = n // 2
            for h, out_ref in enumerate(out_refs):
                piece = part[h * half : (h + 1) * half].reshape(half // keep, keep, last)
                out_ref[:, m] = piece.astype(out_ref.dtype)
        else:
            for q in range(len(ahead)):
                piece = part[:, q * width : (q + 1) * width].reshape(n // keep, keep, width)
                out_refs[0][q, :, m] = piece


def parts(me, turned, orbitals, ahead, owners, dests, send=False):
    mu, n, nu = turned.shape
    width = orbitals.shape[1] // owners
    if send:
        shape = (dests // 2, mu, n // dests, width)
        out_shape = (jax.ShapeDtypeStruct(shape, BF16),) * 2
    else:
        shape = (len(ahead), dests, mu, n // dests, width)
        out_shape = jax.ShapeDtypeStruct(shape, F32)
    vmem = pl.BlockSpec(memory_space=pltpu.VMEM)
    return pl.pallas_call(
        functools.partial(parts_kernel, ahead=ahead, owners=owners),
        out_shape=out_shape,
        in_specs=[pl.BlockSpec(memory_space=pltpu.SMEM), vmem, vmem],
        out_specs=(vmem, vmem) if send else vmem,
        compiler_params=pltpu.CompilerParams(vmem_limit_bytes=20 << 20),
        cost_estimate=pl.CostEstimate(
            flops=2 * mu * n * nu * width * len(ahead),
            bytes_accessed=2 * mu * n * nu,
            transcendentals=0,
        ),
        name="parts",
    )(me, turned, orbitals)


def join_kernel(own_ref, came_ref, out_ref, *, second):
    half = came_ref.shape[0]
    mine, other = (slice(half, None), slice(0, half)) if second else (slice(0, half), slice(half, None))
    out_ref[mine] = (own_ref[0, mine] + came_ref[...].astype(F32)).astype(BF16)
    out_ref[other] = own_ref[0, other].astype(BF16)


def join(part, which, came, second):
    shape = part.shape[1:]
    return pl.pallas_call(
        functools.partial(join_kernel, second=second),
        grid=(1,),
        out_shape=jax.ShapeDtypeStruct(shape, BF16),
        in_specs=[
            pl.BlockSpec((1,) + shape, lambda i: (which, 0, 0, 0, 0)),
            pl.BlockSpec(came.shape, lambda i: (0, 0, 0, 0)),
        ],
        out_specs=pl.BlockSpec(shape, lambda i: (0, 0, 0, 0)),
        compiler_params=pltpu.CompilerParams(vmem_limit_bytes=6 << 20),
        cost_estimate=pl.CostEstimate(
            flops=came.size, bytes_accessed=12 * came.size, transcendentals=0
        ),
        name="join",
    )(part, came)


def reduce_to_owner(me, turned, orbitals, owners, dests):
    far = owners // 2

    def hop(x, way):
        return lax.ppermute(x, "grp", [(i, (i + way) % owners) for i in range(owners)])

    def own(ahead, **more):
        return parts(me, turned, orbitals, ahead, owners, dests, **more)

    right, left = own((far,), send=True)
    right, left = hop(right, 1), hop(left, -1)
    near = own((far - 1, far + 1))
    right, left = hop(join(near, 0, right, False), 1), hop(join(near, 1, left, True), -1)
    for ahead in range(far - 2, 0, -1):
        near = own((ahead, owners - ahead))
        right, left = (
            hop((near[q] + x.astype(F32)).astype(BF16), way)
            for q, (x, way) in enumerate(((right, 1), (left, -1)))
        )
    return own((0,))[0] + right.astype(F32) + left.astype(F32)


def final_kernel(half_ref, slab_ref, out_ref):
    rows, width = half_ref.shape
    mu = slab_ref.shape[0]
    keep = rows // mu
    slab_t = slab_ref[...].T
    slab_t = jnp.concatenate([slab_t, slab_t], axis=1)
    for p in range(0, keep, 2):
        pair = jnp.concatenate(
            [half_ref[pl.ds(q, mu, stride=keep), :] for q in (p, p + 1)], axis=1
        )
        high = pair.astype(BF16)
        low = (pair - high.astype(F32)).astype(BF16)
        both = jnp.dot(slab_t, jnp.concatenate([high, low], axis=0), preferred_element_type=F32)
        out_ref[p] = both[:, :width].astype(BF16)
        out_ref[p + 1] = both[:, width:].astype(BF16)


def final(half, slab):
    mu, occ = slab.shape
    rows, width = half.shape
    keep = rows // mu
    return pl.pallas_call(
        final_kernel,
        out_shape=jax.ShapeDtypeStruct((keep, occ, width), BF16),
        compiler_params=pltpu.CompilerParams(vmem_limit_bytes=16 << 20),
        cost_estimate=pl.CostEstimate(
            flops=4 * rows * width * occ,
            bytes_accessed=2 * keep * width * (2 * mu + occ),
            transcendentals=0,
        ),
        name="final",
    )(half, slab)


def exchange(x, axis):
    return lax.all_to_all(x, axis, split_axis=0, concat_axis=0, tiled=True)


def pivot_halves(n_rows, n_grp, pivots, previous):
    mu, nu, k = previous.shape
    n = pivots.shape[0]
    half = k // 2
    per_line = mu * NBAS
    line = lax.axis_index("rows") * per_line
    base = line + lax.axis_index("grp") * nu
    line, base = line.astype(jnp.int32), base.astype(jnp.int32)

    def one_round(index, so_far):
        index = jnp.asarray(index, jnp.int32)
        picked = pick_rows(jnp.stack([line, base, index]), pivots, previous)
        came = exchange(jnp.broadcast_to(picked, (n_grp,) + picked.shape), "grp")
        slots = exchange(spread(came, n_rows), "rows")
        return select_rows(
            index.reshape(1), pivots, slots.reshape(n_rows * SLOTS, half), so_far, per_line
        )

    mine, rounds = one_round(0, jnp.zeros((n, half), BF16))
    start, mine, rounds = lax.optimization_barrier((jnp.int32(1), mine, rounds))
    mine = lax.fori_loop(start, rounds[0], lambda i, rows: one_round(i, rows)[0], mine)
    other = lax.ppermute(mine, "rows", [(i, i ^ 1) for i in range(n_rows)])
    return mine, other


def per_device(n_rows, n_grp, pivot_columns, previous, pivots, pivot_inverse, orbitals, slab_orbitals):
    in_hbm = pltpu.with_memory_space_constraint(previous, pltpu.HBM)
    mine, other = pivot_halves(n_rows, n_grp, pivots, in_hbm)
    core = (lax.axis_index("rows") % 2).reshape(1).astype(jnp.int32)
    me = lax.axis_index("grp").reshape(1).astype(jnp.int32)
    close = preload(in_hbm, mine)
    new_vectors, turned = vectors(core, pivot_columns, close, mine, other, pivot_inverse)
    half = exchange(reduce_to_owner(me, turned, orbitals, n_grp, n_rows), "rows")
    return new_vectors, final(half.reshape(-1, half.shape[-1]), slab_orbitals)


def solution(mesh):
    in_specs = (P("rows", "grp", None), P("rows", "grp", None), P(), P(), P("grp", None), P())
    out_specs = (P("rows", "grp", None), P("rows", None, "grp"))
    body = functools.partial(per_device, mesh.shape["rows"], mesh.shape["grp"])
    return jax.shard_map(body, mesh=mesh, in_specs=in_specs, out_specs=out_specs, check_vma=False)
```

```python
import functools

import jax
import jax.numpy as jnp
from jax import lax
from jax.experimental import pallas as pl
from jax.experimental.pallas import tpu as pltpu
from jax.sharding import PartitionSpec as P

NBAS = 10240
F32 = jnp.float32
BF16 = jnp.bfloat16
DEPTH = 8
SLOTS = 24
PARTS = 3


def pick_kernel(where_from_ref, piv_ref, prev_ref, out_ref, acc_ref, held, sems, rows_ref):
    mu, nu, _ = prev_ref.shape
    depth, group, _ = held.shape
    base, turn = where_from_ref[1], where_from_ref[2]
    acc_ref[...] = jnp.zeros_like(acc_ref)
    pivots = piv_ref[...]
    order = lax.broadcasted_iota(jnp.int32, pivots.shape, 0) * pivots.shape[1]
    order += lax.broadcasted_iota(jnp.int32, pivots.shape, 1)
    many = 1 << (mu * nu - 1).bit_length()
    last = many * pivots.size
    keys = jnp.full_like(pivots, last)
    for m in range(mu):
        inside = pivots - base - m * NBAS
        keys = jnp.where((inside >= 0) & (inside < nu), order * many + inside + m * nu, keys)
    owned = jnp.sum((keys < last).astype(jnp.int32))
    skip = turn * depth
    total = jnp.clip(owned - skip, 0, depth)

    def fetch(row, i):
        m = jnp.int32(0)
        for step in range(1, mu):
            m += (row >= step * nu).astype(jnp.int32)
        start = pl.multiple_of((row - m * nu) // group * group, group)
        return pltpu.make_async_copy(prev_ref.at[m, pl.ds(start, group)], held.at[i], sems.at[i])

    def find(i, key):
        key = jnp.min(jnp.where(keys > key, keys, last))

        @pl.when(i >= skip)
        def _():
            row = key & (many - 1)
            rows_ref[i - skip] = row
            fetch(row, i - skip).start()

        return key

    lax.fori_loop(0, skip + total, find, jnp.int32(-1))

    def place(i, _):
        row = rows_ref[i]
        fetch(row, i).wait()
        rows = held[i].astype(F32)
        keep = lax.broadcasted_iota(jnp.int32, rows.shape, 0) == row % group
        acc_ref[pl.ds(i, 1), :] = jnp.sum(jnp.where(keep, rows, 0.0), axis=0, keepdims=True)
        return 0

    lax.fori_loop(0, total, place, 0)
    out_ref[...] = acc_ref[...].astype(BF16)


def pick_rows(where_from, pivots, previous):
    n = pivots.shape[0]
    k = previous.shape[2]
    lanes = 128
    return pl.pallas_call(
        pick_kernel,
        out_shape=jax.ShapeDtypeStruct((DEPTH, k), BF16),
        in_specs=[
            pl.BlockSpec(memory_space=pltpu.SMEM),
            pl.BlockSpec(memory_space=pltpu.VMEM),
            pl.BlockSpec(memory_space=pltpu.HBM),
        ],
        out_specs=pl.BlockSpec(memory_space=pltpu.VMEM),
        scratch_shapes=[
            pltpu.VMEM((DEPTH, k), F32),
            pltpu.VMEM((DEPTH, 16, k), BF16),
            pltpu.SemaphoreType.DMA((DEPTH,)),
            pltpu.SMEM((DEPTH,), jnp.int32),
        ],
        compiler_params=pltpu.CompilerParams(vmem_limit_bytes=4 << 20),
        cost_estimate=pl.CostEstimate(flops=n * k, bytes_accessed=2 * n * k, transcendentals=0),
        name="pick_rows",
    )(where_from, pivots.reshape(n // lanes, lanes), previous)


def whole_part(x, by):
    return jnp.floor((x + 0.5) * (1.0 / by))


def select_kernel(round_ref, piv_ref, slots_ref, so_far_ref, out_ref, rounds_ref, *, per_line, nu, owners):
    total, _ = slots_ref.shape
    n = piv_ref.shape[1]
    pivot = piv_ref[...].astype(F32)
    line = whole_part(pivot, per_line)
    inside = pivot - line * per_line
    inside = inside - whole_part(inside, NBAS) * NBAS
    device = jnp.broadcast_to(line * owners + whole_part(inside, nu), (n, n))
    mine = device.T
    before = lax.broadcasted_iota(jnp.int32, (n, n), 1) < lax.broadcasted_iota(jnp.int32, (n, n), 0)
    rank = jnp.sum(jnp.where((device == mine) & before, 1.0, 0.0), axis=1, keepdims=True)
    turn = whole_part(rank, DEPTH)
    turns = jnp.broadcast_to(turn, (n, n))
    my_line = whole_part(mine, owners)
    ahead = (device >= my_line * owners) & (device < mine) & (turns.T == turns)
    place = jnp.sum(jnp.where(ahead, 1.0, 0.0), axis=1, keepdims=True) + rank - turn * DEPTH
    part = whole_part(place, SLOTS)
    when = turn * PARTS + part
    rounds_ref[0] = jnp.max(when).astype(jnp.int32) + 1
    index = my_line[:, :1] * SLOTS + place - part * SLOTS
    index = jnp.where(when == round_ref[0].astype(F32), index, -1.0).astype(jnp.int32)
    hot = index == lax.broadcasted_iota(jnp.int32, (n, total), 1)
    hot = jnp.where(hot, 1.0, 0.0).astype(BF16)
    picked = jnp.dot(hot, slots_ref[...], preferred_element_type=F32)
    out_ref[...] = (picked + so_far_ref[...].astype(F32)).astype(BF16)


def select_rows(round_index, pivots, slots, so_far, per_line, nu, owners):
    total, width = slots.shape
    n = pivots.shape[0]
    vmem = pl.BlockSpec(memory_space=pltpu.VMEM)
    return pl.pallas_call(
        functools.partial(select_kernel, per_line=per_line, nu=nu, owners=owners),
        out_shape=(
            jax.ShapeDtypeStruct((n, width), BF16),
            jax.ShapeDtypeStruct((1,), jnp.int32),
        ),
        in_specs=[pl.BlockSpec(memory_space=pltpu.SMEM), vmem, vmem, vmem],
        out_specs=(vmem, pl.BlockSpec(memory_space=pltpu.SMEM)),
        compiler_params=pltpu.CompilerParams(vmem_limit_bytes=8 << 20),
        cost_estimate=pl.CostEstimate(
            flops=2 * n * total * width, bytes_accessed=2 * total * width, transcendentals=0
        ),
        name="select_rows",
    )(round_index, pivots.reshape(1, n), slots, so_far)


def spread_kernel(where_from_ref, piv_ref, came_ref, out_ref, *, mu, nu):
    owners, depth, k = came_ref.shape
    n = piv_ref.shape[1]
    line, turn, part = (where_from_ref[i] for i in (0, 2, 3))
    offset = jnp.broadcast_to(piv_ref[...] - line, (owners, n))
    low = lax.broadcasted_iota(jnp.int32, (owners, n), 0) * nu
    count = jnp.zeros((owners, n), F32)
    for m in range(mu):
        inside = offset - m * NBAS - low
        count += jnp.where((inside >= 0) & (inside < nu), 1.0, 0.0)
    count = jnp.sum(count, axis=1, keepdims=True) - (turn * depth).astype(F32)
    count = jnp.clip(count, 0.0, depth)
    wide = (owners, owners * depth)
    slot = lax.broadcasted_iota(jnp.int32, wide, 1) - lax.broadcasted_iota(jnp.int32, wide, 0) * depth
    here = (slot >= 0) & (slot < depth)
    start = jnp.sum(jnp.where(slot >= depth, count, 0.0), axis=0, keepdims=True)
    used = jnp.sum(jnp.where(here & (slot.astype(F32) < count), 1.0, 0.0), axis=0, keepdims=True)
    place = start + jnp.sum(jnp.where(here, slot.astype(F32), 0.0), axis=0, keepdims=True)
    place = place - (part * SLOTS).astype(F32)
    packed = lax.broadcasted_iota(jnp.int32, (SLOTS, wide[1]), 0).astype(F32)
    hot = jnp.where((packed == place) & (used > 0.0), 1.0, 0.0).astype(BF16)
    rows = came_ref[...].astype(F32).reshape(wide[1], k).astype(BF16)
    rows = jnp.dot(hot, rows, preferred_element_type=F32).astype(BF16)
    half = out_ref.shape[2]
    for c in range(2):
        piece = rows[:, c * half : (c + 1) * half]

        @pl.loop(0, out_ref.shape[0] // 2)
        def _(chip):
            out_ref[2 * chip + c] = piece


def spread(where_from, pivots, came, n_rows, mu, nu):
    k = came.shape[2]
    n = pivots.shape[0]
    vmem = pl.BlockSpec(memory_space=pltpu.VMEM)
    return pl.pallas_call(
        functools.partial(spread_kernel, mu=mu, nu=nu),
        out_shape=jax.ShapeDtypeStruct((n_rows, SLOTS, k // 2), BF16),
        in_specs=[pl.BlockSpec(memory_space=pltpu.SMEM), vmem, vmem],
        out_specs=vmem,
        compiler_params=pltpu.CompilerParams(vmem_limit_bytes=4 << 20),
        cost_estimate=pl.CostEstimate(
            flops=came.size, bytes_accessed=n_rows * SLOTS * k, transcendentals=0
        ),
        name="spread",
    )(where_from, pivots.reshape(1, n), came)


def preload_kernel(prev_ref, after_ref, out_ref, sem):
    copy = pltpu.make_async_copy(prev_ref.at[0], out_ref, sem)
    copy.start()
    copy.wait()


def preload(previous, after):
    return pl.pallas_call(
        preload_kernel,
        out_shape=jax.ShapeDtypeStruct(previous.shape[1:], previous.dtype),
        in_specs=[pl.BlockSpec(memory_space=pltpu.HBM), pl.BlockSpec(memory_space=pl.ANY)],
        out_specs=pl.BlockSpec(memory_space=pltpu.VMEM),
        scratch_shapes=[pltpu.SemaphoreType.DMA],
        compiler_params=pltpu.CompilerParams(vmem_limit_bytes=4 << 20),
        cost_estimate=pl.CostEstimate(
            flops=0, bytes_accessed=previous.size // 2, transcendentals=0
        ),
        name="preload",
    )(previous, after)


def vectors_kernel(
    core_ref, cols_ref, close_ref, prev_ref, mine_ref, other_ref, inv_ref, new_ref, turned_ref, came, made, load, store
):
    mu = cols_ref.shape[0]

    def load_of(m):
        return pltpu.make_async_copy(prev_ref.at[m], came.at[m - 1], load.at[m - 1])

    def store_of(m):
        return pltpu.make_async_copy(made.at[m], new_ref.at[m], store.at[m])

    def step(m, prev):
        mine, other = mine_ref[...].astype(F32), other_ref[...].astype(F32)
        first = core_ref[0] == 0
        rows = jnp.concatenate(
            [jnp.where(first, mine, other), jnp.where(first, other, mine)], axis=1
        ).astype(BF16)
        contract = (((1,), (1,)), ((), ()))
        correction = lax.dot_general(prev, rows, contract, preferred_element_type=F32)
        residual = (cols_ref[m].astype(F32) - correction).astype(BF16)
        inv = inv_ref[...]
        row, column = (lax.broadcasted_iota(jnp.int32, inv.shape, d) for d in (0, 1))
        upper = jnp.where(row > column, 0.0, inv.astype(F32)).astype(BF16)
        new = jnp.dot(residual, upper, preferred_element_type=F32).astype(BF16)
        made[m] = new
        store_of(m).start()
        turned_ref[m] = new.T

    load_of(1).start()
    step(0, close_ref[...])

    @pl.loop(1, mu)
    def _(m):
        load_of(m).wait()

        @pl.when(m + 1 < mu)
        def _():
            load_of(m + 1).start()

        step(m, came[m - 1])

    for m in range(mu):
        store_of(m).wait()


def vectors(core, pivot_columns, close, previous, mine, other, pivot_inverse):
    mu, nu, k = previous.shape
    n = pivot_columns.shape[2]
    vmem = pl.BlockSpec(memory_space=pltpu.VMEM)
    hbm = pl.BlockSpec(memory_space=pltpu.HBM)
    return pl.pallas_call(
        vectors_kernel,
        out_shape=(
            jax.ShapeDtypeStruct((mu, nu, n), BF16),
            jax.ShapeDtypeStruct((mu, n, nu), BF16),
        ),
        in_specs=[pl.BlockSpec(memory_space=pltpu.SMEM), vmem, vmem, hbm, vmem, vmem, vmem],
        out_specs=(pl.BlockSpec(memory_space=pl.ANY), vmem),
        scratch_shapes=[
            pltpu.VMEM((mu - 1, nu, k), BF16),
            pltpu.VMEM((mu, nu, n), BF16),
            pltpu.SemaphoreType.DMA((mu - 1,)),
            pltpu.SemaphoreType.DMA((mu,)),
        ],
        compiler_params=pltpu.CompilerParams(vmem_limit_bytes=24 << 20),
        cost_estimate=pl.CostEstimate(
            flops=2 * mu * nu * n * (k + n),
            bytes_accessed=2 * mu * nu * (k + 3 * n),
            transcendentals=0,
        ),
        name="vectors",
    )(core, pivot_columns, close, previous, mine, other, pivot_inverse)


def parts_kernel(me_ref, turned_ref, orb_ref, *out_refs, ahead, owners):
    mu, n, nu = turned_ref.shape
    width = orb_ref.shape[1] // owners
    keep, last = out_refs[0].shape[-2:]
    columns = []
    for a in ahead:
        start = pl.multiple_of(lax.rem(me_ref[0] + a, owners) * width, width)
        columns.append(orb_ref[:, pl.ds(start, width)])
    columns = columns[0] if len(columns) == 1 else jnp.concatenate(columns, axis=1)
    for m in range(mu):
        part = jnp.dot(turned_ref[m], columns, preferred_element_type=F32)
        if len(out_refs) == 2:
            half = n // 2
            for h, out_ref in enumerate(out_refs):
                piece = part[h * half : (h + 1) * half].reshape(half // keep, keep, last)
                out_ref[:, m] = piece.astype(out_ref.dtype)
        else:
            for q in range(len(ahead)):
                piece = part[:, q * width : (q + 1) * width].reshape(n // keep, keep, width)
                out_refs[0][q, :, m] = piece


def parts(me, turned, orbitals, ahead, owners, dests, send=False):
    mu, n, nu = turned.shape
    width = orbitals.shape[1] // owners
    if send:
        shape = (dests // 2, mu, n // dests, width)
        out_shape = (jax.ShapeDtypeStruct(shape, BF16),) * 2
    else:
        shape = (len(ahead), dests, mu, n // dests, width)
        out_shape = jax.ShapeDtypeStruct(shape, F32)
    vmem = pl.BlockSpec(memory_space=pltpu.VMEM)
    return pl.pallas_call(
        functools.partial(parts_kernel, ahead=ahead, owners=owners),
        out_shape=out_shape,
        in_specs=[pl.BlockSpec(memory_space=pltpu.SMEM), vmem, vmem],
        out_specs=(vmem, vmem) if send else vmem,
        compiler_params=pltpu.CompilerParams(vmem_limit_bytes=20 << 20),
        cost_estimate=pl.CostEstimate(
            flops=2 * mu * n * nu * width * len(ahead),
            bytes_accessed=2 * mu * n * nu,
            transcendentals=0,
        ),
        name="parts",
    )(me, turned, orbitals)


def join_kernel(own_ref, came_ref, out_ref, *, second):
    half = came_ref.shape[0]
    mine, other = (slice(half, None), slice(0, half)) if second else (slice(0, half), slice(half, None))
    out_ref[mine] = (own_ref[0, mine] + came_ref[...].astype(F32)).astype(BF16)
    out_ref[other] = own_ref[0, other].astype(BF16)


def join(part, which, came, second):
    shape = part.shape[1:]
    return pl.pallas_call(
        functools.partial(join_kernel, second=second),
        grid=(1,),
        out_shape=jax.ShapeDtypeStruct(shape, BF16),
        in_specs=[
            pl.BlockSpec((1,) + shape, lambda i: (which, 0, 0, 0, 0)),
            pl.BlockSpec(came.shape, lambda i: (0, 0, 0, 0)),
        ],
        out_specs=pl.BlockSpec(shape, lambda i: (0, 0, 0, 0)),
        compiler_params=pltpu.CompilerParams(vmem_limit_bytes=6 << 20),
        cost_estimate=pl.CostEstimate(
            flops=came.size, bytes_accessed=12 * came.size, transcendentals=0
        ),
        name="join",
    )(part, came)


def reduce_to_owner(me, turned, orbitals, owners, dests):
    far = owners // 2

    def hop(x, way):
        return lax.ppermute(x, "grp", [(i, (i + way) % owners) for i in range(owners)])

    def own(ahead, **more):
        return parts(me, turned, orbitals, ahead, owners, dests, **more)

    right, left = own((far,), send=True)
    right, left = hop(right, 1), hop(left, -1)
    near = own((far - 1, far + 1))
    right, left = hop(join(near, 0, right, False), 1), hop(join(near, 1, left, True), -1)
    for ahead in range(far - 2, 0, -1):
        near = own((ahead, owners - ahead))
        right, left = (
            hop((near[q] + x.astype(F32)).astype(BF16), way)
            for q, (x, way) in enumerate(((right, 1), (left, -1)))
        )
    return own((0,))[0] + right.astype(F32) + left.astype(F32)


def final_kernel(half_ref, slab_ref, out_ref):
    rows, width = half_ref.shape
    mu = slab_ref.shape[0]
    keep = rows // mu
    slab_t = slab_ref[...].T
    slab_t = jnp.concatenate([slab_t, slab_t], axis=1)
    for p in range(0, keep, 2):
        pair = jnp.concatenate(
            [half_ref[pl.ds(q, mu, stride=keep), :] for q in (p, p + 1)], axis=1
        )
        high = pair.astype(BF16)
        low = (pair - high.astype(F32)).astype(BF16)
        both = jnp.dot(slab_t, jnp.concatenate([high, low], axis=0), preferred_element_type=F32)
        out_ref[p] = both[:, :width].astype(BF16)
        out_ref[p + 1] = both[:, width:].astype(BF16)


def final(half, slab):
    mu, occ = slab.shape
    rows, width = half.shape
    keep = rows // mu
    return pl.pallas_call(
        final_kernel,
        out_shape=jax.ShapeDtypeStruct((keep, occ, width), BF16),
        compiler_params=pltpu.CompilerParams(vmem_limit_bytes=16 << 20),
        cost_estimate=pl.CostEstimate(
            flops=4 * rows * width * occ,
            bytes_accessed=2 * keep * width * (2 * mu + occ),
            transcendentals=0,
        ),
        name="final",
    )(half, slab)


def exchange(x, axis):
    return lax.all_to_all(x, axis, split_axis=0, concat_axis=0, tiled=True)


def pivot_halves(n_rows, n_grp, pivots, previous):
    mu, nu, k = previous.shape
    n = pivots.shape[0]
    half = k // 2
    per_line = mu * NBAS
    line = lax.axis_index("rows") * per_line
    base = line + lax.axis_index("grp") * nu
    line, base = line.astype(jnp.int32), base.astype(jnp.int32)

    def one_round(index, so_far):
        index = jnp.asarray(index, jnp.int32)
        turn, part = index // PARTS, index % PARTS
        where_from = jnp.stack([line, base, turn, part])
        picked = pick_rows(where_from, pivots, previous)
        came = exchange(jnp.broadcast_to(picked, (n_grp,) + picked.shape), "grp")
        messages = spread(where_from, pivots, came, n_rows, mu, nu)
        slots = exchange(messages, "rows").reshape(n_rows * SLOTS, half)
        return select_rows(index.reshape(1), pivots, slots, so_far, per_line, nu, n_grp)

    mine, rounds = one_round(0, jnp.zeros((n, half), BF16))
    start, mine, rounds = lax.optimization_barrier((jnp.int32(1), mine, rounds))
    mine = lax.fori_loop(start, rounds[0], lambda i, rows: one_round(i, rows)[0], mine)
    other = lax.ppermute(mine, "rows", [(i, i ^ 1) for i in range(n_rows)])
    return mine, other


def per_device(n_rows, n_grp, pivot_columns, previous, pivots, pivot_inverse, orbitals, slab_orbitals):
    in_hbm = pltpu.with_memory_space_constraint(previous, pltpu.HBM)
    mine, other = pivot_halves(n_rows, n_grp, pivots, in_hbm)
    core = (lax.axis_index("rows") % 2).reshape(1).astype(jnp.int32)
    me = lax.axis_index("grp").reshape(1).astype(jnp.int32)
    close = preload(in_hbm, mine)
    new_vectors, turned = vectors(
        core, pivot_columns, close, in_hbm, mine, other, pivot_inverse
    )
    half = exchange(reduce_to_owner(me, turned, orbitals, n_grp, n_rows), "rows")
    return new_vectors, final(half.reshape(-1, half.shape[-1]), slab_orbitals)


def solution(mesh):
    in_specs = (P("rows", "grp", None), P("rows", "grp", None), P(), P(), P("grp", None), P())
    out_specs = (P("rows", "grp", None), P("rows", None, "grp"))
    body = functools.partial(per_device, mesh.shape["rows"], mesh.shape["grp"])
    return jax.shard_map(body, mesh=mesh, in_specs=in_specs, out_specs=out_specs, check_vma=False)
```

```python
import functools

import jax
import jax.numpy as jnp
from jax import lax
from jax.experimental import pallas as pl
from jax.experimental.pallas import tpu as pltpu
from jax.sharding import PartitionSpec as P

NBAS = 10240
F32 = jnp.float32
BF16 = jnp.bfloat16
DEPTH = 8
SLOTS = 64
PARTS = 4
PIECES = 4


def pick_kernel(where_from_ref, piv_ref, prev_ref, out_ref, acc_ref, held, sems, rows_ref):
    mu, nu, _ = prev_ref.shape
    depth, group, _ = held.shape
    base, turn = where_from_ref[0], where_from_ref[2]
    acc_ref[...] = jnp.zeros_like(acc_ref)
    pivots = piv_ref[...]
    order = lax.broadcasted_iota(jnp.int32, pivots.shape, 0) * pivots.shape[1]
    order += lax.broadcasted_iota(jnp.int32, pivots.shape, 1)
    many = 1 << (mu * nu - 1).bit_length()
    last = many * pivots.size
    keys = jnp.full_like(pivots, last)
    for m in range(mu):
        inside = pivots - base - m * NBAS
        keys = jnp.where((inside >= 0) & (inside < nu), order * many + inside + m * nu, keys)
    owned = jnp.sum((keys < last).astype(jnp.int32))
    skip = turn * depth
    total = jnp.clip(owned - skip, 0, depth)

    def fetch(row, i):
        m = jnp.int32(0)
        for step in range(1, mu):
            m += (row >= step * nu).astype(jnp.int32)
        start = pl.multiple_of((row - m * nu) // group * group, group)
        return pltpu.make_async_copy(prev_ref.at[m, pl.ds(start, group)], held.at[i], sems.at[i])

    def find(i, key):
        key = jnp.min(jnp.where(keys > key, keys, last))

        @pl.when(i >= skip)
        def _():
            row = key & (many - 1)
            rows_ref[i - skip] = row
            fetch(row, i - skip).start()

        return key

    lax.fori_loop(0, skip + total, find, jnp.int32(-1))

    def place(i, _):
        row = rows_ref[i]
        fetch(row, i).wait()
        rows = held[i].astype(F32)
        keep = lax.broadcasted_iota(jnp.int32, rows.shape, 0) == row % group
        acc_ref[pl.ds(i, 1), :] = jnp.sum(jnp.where(keep, rows, 0.0), axis=0, keepdims=True)
        return 0

    lax.fori_loop(0, total, place, 0)
    half = out_ref.shape[2]
    for c in range(2):
        piece = acc_ref[:, c * half : (c + 1) * half].astype(BF16)
        for chip in range(out_ref.shape[0] // 2):
            out_ref[2 * chip + c] = piece


def pick_rows(where_from, pivots, previous, n_rows):
    n = pivots.shape[0]
    k = previous.shape[2]
    lanes = 128
    return pl.pallas_call(
        pick_kernel,
        out_shape=jax.ShapeDtypeStruct((n_rows, DEPTH, k // 2), BF16),
        in_specs=[
            pl.BlockSpec(memory_space=pltpu.SMEM),
            pl.BlockSpec(memory_space=pltpu.VMEM),
            pl.BlockSpec(memory_space=pltpu.HBM),
        ],
        out_specs=pl.BlockSpec(memory_space=pltpu.VMEM),
        scratch_shapes=[
            pltpu.VMEM((DEPTH, k), F32),
            pltpu.VMEM((DEPTH, 16, k), BF16),
            pltpu.SemaphoreType.DMA((DEPTH,)),
            pltpu.SMEM((DEPTH,), jnp.int32),
        ],
        compiler_params=pltpu.CompilerParams(vmem_limit_bytes=4 << 20),
        cost_estimate=pl.CostEstimate(flops=n * k, bytes_accessed=2 * n * k, transcendentals=0),
        name="pick_rows",
    )(where_from, pivots.reshape(n // lanes, lanes), previous)


def whole_part(x, by):
    return jnp.floor((x + 0.5) * (1.0 / by))


def select_kernel(round_ref, piv_ref, slots_ref, so_far_ref, out_ref, rounds_ref, *, per_line, nu, n_rows):
    total, _ = slots_ref.shape
    n = piv_ref.shape[1]
    pivot = piv_ref[...].astype(F32)
    line = whole_part(pivot, per_line)
    inside = pivot - line * per_line
    inside = inside - whole_part(inside, NBAS) * NBAS
    device = jnp.broadcast_to(whole_part(inside, nu) * n_rows + line, (n, n))
    mine = device.T
    before = lax.broadcasted_iota(jnp.int32, (n, n), 1) < lax.broadcasted_iota(jnp.int32, (n, n), 0)
    rank = jnp.sum(jnp.where((device == mine) & before, 1.0, 0.0), axis=1, keepdims=True)
    turn = whole_part(rank, DEPTH)
    turns = jnp.broadcast_to(turn, (n, n))
    plane = whole_part(mine, n_rows)
    ahead = (device >= plane * n_rows) & (device < mine) & (turns.T == turns)
    place = jnp.sum(jnp.where(ahead, 1.0, 0.0), axis=1, keepdims=True) + rank - turn * DEPTH
    part = whole_part(place, SLOTS)
    when = turn * PARTS + part
    rounds_ref[0] = jnp.max(when).astype(jnp.int32) + 1
    index = plane[:, :1] * SLOTS + place - part * SLOTS
    index = jnp.where(when == round_ref[0].astype(F32), index, -1.0).astype(jnp.int32)
    hot = index == lax.broadcasted_iota(jnp.int32, (n, total), 1)
    hot = jnp.where(hot, 1.0, 0.0).astype(BF16)
    picked = jnp.dot(hot, slots_ref[...], preferred_element_type=F32)
    out_ref[...] = (picked + so_far_ref[...].astype(F32)).astype(BF16)


def select_rows(round_index, pivots, slots, so_far, per_line, nu, n_rows):
    total, width = slots.shape
    n = pivots.shape[0]
    vmem = pl.BlockSpec(memory_space=pltpu.VMEM)
    return pl.pallas_call(
        functools.partial(select_kernel, per_line=per_line, nu=nu, n_rows=n_rows),
        out_shape=(
            jax.ShapeDtypeStruct((n, width), BF16),
            jax.ShapeDtypeStruct((1,), jnp.int32),
        ),
        in_specs=[pl.BlockSpec(memory_space=pltpu.SMEM), vmem, vmem, vmem],
        out_specs=(vmem, pl.BlockSpec(memory_space=pltpu.SMEM)),
        compiler_params=pltpu.CompilerParams(vmem_limit_bytes=8 << 20),
        cost_estimate=pl.CostEstimate(
            flops=2 * n * total * width, bytes_accessed=2 * total * width, transcendentals=0
        ),
        name="select_rows",
    )(round_index, pivots.reshape(1, n), slots, so_far)


def pack_kernel(where_from_ref, piv_ref, came_ref, out_ref, *, mu, nu):
    n_rows, depth, half = came_ref.shape
    n = piv_ref.shape[1]
    nu_first, turn, part = (where_from_ref[i] for i in (1, 2, 3))
    low = lax.broadcasted_iota(jnp.int32, (n_rows, n), 0) * (mu * NBAS) + nu_first
    offset = jnp.broadcast_to(piv_ref[...], (n_rows, n)) - low
    count = jnp.zeros((n_rows, n), F32)
    for m in range(mu):
        inside = offset - m * NBAS
        count += jnp.where((inside >= 0) & (inside < nu), 1.0, 0.0)
    count = jnp.sum(count, axis=1, keepdims=True) - (turn * depth).astype(F32)
    count = jnp.clip(count, 0.0, depth)
    wide = (n_rows, n_rows * depth)
    slot = lax.broadcasted_iota(jnp.int32, wide, 1) - lax.broadcasted_iota(jnp.int32, wide, 0) * depth
    here = (slot >= 0) & (slot < depth)
    slot = slot.astype(F32)
    start = jnp.sum(jnp.where(slot >= depth, count, 0.0), axis=0, keepdims=True)
    used = jnp.sum(jnp.where(here & (slot < count), 1.0, 0.0), axis=0, keepdims=True)
    place = start + jnp.sum(jnp.where(here, slot, 0.0), axis=0, keepdims=True)
    place = place - (part * SLOTS).astype(F32)
    packed = lax.broadcasted_iota(jnp.int32, (SLOTS, wide[1]), 0).astype(F32)
    hot = jnp.where((packed == place) & (used > 0.0), 1.0, 0.0).astype(BF16)
    rows = came_ref[...].astype(F32).reshape(wide[1], half).astype(BF16)
    rows = jnp.dot(hot, rows, preferred_element_type=F32).astype(BF16)
    for g in range(out_ref.shape[0]):
        out_ref[g] = rows


def pack(where_from, pivots, came, n_grp, mu, nu):
    half = came.shape[2]
    n = pivots.shape[0]
    vmem = pl.BlockSpec(memory_space=pltpu.VMEM)
    return pl.pallas_call(
        functools.partial(pack_kernel, mu=mu, nu=nu),
        out_shape=jax.ShapeDtypeStruct((n_grp, SLOTS, half), BF16),
        in_specs=[pl.BlockSpec(memory_space=pltpu.SMEM), vmem, vmem],
        out_specs=vmem,
        compiler_params=pltpu.CompilerParams(vmem_limit_bytes=4 << 20),
        cost_estimate=pl.CostEstimate(
            flops=came.size, bytes_accessed=2 * n_grp * SLOTS * half, transcendentals=0
        ),
        name="pack",
    )(where_from, pivots.reshape(1, n), came)


def pieces(source, target, sems):
    count = sems.shape[0]
    rows = target.shape[0] // count
    return [
        pltpu.make_async_copy(
            source.at[pl.ds(i * rows, rows)], target.at[pl.ds(i * rows, rows)], sems.at[i]
        )
        for i in range(count)
    ]


def preload_kernel(prev_ref, after_ref, out_ref, sems):
    copies = pieces(prev_ref.at[0], out_ref, sems)
    for copy in copies:
        copy.start()
    for copy in copies:
        copy.wait()


def preload(previous, after):
    return pl.pallas_call(
        preload_kernel,
        out_shape=jax.ShapeDtypeStruct(previous.shape[1:], previous.dtype),
        in_specs=[pl.BlockSpec(memory_space=pltpu.HBM), pl.BlockSpec(memory_space=pl.ANY)],
        out_specs=pl.BlockSpec(memory_space=pltpu.VMEM),
        scratch_shapes=[pltpu.SemaphoreType.DMA((PIECES,))],
        compiler_params=pltpu.CompilerParams(vmem_limit_bytes=4 << 20),
        cost_estimate=pl.CostEstimate(
            flops=0, bytes_accessed=previous.size // 2, transcendentals=0
        ),
        name="preload",
    )(previous, after)


def vectors_kernel(
    core_ref, cols_ref, close_ref, prev_ref, mine_ref, other_ref, inv_ref, new_ref, turned_ref, came, made, load, store
):
    mu = cols_ref.shape[0]

    def start_load(m):
        for copy in pieces(prev_ref.at[m], came.at[m - 1], load.at[m - 1]):
            copy.start()

    def store_of(m):
        return pieces(made.at[m], new_ref.at[m], store.at[m])

    def step(m, prev):
        mine, other = mine_ref[...].astype(F32), other_ref[...].astype(F32)
        first = core_ref[0] == 0
        rows = jnp.concatenate(
            [jnp.where(first, mine, other), jnp.where(first, other, mine)], axis=1
        ).astype(BF16)
        contract = (((1,), (1,)), ((), ()))
        correction = lax.dot_general(prev, rows, contract, preferred_element_type=F32)
        residual = (cols_ref[m].astype(F32) - correction).astype(BF16)
        inv = inv_ref[...]
        row, column = (lax.broadcasted_iota(jnp.int32, inv.shape, d) for d in (0, 1))
        upper = jnp.where(row > column, 0.0, inv.astype(F32)).astype(BF16)
        new = jnp.dot(residual, upper, preferred_element_type=F32).astype(BF16)
        made[m] = new
        for copy in store_of(m):
            copy.start()
        turned_ref[m] = new.T

    start_load(1)
    step(0, close_ref[...])

    @pl.loop(1, mu)
    def _(m):
        for copy in pieces(prev_ref.at[m], came.at[m - 1], load.at[m - 1]):
            copy.wait()

        @pl.when(m + 1 < mu)
        def _():
            start_load(m + 1)

        step(m, came[m - 1])

    for m in range(mu):
        for copy in store_of(m):
            copy.wait()


def vectors(core, pivot_columns, close, previous, mine, other, pivot_inverse):
    mu, nu, k = previous.shape
    n = pivot_columns.shape[2]
    vmem = pl.BlockSpec(memory_space=pltpu.VMEM)
    hbm = pl.BlockSpec(memory_space=pltpu.HBM)
    return pl.pallas_call(
        vectors_kernel,
        out_shape=(
            jax.ShapeDtypeStruct((mu, nu, n), BF16),
            jax.ShapeDtypeStruct((mu, n, nu), BF16),
        ),
        in_specs=[pl.BlockSpec(memory_space=pltpu.SMEM), vmem, vmem, hbm, vmem, vmem, vmem],
        out_specs=(pl.BlockSpec(memory_space=pl.ANY), vmem),
        scratch_shapes=[
            pltpu.VMEM((mu - 1, nu, k), BF16),
            pltpu.VMEM((mu, nu, n), BF16),
            pltpu.SemaphoreType.DMA((mu - 1, PIECES)),
            pltpu.SemaphoreType.DMA((mu, PIECES)),
        ],
        compiler_params=pltpu.CompilerParams(vmem_limit_bytes=24 << 20),
        cost_estimate=pl.CostEstimate(
            flops=2 * mu * nu * n * (k + n),
            bytes_accessed=2 * mu * nu * (k + 3 * n),
            transcendentals=0,
        ),
        name="vectors",
    )(core, pivot_columns, close, previous, mine, other, pivot_inverse)


def parts_kernel(me_ref, turned_ref, orb_ref, *out_refs, ahead, owners):
    mu, n, nu = turned_ref.shape
    width = orb_ref.shape[1] // owners
    keep, last = out_refs[0].shape[-2:]
    columns = []
    for a in ahead:
        start = pl.multiple_of(lax.rem(me_ref[0] + a, owners) * width, width)
        columns.append(orb_ref[:, pl.ds(start, width)])
    columns = columns[0] if len(columns) == 1 else jnp.concatenate(columns, axis=1)
    for m in range(mu):
        part = jnp.dot(turned_ref[m], columns, preferred_element_type=F32)
        if len(out_refs) == 2:
            half = n // 2
            for h, out_ref in enumerate(out_refs):
                piece = part[h * half : (h + 1) * half].reshape(half // keep, keep, last)
                out_ref[:, m] = piece.astype(out_ref.dtype)
        else:
            for q in range(len(ahead)):
                piece = part[:, q * width : (q + 1) * width].reshape(n // keep, keep, width)
                out_refs[0][q, :, m] = piece


def parts(me, turned, orbitals, ahead, owners, dests, send=False):
    mu, n, nu = turned.shape
    width = orbitals.shape[1] // owners
    if send:
        shape = (dests // 2, mu, n // dests, width)
        out_shape = (jax.ShapeDtypeStruct(shape, BF16),) * 2
    else:
        shape = (len(ahead), dests, mu, n // dests, width)
        out_shape = jax.ShapeDtypeStruct(shape, F32)
    vmem = pl.BlockSpec(memory_space=pltpu.VMEM)
    return pl.pallas_call(
        functools.partial(parts_kernel, ahead=ahead, owners=owners),
        out_shape=out_shape,
        in_specs=[pl.BlockSpec(memory_space=pltpu.SMEM), vmem, vmem],
        out_specs=(vmem, vmem) if send else vmem,
        compiler_params=pltpu.CompilerParams(vmem_limit_bytes=20 << 20),
        cost_estimate=pl.CostEstimate(
            flops=2 * mu * n * nu * width * len(ahead),
            bytes_accessed=2 * mu * n * nu,
            transcendentals=0,
        ),
        name="parts",
    )(me, turned, orbitals)


def join_kernel(own_ref, came_ref, out_ref, *, second):
    half = came_ref.shape[0]
    mine, other = (slice(half, None), slice(0, half)) if second else (slice(0, half), slice(half, None))
    out_ref[mine] = (own_ref[0, mine] + came_ref[...].astype(F32)).astype(BF16)
    out_ref[other] = own_ref[0, other].astype(BF16)


def join(part, which, came, second):
    shape = part.shape[1:]
    return pl.pallas_call(
        functools.partial(join_kernel, second=second),
        grid=(1,),
        out_shape=jax.ShapeDtypeStruct(shape, BF16),
        in_specs=[
            pl.BlockSpec((1,) + shape, lambda i: (which, 0, 0, 0, 0)),
            pl.BlockSpec(came.shape, lambda i: (0, 0, 0, 0)),
        ],
        out_specs=pl.BlockSpec(shape, lambda i: (0, 0, 0, 0)),
        compiler_params=pltpu.CompilerParams(vmem_limit_bytes=6 << 20),
        cost_estimate=pl.CostEstimate(
            flops=came.size, bytes_accessed=12 * came.size, transcendentals=0
        ),
        name="join",
    )(part, came)


def reduce_to_owner(me, turned, orbitals, owners, dests):
    far = owners // 2

    def hop(x, way):
        return lax.ppermute(x, "grp", [(i, (i + way) % owners) for i in range(owners)])

    def own(ahead, **more):
        return parts(me, turned, orbitals, ahead, owners, dests, **more)

    right, left = own((far,), send=True)
    right, left = hop(right, 1), hop(left, -1)
    near = own((far - 1, far + 1))
    right, left = hop(join(near, 0, right, False), 1), hop(join(near, 1, left, True), -1)
    for ahead in range(far - 2, 0, -1):
        near = own((ahead, owners - ahead))
        right, left = (
            hop((near[q] + x.astype(F32)).astype(BF16), way)
            for q, (x, way) in enumerate(((right, 1), (left, -1)))
        )
    return own((0,))[0] + right.astype(F32) + left.astype(F32)


def final_kernel(half_ref, slab_ref, out_ref):
    rows, width = half_ref.shape
    mu = slab_ref.shape[0]
    keep = rows // mu
    slab_t = slab_ref[...].T
    slab_t = jnp.concatenate([slab_t, slab_t], axis=1)
    for p in range(0, keep, 2):
        pair = jnp.concatenate(
            [half_ref[pl.ds(q, mu, stride=keep), :] for q in (p, p + 1)], axis=1
        )
        high = pair.astype(BF16)
        low = (pair - high.astype(F32)).astype(BF16)
        both = jnp.dot(slab_t, jnp.concatenate([high, low], axis=0), preferred_element_type=F32)
        out_ref[p] = both[:, :width].astype(BF16)
        out_ref[p + 1] = both[:, width:].astype(BF16)


def final(half, slab):
    mu, occ = slab.shape
    rows, width = half.shape
    keep = rows // mu
    return pl.pallas_call(
        final_kernel,
        out_shape=jax.ShapeDtypeStruct((keep, occ, width), BF16),
        compiler_params=pltpu.CompilerParams(vmem_limit_bytes=16 << 20),
        cost_estimate=pl.CostEstimate(
            flops=4 * rows * width * occ,
            bytes_accessed=2 * keep * width * (2 * mu + occ),
            transcendentals=0,
        ),
        name="final",
    )(half, slab)


def exchange(x, axis):
    return lax.all_to_all(x, axis, split_axis=0, concat_axis=0, tiled=True)


def pivot_halves(n_rows, n_grp, pivots, previous):
    mu, nu, k = previous.shape
    n = pivots.shape[0]
    half = k // 2
    per_line = mu * NBAS
    nu_first = (lax.axis_index("grp") * nu).astype(jnp.int32)
    base = (lax.axis_index("rows") * per_line).astype(jnp.int32) + nu_first

    def one_round(index, so_far):
        index = jnp.asarray(index, jnp.int32)
        where_from = jnp.stack([base, nu_first, index // PARTS, index % PARTS])
        came = exchange(pick_rows(where_from, pivots, previous, n_rows), "rows")
        slots = exchange(pack(where_from, pivots, came, n_grp, mu, nu), "grp")
        slots = slots.reshape(n_grp * SLOTS, half)
        return select_rows(index.reshape(1), pivots, slots, so_far, per_line, nu, n_rows)

    mine, rounds = one_round(0, jnp.zeros((n, half), BF16))
    start, mine, rounds = lax.optimization_barrier((jnp.int32(1), mine, rounds))
    mine = lax.fori_loop(start, rounds[0], lambda i, rows: one_round(i, rows)[0], mine)
    other = lax.ppermute(mine, "rows", [(i, i ^ 1) for i in range(n_rows)])
    return mine, other


def per_device(n_rows, n_grp, pivot_columns, previous, pivots, pivot_inverse, orbitals, slab_orbitals):
    in_hbm = pltpu.with_memory_space_constraint(previous, pltpu.HBM)
    mine, other = pivot_halves(n_rows, n_grp, pivots, in_hbm)
    core = (lax.axis_index("rows") % 2).reshape(1).astype(jnp.int32)
    me = lax.axis_index("grp").reshape(1).astype(jnp.int32)
    close = preload(in_hbm, mine)
    new_vectors, turned = vectors(
        core, pivot_columns, close, in_hbm, mine, other, pivot_inverse
    )
    half = exchange(reduce_to_owner(me, turned, orbitals, n_grp, n_rows), "rows")
    return new_vectors, final(half.reshape(-1, half.shape[-1]), slab_orbitals)


def solution(mesh):
    in_specs = (P("rows", "grp", None), P("rows", "grp", None), P(), P(), P("grp", None), P())
    out_specs = (P("rows", "grp", None), P("rows", None, "grp"))
    body = functools.partial(per_device, mesh.shape["rows"], mesh.shape["grp"])
    return jax.shard_map(body, mesh=mesh, in_specs=in_specs, out_specs=out_specs, check_vma=False)
```

```python
import functools

import jax
import jax.numpy as jnp
from jax import lax
from jax.experimental import pallas as pl
from jax.experimental.pallas import tpu as pltpu
from jax.sharding import PartitionSpec as P

NBAS = 10240
F32 = jnp.float32
BF16 = jnp.bfloat16
DEPTH = 8
SLOTS = 24
PARTS = 3


def pick_kernel(where_from_ref, piv_ref, prev_ref, out_ref, acc_ref, held, sems, rows_ref):
    mu, nu, _ = prev_ref.shape
    depth, group, _ = held.shape
    base, turn = where_from_ref[1], where_from_ref[2]
    acc_ref[...] = jnp.zeros_like(acc_ref)
    pivots = piv_ref[...]
    order = lax.broadcasted_iota(jnp.int32, pivots.shape, 0) * pivots.shape[1]
    order += lax.broadcasted_iota(jnp.int32, pivots.shape, 1)
    many = 1 << (mu * nu - 1).bit_length()
    last = many * pivots.size
    keys = jnp.full_like(pivots, last)
    for m in range(mu):
        inside = pivots - base - m * NBAS
        keys = jnp.where((inside >= 0) & (inside < nu), order * many + inside + m * nu, keys)
    owned = jnp.sum((keys < last).astype(jnp.int32))
    skip = turn * depth
    total = jnp.clip(owned - skip, 0, depth)

    def fetch(row, i):
        m = jnp.int32(0)
        for step in range(1, mu):
            m += (row >= step * nu).astype(jnp.int32)
        start = pl.multiple_of((row - m * nu) // group * group, group)
        return pltpu.make_async_copy(prev_ref.at[m, pl.ds(start, group)], held.at[i], sems.at[i])

    def find(i, key):
        key = jnp.min(jnp.where(keys > key, keys, last))

        @pl.when(i >= skip)
        def _():
            row = key & (many - 1)
            rows_ref[i - skip] = row
            fetch(row, i - skip).start()

        return key

    lax.fori_loop(0, skip + total, find, jnp.int32(-1))

    def place(i, _):
        row = rows_ref[i]
        fetch(row, i).wait()
        rows = held[i].astype(F32)
        keep = lax.broadcasted_iota(jnp.int32, rows.shape, 0) == row % group
        acc_ref[pl.ds(i, 1), :] = jnp.sum(jnp.where(keep, rows, 0.0), axis=0, keepdims=True)
        return 0

    lax.fori_loop(0, total, place, 0)
    out_ref[...] = acc_ref[...].astype(BF16)


def pick_rows(where_from, pivots, previous):
    n = pivots.shape[0]
    k = previous.shape[2]
    lanes = 128
    return pl.pallas_call(
        pick_kernel,
        out_shape=jax.ShapeDtypeStruct((DEPTH, k), BF16),
        in_specs=[
            pl.BlockSpec(memory_space=pltpu.SMEM),
            pl.BlockSpec(memory_space=pltpu.VMEM),
            pl.BlockSpec(memory_space=pltpu.HBM),
        ],
        out_specs=pl.BlockSpec(memory_space=pltpu.VMEM),
        scratch_shapes=[
            pltpu.VMEM((DEPTH, k), F32),
            pltpu.VMEM((DEPTH, 16, k), BF16),
            pltpu.SemaphoreType.DMA((DEPTH,)),
            pltpu.SMEM((DEPTH,), jnp.int32),
        ],
        compiler_params=pltpu.CompilerParams(vmem_limit_bytes=4 << 20),
        cost_estimate=pl.CostEstimate(flops=n * k, bytes_accessed=2 * n * k, transcendentals=0),
        name="pick_rows",
    )(where_from, pivots.reshape(n // lanes, lanes), previous)


def whole_part(x, by):
    return jnp.floor((x + 0.5) * (1.0 / by))


def select_kernel(round_ref, piv_ref, slots_ref, so_far_ref, out_ref, rounds_ref, *, per_line, nu, owners):
    total, _ = slots_ref.shape
    n = piv_ref.shape[1]
    pivot = piv_ref[...].astype(F32)
    line = whole_part(pivot, per_line)
    inside = pivot - line * per_line
    inside = inside - whole_part(inside, NBAS) * NBAS
    device = jnp.broadcast_to(line * owners + whole_part(inside, nu), (n, n))
    mine = device.T
    before = lax.broadcasted_iota(jnp.int32, (n, n), 1) < lax.broadcasted_iota(jnp.int32, (n, n), 0)
    rank = jnp.sum(jnp.where((device == mine) & before, 1.0, 0.0), axis=1, keepdims=True)
    turn = whole_part(rank, DEPTH)
    turns = jnp.broadcast_to(turn, (n, n))
    my_line = whole_part(mine, owners)
    ahead = (device >= my_line * owners) & (device < mine) & (turns.T == turns)
    place = jnp.sum(jnp.where(ahead, 1.0, 0.0), axis=1, keepdims=True) + rank - turn * DEPTH
    part = whole_part(place, SLOTS)
    when = turn * PARTS + part
    rounds_ref[0] = jnp.max(when).astype(jnp.int32) + 1
    index = my_line[:, :1] * SLOTS + place - part * SLOTS
    index = jnp.where(when == round_ref[0].astype(F32), index, -1.0).astype(jnp.int32)
    hot = index == lax.broadcasted_iota(jnp.int32, (n, total), 1)
    hot = jnp.where(hot, 1.0, 0.0).astype(BF16)
    picked = jnp.dot(hot, slots_ref[...], preferred_element_type=F32)
    out_ref[...] = (picked + so_far_ref[...].astype(F32)).astype(BF16)


def select_rows(round_index, pivots, slots, so_far, per_line, nu, owners):
    total, width = slots.shape
    n = pivots.shape[0]
    vmem = pl.BlockSpec(memory_space=pltpu.VMEM)
    return pl.pallas_call(
        functools.partial(select_kernel, per_line=per_line, nu=nu, owners=owners),
        out_shape=(
            jax.ShapeDtypeStruct((n, width), BF16),
            jax.ShapeDtypeStruct((1,), jnp.int32),
        ),
        in_specs=[pl.BlockSpec(memory_space=pltpu.SMEM), vmem, vmem, vmem],
        out_specs=(vmem, pl.BlockSpec(memory_space=pltpu.SMEM)),
        compiler_params=pltpu.CompilerParams(vmem_limit_bytes=8 << 20),
        cost_estimate=pl.CostEstimate(
            flops=2 * n * total * width, bytes_accessed=2 * total * width, transcendentals=0
        ),
        name="select_rows",
    )(round_index, pivots.reshape(1, n), slots, so_far)


def spread_kernel(where_from_ref, piv_ref, came_ref, out_ref, *, mu, nu):
    owners, depth, k = came_ref.shape
    n = piv_ref.shape[1]
    line, turn, part = (where_from_ref[i] for i in (0, 2, 3))
    offset = jnp.broadcast_to(piv_ref[...] - line, (owners, n))
    low = lax.broadcasted_iota(jnp.int32, (owners, n), 0) * nu
    count = jnp.zeros((owners, n), F32)
    for m in range(mu):
        inside = offset - m * NBAS - low
        count += jnp.where((inside >= 0) & (inside < nu), 1.0, 0.0)
    count = jnp.sum(count, axis=1, keepdims=True) - (turn * depth).astype(F32)
    count = jnp.clip(count, 0.0, depth)
    wide = (owners, owners * depth)
    slot = lax.broadcasted_iota(jnp.int32, wide, 1) - lax.broadcasted_iota(jnp.int32, wide, 0) * depth
    here = (slot >= 0) & (slot < depth)
    start = jnp.sum(jnp.where(slot >= depth, count, 0.0), axis=0, keepdims=True)
    used = jnp.sum(jnp.where(here & (slot.astype(F32) < count), 1.0, 0.0), axis=0, keepdims=True)
    place = start + jnp.sum(jnp.where(here, slot.astype(F32), 0.0), axis=0, keepdims=True)
    place = place - (part * SLOTS).astype(F32)
    packed = lax.broadcasted_iota(jnp.int32, (SLOTS, wide[1]), 0).astype(F32)
    hot = jnp.where((packed == place) & (used > 0.0), 1.0, 0.0).astype(BF16)
    rows = came_ref[...].astype(F32).reshape(wide[1], k).astype(BF16)
    rows = jnp.dot(hot, rows, preferred_element_type=F32).astype(BF16)
    half = out_ref.shape[2]
    for c in range(2):
        piece = rows[:, c * half : (c + 1) * half]

        @pl.loop(0, out_ref.shape[0] // 2)
        def _(chip):
            out_ref[2 * chip + c] = piece


def spread(where_from, pivots, came, n_rows, mu, nu):
    k = came.shape[2]
    n = pivots.shape[0]
    vmem = pl.BlockSpec(memory_space=pltpu.VMEM)
    return pl.pallas_call(
        functools.partial(spread_kernel, mu=mu, nu=nu),
        out_shape=jax.ShapeDtypeStruct((n_rows, SLOTS, k // 2), BF16),
        in_specs=[pl.BlockSpec(memory_space=pltpu.SMEM), vmem, vmem],
        out_specs=vmem,
        compiler_params=pltpu.CompilerParams(vmem_limit_bytes=4 << 20),
        cost_estimate=pl.CostEstimate(
            flops=came.size, bytes_accessed=n_rows * SLOTS * k, transcendentals=0
        ),
        name="spread",
    )(where_from, pivots.reshape(1, n), came)


def vectors_kernel(
    core_ref, cols_ref, prev_ref, mine_ref, other_ref, inv_ref, new_ref, turned_ref, came, made, load, store
):
    mu = came.shape[0]

    def load_of(m):
        return pltpu.make_async_copy(prev_ref.at[m], came.at[m], load.at[m])

    def store_of(m):
        return pltpu.make_async_copy(made.at[m], new_ref.at[m], store.at[m])

    for m in range(mu):
        load_of(m).start()

    @pl.loop(0, mu)
    def _(m):
        load_of(m).wait()
        mine, other = mine_ref[...].astype(F32), other_ref[...].astype(F32)
        first = core_ref[0] == 0
        rows = jnp.concatenate(
            [jnp.where(first, mine, other), jnp.where(first, other, mine)], axis=1
        ).astype(BF16)
        contract = (((1,), (1,)), ((), ()))
        correction = lax.dot_general(came[m], rows, contract, preferred_element_type=F32)
        residual = (cols_ref[m].astype(F32) - correction).astype(BF16)
        inv = inv_ref[...]
        row, column = (lax.broadcasted_iota(jnp.int32, inv.shape, d) for d in (0, 1))
        upper = jnp.where(row > column, 0.0, inv.astype(F32)).astype(BF16)
        new = jnp.dot(residual, upper, preferred_element_type=F32).astype(BF16)
        made[m] = new
        store_of(m).start()
        turned_ref[m] = new.T

    for m in range(mu):
        store_of(m).wait()


def vectors(core, pivot_columns, previous, mine, other, pivot_inverse):
    mu, nu, k = previous.shape
    n = pivot_columns.shape[2]
    vmem = pl.BlockSpec(memory_space=pltpu.VMEM)
    return pl.pallas_call(
        vectors_kernel,
        out_shape=(
            jax.ShapeDtypeStruct((mu, nu, n), BF16),
            jax.ShapeDtypeStruct((mu, n, nu), BF16),
        ),
        in_specs=[
            pl.BlockSpec(memory_space=pltpu.SMEM),
            vmem,
            pl.BlockSpec(memory_space=pltpu.HBM),
            vmem,
            vmem,
            vmem,
        ],
        out_specs=(pl.BlockSpec(memory_space=pl.ANY), vmem),
        scratch_shapes=[
            pltpu.VMEM((mu, nu, k), BF16),
            pltpu.VMEM((mu, nu, n), BF16),
            pltpu.SemaphoreType.DMA((mu,)),
            pltpu.SemaphoreType.DMA((mu,)),
        ],
        compiler_params=pltpu.CompilerParams(vmem_limit_bytes=24 << 20),
        cost_estimate=pl.CostEstimate(
            flops=2 * mu * nu * n * (k + n),
            bytes_accessed=2 * mu * nu * (k + 3 * n),
            transcendentals=0,
        ),
        name="vectors",
    )(core, pivot_columns, previous, mine, other, pivot_inverse)


def parts_kernel(me_ref, turned_ref, orb_ref, *out_refs, ahead, owners):
    mu, n, nu = turned_ref.shape
    width = orb_ref.shape[1] // owners
    keep, last = out_refs[0].shape[-2:]
    columns = []
    for a in ahead:
        start = pl.multiple_of(lax.rem(me_ref[0] + a, owners) * width, width)
        columns.append(orb_ref[:, pl.ds(start, width)])
    columns = columns[0] if len(columns) == 1 else jnp.concatenate(columns, axis=1)
    for m in range(mu):
        part = jnp.dot(turned_ref[m], columns, preferred_element_type=F32)
        if len(out_refs) == 2:
            half = n // 2
            for h, out_ref in enumerate(out_refs):
                piece = part[h * half : (h + 1) * half].reshape(half // keep, keep, last)
                out_ref[:, m] = piece.astype(out_ref.dtype)
        else:
            for q in range(len(ahead)):
                piece = part[:, q * width : (q + 1) * width].reshape(n // keep, keep, width)
                out_refs[0][q, :, m] = piece


def parts(me, turned, orbitals, ahead, owners, dests, send=False):
    mu, n, nu = turned.shape
    width = orbitals.shape[1] // owners
    if send:
        shape = (dests // 2, mu, n // dests, width)
        out_shape = (jax.ShapeDtypeStruct(shape, BF16),) * 2
    else:
        shape = (len(ahead), dests, mu, n // dests, width)
        out_shape = jax.ShapeDtypeStruct(shape, F32)
    vmem = pl.BlockSpec(memory_space=pltpu.VMEM)
    return pl.pallas_call(
        functools.partial(parts_kernel, ahead=ahead, owners=owners),
        out_shape=out_shape,
        in_specs=[pl.BlockSpec(memory_space=pltpu.SMEM), vmem, vmem],
        out_specs=(vmem, vmem) if send else vmem,
        compiler_params=pltpu.CompilerParams(vmem_limit_bytes=20 << 20),
        cost_estimate=pl.CostEstimate(
            flops=2 * mu * n * nu * width * len(ahead),
            bytes_accessed=2 * mu * n * nu,
            transcendentals=0,
        ),
        name="parts",
    )(me, turned, orbitals)


def join_kernel(own_ref, came_ref, out_ref, *, second):
    half = came_ref.shape[0]
    mine, other = (slice(half, None), slice(0, half)) if second else (slice(0, half), slice(half, None))
    out_ref[mine] = (own_ref[0, mine] + came_ref[...].astype(F32)).astype(BF16)
    out_ref[other] = own_ref[0, other].astype(BF16)


def join(part, which, came, second):
    shape = part.shape[1:]
    return pl.pallas_call(
        functools.partial(join_kernel, second=second),
        grid=(1,),
        out_shape=jax.ShapeDtypeStruct(shape, BF16),
        in_specs=[
            pl.BlockSpec((1,) + shape, lambda i: (which, 0, 0, 0, 0)),
            pl.BlockSpec(came.shape, lambda i: (0, 0, 0, 0)),
        ],
        out_specs=pl.BlockSpec(shape, lambda i: (0, 0, 0, 0)),
        compiler_params=pltpu.CompilerParams(vmem_limit_bytes=6 << 20),
        cost_estimate=pl.CostEstimate(
            flops=came.size, bytes_accessed=12 * came.size, transcendentals=0
        ),
        name="join",
    )(part, came)


def add_kernel(own_ref, came_ref, out_ref):
    out_ref[...] = (own_ref[0] + came_ref[...].astype(F32)).astype(BF16)


def add(part, which, came):
    shape = came.shape
    zeros = lambda i: (0, 0, 0, 0)
    return pl.pallas_call(
        add_kernel,
        grid=(1,),
        out_shape=jax.ShapeDtypeStruct(shape, BF16),
        in_specs=[
            pl.BlockSpec((1,) + shape, lambda i: (which, 0, 0, 0, 0)),
            pl.BlockSpec(shape, zeros),
        ],
        out_specs=pl.BlockSpec(shape, zeros),
        compiler_params=pltpu.CompilerParams(vmem_limit_bytes=6 << 20),
        cost_estimate=pl.CostEstimate(
            flops=came.size, bytes_accessed=8 * came.size, transcendentals=0
        ),
        name="add",
    )(part, came)


def reduce_to_owner(me, turned, orbitals, owners, dests):
    far = owners // 2

    def hop(x, way):
        return lax.ppermute(x, "grp", [(i, (i + way) % owners) for i in range(owners)])

    def own(ahead, **more):
        return parts(me, turned, orbitals, ahead, owners, dests, **more)

    right, left = own((far,), send=True)
    right, left = hop(right, 1), hop(left, -1)
    near = own((far - 1, far + 1))
    right, left = hop(join(near, 0, right, False), 1), hop(join(near, 1, left, True), -1)
    for ahead in range(far - 2, 0, -1):
        near = own((ahead, owners - ahead))
        right, left = (
            hop(add(near, q, x), way)
            for q, (x, way) in enumerate(((right, 1), (left, -1)))
        )
    return own((0,))[0] + right.astype(F32) + left.astype(F32)


def final_kernel(half_ref, slab_ref, out_ref):
    rows, width = half_ref.shape
    mu = slab_ref.shape[0]
    keep = rows // mu
    slab_t = slab_ref[...].T
    slab_t = jnp.concatenate([slab_t, slab_t], axis=1)
    for p in range(0, keep, 2):
        pair = jnp.concatenate(
            [half_ref[pl.ds(q, mu, stride=keep), :] for q in (p, p + 1)], axis=1
        )
        high = pair.astype(BF16)
        low = (pair - high.astype(F32)).astype(BF16)
        both = jnp.dot(slab_t, jnp.concatenate([high, low], axis=0), preferred_element_type=F32)
        out_ref[p] = both[:, :width].astype(BF16)
        out_ref[p + 1] = both[:, width:].astype(BF16)


def final(half, slab):
    mu, occ = slab.shape
    rows, width = half.shape
    keep = rows // mu
    return pl.pallas_call(
        final_kernel,
        out_shape=jax.ShapeDtypeStruct((keep, occ, width), BF16),
        compiler_params=pltpu.CompilerParams(vmem_limit_bytes=16 << 20),
        cost_estimate=pl.CostEstimate(
            flops=4 * rows * width * occ,
            bytes_accessed=2 * keep * width * (2 * mu + occ),
            transcendentals=0,
        ),
        name="final",
    )(half, slab)


def exchange(x, axis):
    return lax.all_to_all(x, axis, split_axis=0, concat_axis=0, tiled=True)


def pivot_halves(n_rows, n_grp, pivots, previous):
    mu, nu, k = previous.shape
    n = pivots.shape[0]
    half = k // 2
    per_line = mu * NBAS
    line = lax.axis_index("rows") * per_line
    base = line + lax.axis_index("grp") * nu
    line, base = line.astype(jnp.int32), base.astype(jnp.int32)

    def one_round(index, so_far):
        index = jnp.asarray(index, jnp.int32)
        turn, part = index // PARTS, index % PARTS
        where_from = jnp.stack([line, base, turn, part])
        picked = pick_rows(where_from, pivots, previous)
        came = exchange(jnp.broadcast_to(picked, (n_grp,) + picked.shape), "grp")
        messages = spread(where_from, pivots, came, n_rows, mu, nu)
        slots = exchange(messages, "rows").reshape(n_rows * SLOTS, half)
        return select_rows(index.reshape(1), pivots, slots, so_far, per_line, nu, n_grp)

    mine, rounds = one_round(0, jnp.zeros((n, half), BF16))
    start, mine, rounds = lax.optimization_barrier((jnp.int32(1), mine, rounds))
    mine = lax.fori_loop(start, rounds[0], lambda i, rows: one_round(i, rows)[0], mine)
    other = lax.ppermute(mine, "rows", [(i, i ^ 1) for i in range(n_rows)])
    return mine, other


def per_device(n_rows, n_grp, pivot_columns, previous, pivots, pivot_inverse, orbitals, slab_orbitals):
    in_hbm = pltpu.with_memory_space_constraint(previous, pltpu.HBM)
    mine, other = pivot_halves(n_rows, n_grp, pivots, in_hbm)
    core = (lax.axis_index("rows") % 2).reshape(1).astype(jnp.int32)
    me = lax.axis_index("grp").reshape(1).astype(jnp.int32)
    new_vectors, turned = vectors(core, pivot_columns, in_hbm, mine, other, pivot_inverse)
    half = exchange(reduce_to_owner(me, turned, orbitals, n_grp, n_rows), "rows")
    return new_vectors, final(half.reshape(-1, half.shape[-1]), slab_orbitals)


def solution(mesh):
    in_specs = (P("rows", "grp", None), P("rows", "grp", None), P(), P(), P("grp", None), P())
    out_specs = (P("rows", "grp", None), P("rows", None, "grp"))
    body = functools.partial(per_device, mesh.shape["rows"], mesh.shape["grp"])
    return jax.shard_map(body, mesh=mesh, in_specs=in_specs, out_specs=out_specs, check_vma=False)
```

```python
import functools

import jax
import jax.numpy as jnp
from jax import lax
from jax.experimental import pallas as pl
from jax.experimental.pallas import tpu as pltpu
from jax.sharding import PartitionSpec as P

NBAS = 10240
F32 = jnp.float32
BF16 = jnp.bfloat16
DEPTH = 8
SLOTS = 24
PARTS = 3


def pick_kernel(where_from_ref, piv_ref, prev_ref, *refs, bring):
    if bring:
        cols_ref, out_ref, close_ref, acc_ref, held, sems, rows_ref, close_sems = refs
        copies = [
            pltpu.make_async_copy(cols_ref.at[m], close_ref.at[m], close_sems.at[m])
            for m in range(cols_ref.shape[0])
        ]
    else:
        out_ref, acc_ref, held, sems, rows_ref = refs
        copies = []
    for copy in copies:
        copy.start()
    mu, nu, _ = prev_ref.shape
    depth, group, _ = held.shape
    base, turn = where_from_ref[1], where_from_ref[2]
    acc_ref[...] = jnp.zeros_like(acc_ref)
    pivots = piv_ref[...]
    order = lax.broadcasted_iota(jnp.int32, pivots.shape, 0) * pivots.shape[1]
    order += lax.broadcasted_iota(jnp.int32, pivots.shape, 1)
    many = 1 << (mu * nu - 1).bit_length()
    last = many * pivots.size
    keys = jnp.full_like(pivots, last)
    for m in range(mu):
        inside = pivots - base - m * NBAS
        keys = jnp.where((inside >= 0) & (inside < nu), order * many + inside + m * nu, keys)
    owned = jnp.sum((keys < last).astype(jnp.int32))
    skip = turn * depth
    total = jnp.clip(owned - skip, 0, depth)

    def fetch(row, i):
        m = jnp.int32(0)
        for step in range(1, mu):
            m += (row >= step * nu).astype(jnp.int32)
        start = pl.multiple_of((row - m * nu) // group * group, group)
        return pltpu.make_async_copy(prev_ref.at[m, pl.ds(start, group)], held.at[i], sems.at[i])

    def find(i, key):
        key = jnp.min(jnp.where(keys > key, keys, last))

        @pl.when(i >= skip)
        def _():
            row = key & (many - 1)
            rows_ref[i - skip] = row
            fetch(row, i - skip).start()

        return key

    lax.fori_loop(0, skip + total, find, jnp.int32(-1))

    def place(i, _):
        row = rows_ref[i]
        fetch(row, i).wait()
        rows = held[i].astype(F32)
        keep = lax.broadcasted_iota(jnp.int32, rows.shape, 0) == row % group
        acc_ref[pl.ds(i, 1), :] = jnp.sum(jnp.where(keep, rows, 0.0), axis=0, keepdims=True)
        return 0

    lax.fori_loop(0, total, place, 0)
    out_ref[...] = acc_ref[...].astype(BF16)
    for copy in copies:
        copy.wait()


def pick_rows(where_from, pivots, previous, columns=None):
    n = pivots.shape[0]
    k = previous.shape[2]
    lanes = 128
    vmem = pl.BlockSpec(memory_space=pltpu.VMEM)
    hbm = pl.BlockSpec(memory_space=pltpu.HBM)
    args = [where_from, pivots.reshape(n // lanes, lanes), previous]
    out_shape = [jax.ShapeDtypeStruct((DEPTH, k), BF16)]
    scratch = [
        pltpu.VMEM((DEPTH, k), F32),
        pltpu.VMEM((DEPTH, 16, k), BF16),
        pltpu.SemaphoreType.DMA((DEPTH,)),
        pltpu.SMEM((DEPTH,), jnp.int32),
    ]
    bring = columns is not None
    if bring:
        args.append(columns)
        out_shape.append(jax.ShapeDtypeStruct(columns.shape, columns.dtype))
        scratch.append(pltpu.SemaphoreType.DMA((columns.shape[0],)))
    return pl.pallas_call(
        functools.partial(pick_kernel, bring=bring),
        out_shape=out_shape,
        in_specs=[pl.BlockSpec(memory_space=pltpu.SMEM), vmem, hbm] + [hbm] * bring,
        out_specs=[vmem] * len(out_shape),
        scratch_shapes=scratch,
        compiler_params=pltpu.CompilerParams(vmem_limit_bytes=4 << 20),
        cost_estimate=pl.CostEstimate(flops=n * k, bytes_accessed=2 * n * k, transcendentals=0),
        name="pick_rows",
    )(*args)


def whole_part(x, by):
    return jnp.floor((x + 0.5) * (1.0 / by))


def select_kernel(round_ref, piv_ref, slots_ref, so_far_ref, out_ref, rounds_ref, *, per_line, nu, owners):
    total, _ = slots_ref.shape
    n = piv_ref.shape[1]
    pivot = piv_ref[...].astype(F32)
    line = whole_part(pivot, per_line)
    inside = pivot - line * per_line
    inside = inside - whole_part(inside, NBAS) * NBAS
    device = jnp.broadcast_to(line * owners + whole_part(inside, nu), (n, n))
    mine = device.T
    before = lax.broadcasted_iota(jnp.int32, (n, n), 1) < lax.broadcasted_iota(jnp.int32, (n, n), 0)
    rank = jnp.sum(jnp.where((device == mine) & before, 1.0, 0.0), axis=1, keepdims=True)
    turn = whole_part(rank, DEPTH)
    turns = jnp.broadcast_to(turn, (n, n))
    my_line = whole_part(mine, owners)
    ahead = (device >= my_line * owners) & (device < mine) & (turns.T == turns)
    place = jnp.sum(jnp.where(ahead, 1.0, 0.0), axis=1, keepdims=True) + rank - turn * DEPTH
    part = whole_part(place, SLOTS)
    when = turn * PARTS + part
    rounds_ref[0] = jnp.max(when).astype(jnp.int32) + 1
    index = my_line[:, :1] * SLOTS + place - part * SLOTS
    index = jnp.where(when == round_ref[0].astype(F32), index, -1.0).astype(jnp.int32)
    hot = index == lax.broadcasted_iota(jnp.int32, (n, total), 1)
    hot = jnp.where(hot, 1.0, 0.0).astype(BF16)
    picked = jnp.dot(hot, slots_ref[...], preferred_element_type=F32)
    out_ref[...] = (picked + so_far_ref[...].astype(F32)).astype(BF16)


def select_rows(round_index, pivots, slots, so_far, per_line, nu, owners):
    total, width = slots.shape
    n = pivots.shape[0]
    vmem = pl.BlockSpec(memory_space=pltpu.VMEM)
    return pl.pallas_call(
        functools.partial(select_kernel, per_line=per_line, nu=nu, owners=owners),
        out_shape=(
            jax.ShapeDtypeStruct((n, width), BF16),
            jax.ShapeDtypeStruct((1,), jnp.int32),
        ),
        in_specs=[pl.BlockSpec(memory_space=pltpu.SMEM), vmem, vmem, vmem],
        out_specs=(vmem, pl.BlockSpec(memory_space=pltpu.SMEM)),
        compiler_params=pltpu.CompilerParams(vmem_limit_bytes=8 << 20),
        cost_estimate=pl.CostEstimate(
            flops=2 * n * total * width, bytes_accessed=2 * total * width, transcendentals=0
        ),
        name="select_rows",
    )(round_index, pivots.reshape(1, n), slots, so_far)


def spread_kernel(where_from_ref, piv_ref, came_ref, out_ref, *, mu, nu):
    owners, depth, k = came_ref.shape
    n = piv_ref.shape[1]
    line, turn, part = (where_from_ref[i] for i in (0, 2, 3))
    offset = jnp.broadcast_to(piv_ref[...] - line, (owners, n))
    low = lax.broadcasted_iota(jnp.int32, (owners, n), 0) * nu
    count = jnp.zeros((owners, n), F32)
    for m in range(mu):
        inside = offset - m * NBAS - low
        count += jnp.where((inside >= 0) & (inside < nu), 1.0, 0.0)
    count = jnp.sum(count, axis=1, keepdims=True) - (turn * depth).astype(F32)
    count = jnp.clip(count, 0.0, depth)
    wide = (owners, owners * depth)
    slot = lax.broadcasted_iota(jnp.int32, wide, 1) - lax.broadcasted_iota(jnp.int32, wide, 0) * depth
    here = (slot >= 0) & (slot < depth)
    start = jnp.sum(jnp.where(slot >= depth, count, 0.0), axis=0, keepdims=True)
    used = jnp.sum(jnp.where(here & (slot.astype(F32) < count), 1.0, 0.0), axis=0, keepdims=True)
    place = start + jnp.sum(jnp.where(here, slot.astype(F32), 0.0), axis=0, keepdims=True)
    place = place - (part * SLOTS).astype(F32)
    packed = lax.broadcasted_iota(jnp.int32, (SLOTS, wide[1]), 0).astype(F32)
    hot = jnp.where((packed == place) & (used > 0.0), 1.0, 0.0).astype(BF16)
    rows = came_ref[...].astype(F32).reshape(wide[1], k).astype(BF16)
    rows = jnp.dot(hot, rows, preferred_element_type=F32).astype(BF16)
    half = out_ref.shape[2]
    for c in range(2):
        piece = rows[:, c * half : (c + 1) * half]

        @pl.loop(0, out_ref.shape[0] // 2)
        def _(chip):
            out_ref[2 * chip + c] = piece


def spread(where_from, pivots, came, n_rows, mu, nu):
    k = came.shape[2]
    n = pivots.shape[0]
    vmem = pl.BlockSpec(memory_space=pltpu.VMEM)
    return pl.pallas_call(
        functools.partial(spread_kernel, mu=mu, nu=nu),
        out_shape=jax.ShapeDtypeStruct((n_rows, SLOTS, k // 2), BF16),
        in_specs=[pl.BlockSpec(memory_space=pltpu.SMEM), vmem, vmem],
        out_specs=vmem,
        compiler_params=pltpu.CompilerParams(vmem_limit_bytes=4 << 20),
        cost_estimate=pl.CostEstimate(
            flops=came.size, bytes_accessed=n_rows * SLOTS * k, transcendentals=0
        ),
        name="spread",
    )(where_from, pivots.reshape(1, n), came)


def vectors_kernel(
    core_ref, me_ref, cols_ref, prev_ref, mine_ref, other_ref, inv_ref, orb_ref,
    new_ref, turned_ref, far_ref, came, made, load, store, far_sem, *, owners
):
    mu = came.shape[0]
    width = far_ref.shape[1]
    column = pl.multiple_of(lax.rem(me_ref[0] + owners // 2, owners) * width, width)
    far = pltpu.make_async_copy(orb_ref.at[:, pl.ds(column, width)], far_ref, far_sem)

    def load_of(m):
        return pltpu.make_async_copy(prev_ref.at[m], came.at[m], load.at[m])

    def store_of(m):
        return pltpu.make_async_copy(made.at[m], new_ref.at[m], store.at[m])

    for m in range(mu):
        load_of(m).start()
    far.start()

    @pl.loop(0, mu)
    def _(m):
        load_of(m).wait()
        mine, other = mine_ref[...].astype(F32), other_ref[...].astype(F32)
        first = core_ref[0] == 0
        rows = jnp.concatenate(
            [jnp.where(first, mine, other), jnp.where(first, other, mine)], axis=1
        ).astype(BF16)
        contract = (((1,), (1,)), ((), ()))
        correction = lax.dot_general(came[m], rows, contract, preferred_element_type=F32)
        residual = (cols_ref[m].astype(F32) - correction).astype(BF16)
        inv = inv_ref[...]
        row, column = (lax.broadcasted_iota(jnp.int32, inv.shape, d) for d in (0, 1))
        upper = jnp.where(row > column, 0.0, inv.astype(F32)).astype(BF16)
        new = jnp.dot(residual, upper, preferred_element_type=F32).astype(BF16)
        made[m] = new
        store_of(m).start()
        turned_ref[m] = new.T

    far.wait()
    for m in range(mu):
        store_of(m).wait()


def vectors(core, me, pivot_columns, previous, mine, other, pivot_inverse, orbitals, owners):
    mu, nu, k = previous.shape
    n = pivot_columns.shape[2]
    width = orbitals.shape[1] // owners
    smem = pl.BlockSpec(memory_space=pltpu.SMEM)
    vmem = pl.BlockSpec(memory_space=pltpu.VMEM)
    hbm = pl.BlockSpec(memory_space=pltpu.HBM)
    return pl.pallas_call(
        functools.partial(vectors_kernel, owners=owners),
        out_shape=(
            jax.ShapeDtypeStruct((mu, nu, n), BF16),
            jax.ShapeDtypeStruct((mu, n, nu), BF16),
            jax.ShapeDtypeStruct((nu, width), BF16),
        ),
        in_specs=[smem, smem, vmem, hbm, vmem, vmem, vmem, hbm],
        out_specs=(pl.BlockSpec(memory_space=pl.ANY), vmem, vmem),
        scratch_shapes=[
            pltpu.VMEM((mu, nu, k), BF16),
            pltpu.VMEM((mu, nu, n), BF16),
            pltpu.SemaphoreType.DMA((mu,)),
            pltpu.SemaphoreType.DMA((mu,)),
            pltpu.SemaphoreType.DMA,
        ],
        compiler_params=pltpu.CompilerParams(vmem_limit_bytes=24 << 20),
        cost_estimate=pl.CostEstimate(
            flops=2 * mu * nu * n * (k + n),
            bytes_accessed=2 * mu * nu * (k + 3 * n),
            transcendentals=0,
        ),
        name="vectors",
    )(core, me, pivot_columns, previous, mine, other, pivot_inverse, orbitals)


def bring_kernel(orb_ref, after_ref, out_ref, sems):
    count = sems.shape[0]
    rows = out_ref.shape[0] // count
    copies = [
        pltpu.make_async_copy(
            orb_ref.at[pl.ds(i * rows, rows)], out_ref.at[pl.ds(i * rows, rows)], sems.at[i]
        )
        for i in range(count)
    ]
    for copy in copies:
        copy.start()
    for copy in copies:
        copy.wait()


def bring(orbitals, after):
    return pl.pallas_call(
        bring_kernel,
        out_shape=jax.ShapeDtypeStruct(orbitals.shape, orbitals.dtype),
        in_specs=[pl.BlockSpec(memory_space=pltpu.HBM), pl.BlockSpec(memory_space=pl.ANY)],
        out_specs=pl.BlockSpec(memory_space=pltpu.VMEM),
        scratch_shapes=[pltpu.SemaphoreType.DMA((4,))],
        compiler_params=pltpu.CompilerParams(vmem_limit_bytes=4 << 20),
        cost_estimate=pl.CostEstimate(
            flops=0, bytes_accessed=2 * orbitals.size, transcendentals=0
        ),
        name="bring",
    )(orbitals, after)


def parts_kernel(me_ref, turned_ref, orb_ref, *out_refs, ahead, owners):
    mu, n, nu = turned_ref.shape
    keep, width = out_refs[0].shape[-2:]
    columns = [orb_ref[...]] if len(out_refs) == 2 else []
    for a in ahead[: 0 if columns else None]:
        start = pl.multiple_of(lax.rem(me_ref[0] + a, owners) * width, width)
        columns.append(orb_ref[:, pl.ds(start, width)])
    columns = columns[0] if len(columns) == 1 else jnp.concatenate(columns, axis=1)
    for m in range(mu):
        part = jnp.dot(turned_ref[m], columns, preferred_element_type=F32)
        if len(out_refs) == 2:
            half = n // 2
            for h, out_ref in enumerate(out_refs):
                piece = part[h * half : (h + 1) * half].reshape(half // keep, keep, width)
                out_ref[:, m] = piece.astype(out_ref.dtype)
        else:
            for q in range(len(ahead)):
                piece = part[:, q * width : (q + 1) * width].reshape(n // keep, keep, width)
                out_refs[0][q, :, m] = piece


def parts(me, turned, orbitals, ahead, owners, dests, send=False):
    mu, n, nu = turned.shape
    width = orbitals.shape[1] // (1 if send else owners)
    if send:
        shape = (dests // 2, mu, n // dests, width)
        out_shape = (jax.ShapeDtypeStruct(shape, BF16),) * 2
    else:
        shape = (len(ahead), dests, mu, n // dests, width)
        out_shape = jax.ShapeDtypeStruct(shape, F32)
    vmem = pl.BlockSpec(memory_space=pltpu.VMEM)
    return pl.pallas_call(
        functools.partial(parts_kernel, ahead=ahead, owners=owners),
        out_shape=out_shape,
        in_specs=[pl.BlockSpec(memory_space=pltpu.SMEM), vmem, vmem],
        out_specs=(vmem, vmem) if send else vmem,
        compiler_params=pltpu.CompilerParams(vmem_limit_bytes=20 << 20),
        cost_estimate=pl.CostEstimate(
            flops=2 * mu * n * nu * width * len(ahead),
            bytes_accessed=2 * mu * n * nu,
            transcendentals=0,
        ),
        name="parts",
    )(me, turned, orbitals)


def join_kernel(own_ref, came_ref, out_ref, *, second):
    half = came_ref.shape[0]
    mine, other = (slice(half, None), slice(0, half)) if second else (slice(0, half), slice(half, None))
    out_ref[mine] = (own_ref[0, mine] + came_ref[...].astype(F32)).astype(BF16)
    out_ref[other] = own_ref[0, other].astype(BF16)


def join(part, which, came, second):
    shape = part.shape[1:]
    return pl.pallas_call(
        functools.partial(join_kernel, second=second),
        grid=(1,),
        out_shape=jax.ShapeDtypeStruct(shape, BF16),
        in_specs=[
            pl.BlockSpec((1,) + shape, lambda i: (which, 0, 0, 0, 0)),
            pl.BlockSpec(came.shape, lambda i: (0, 0, 0, 0)),
        ],
        out_specs=pl.BlockSpec(shape, lambda i: (0, 0, 0, 0)),
        compiler_params=pltpu.CompilerParams(vmem_limit_bytes=6 << 20),
        cost_estimate=pl.CostEstimate(
            flops=came.size, bytes_accessed=12 * came.size, transcendentals=0
        ),
        name="join",
    )(part, came)


def add_kernel(own_ref, came_ref, out_ref):
    out_ref[...] = (own_ref[0] + came_ref[...].astype(F32)).astype(BF16)


def add(part, which, came):
    shape = came.shape
    zeros = lambda i: (0, 0, 0, 0)
    return pl.pallas_call(
        add_kernel,
        grid=(1,),
        out_shape=jax.ShapeDtypeStruct(shape, BF16),
        in_specs=[
            pl.BlockSpec((1,) + shape, lambda i: (which, 0, 0, 0, 0)),
            pl.BlockSpec(shape, zeros),
        ],
        out_specs=pl.BlockSpec(shape, zeros),
        compiler_params=pltpu.CompilerParams(vmem_limit_bytes=6 << 20),
        cost_estimate=pl.CostEstimate(
            flops=came.size, bytes_accessed=8 * came.size, transcendentals=0
        ),
        name="add",
    )(part, came)


def reduce_to_owner(me, turned, columns, orbitals, owners, dests):
    far = owners // 2

    def hop(x, way):
        return lax.ppermute(x, "grp", [(i, (i + way) % owners) for i in range(owners)])

    right, left = parts(me, turned, columns, (far,), owners, dests, send=True)
    orbitals = bring(orbitals, right)
    right, left = hop(right, 1), hop(left, -1)

    def own(ahead):
        return parts(me, turned, orbitals, ahead, owners, dests)

    near = own((far - 1, far + 1))
    right, left = hop(join(near, 0, right, False), 1), hop(join(near, 1, left, True), -1)
    for ahead in range(far - 2, 0, -1):
        near = own((ahead, owners - ahead))
        right, left = (
            hop(add(near, q, x), way)
            for q, (x, way) in enumerate(((right, 1), (left, -1)))
        )
    return own((0,))[0] + right.astype(F32) + left.astype(F32)


def final_kernel(half_ref, slab_ref, out_ref):
    rows, width = half_ref.shape
    mu = slab_ref.shape[0]
    keep = rows // mu
    slab_t = slab_ref[...].T
    slab_t = jnp.concatenate([slab_t, slab_t], axis=1)
    for p in range(0, keep, 2):
        pair = jnp.concatenate(
            [half_ref[pl.ds(q, mu, stride=keep), :] for q in (p, p + 1)], axis=1
        )
        high = pair.astype(BF16)
        low = (pair - high.astype(F32)).astype(BF16)
        both = jnp.dot(slab_t, jnp.concatenate([high, low], axis=0), preferred_element_type=F32)
        out_ref[p] = both[:, :width].astype(BF16)
        out_ref[p + 1] = both[:, width:].astype(BF16)


def final(half, slab):
    mu, occ = slab.shape
    rows, width = half.shape
    keep = rows // mu
    return pl.pallas_call(
        final_kernel,
        out_shape=jax.ShapeDtypeStruct((keep, occ, width), BF16),
        compiler_params=pltpu.CompilerParams(vmem_limit_bytes=16 << 20),
        cost_estimate=pl.CostEstimate(
            flops=4 * rows * width * occ,
            bytes_accessed=2 * keep * width * (2 * mu + occ),
            transcendentals=0,
        ),
        name="final",
    )(half, slab)


def exchange(x, axis):
    return lax.all_to_all(x, axis, split_axis=0, concat_axis=0, tiled=True)


def pivot_halves(n_rows, n_grp, pivots, previous, columns):
    mu, nu, k = previous.shape
    n = pivots.shape[0]
    half = k // 2
    per_line = mu * NBAS
    line = lax.axis_index("rows") * per_line
    base = line + lax.axis_index("grp") * nu
    line, base = line.astype(jnp.int32), base.astype(jnp.int32)

    def one_round(index, so_far, columns=None):
        index = jnp.asarray(index, jnp.int32)
        turn, part = index // PARTS, index % PARTS
        where_from = jnp.stack([line, base, turn, part])
        picked, *close = pick_rows(where_from, pivots, previous, columns)
        came = exchange(jnp.broadcast_to(picked, (n_grp,) + picked.shape), "grp")
        messages = spread(where_from, pivots, came, n_rows, mu, nu)
        slots = exchange(messages, "rows").reshape(n_rows * SLOTS, half)
        rows, rounds = select_rows(index.reshape(1), pivots, slots, so_far, per_line, nu, n_grp)
        return rows, rounds, *close

    mine, rounds, close = one_round(0, jnp.zeros((n, half), BF16), columns)
    start, mine, rounds = lax.optimization_barrier((jnp.int32(1), mine, rounds))
    mine = lax.fori_loop(start, rounds[0], lambda i, rows: one_round(i, rows)[0], mine)
    other = lax.ppermute(mine, "rows", [(i, i ^ 1) for i in range(n_rows)])
    return mine, other, close


def per_device(n_rows, n_grp, pivot_columns, previous, pivots, pivot_inverse, orbitals, slab_orbitals):
    previous, pivot_columns, orbitals = (
        pltpu.with_memory_space_constraint(x, pltpu.HBM) for x in (previous, pivot_columns, orbitals)
    )
    mine, other, close = pivot_halves(n_rows, n_grp, pivots, previous, pivot_columns)
    core = (lax.axis_index("rows") % 2).reshape(1).astype(jnp.int32)
    me = lax.axis_index("grp").reshape(1).astype(jnp.int32)
    new_vectors, turned, far = vectors(
        core, me, close, previous, mine, other, pivot_inverse, orbitals, n_grp
    )
    half = exchange(reduce_to_owner(me, turned, far, orbitals, n_grp, n_rows), "rows")
    return new_vectors, final(half.reshape(-1, half.shape[-1]), slab_orbitals)


def solution(mesh):
    in_specs = (P("rows", "grp", None), P("rows", "grp", None), P(), P(), P("grp", None), P())
    out_specs = (P("rows", "grp", None), P("rows", None, "grp"))
    body = functools.partial(per_device, mesh.shape["rows"], mesh.shape["grp"])
    return jax.shard_map(body, mesh=mesh, in_specs=in_specs, out_specs=out_specs, check_vma=False)
```

```python
import functools

import jax
import jax.numpy as jnp
from jax import lax
from jax.experimental import pallas as pl
from jax.experimental.pallas import tpu as pltpu
from jax.sharding import PartitionSpec as P

NBAS = 10240
F32 = jnp.float32
BF16 = jnp.bfloat16
DEPTH = 8
SLOTS = 24
PARTS = 3


def pick_kernel(where_from_ref, piv_ref, prev_ref, *refs, bring):
    if bring:
        cols_ref, out_ref, close_ref, acc_ref, held, sems, rows_ref, close_sems = refs
        copies = [
            pltpu.make_async_copy(cols_ref.at[m], close_ref.at[m], close_sems.at[m])
            for m in range(cols_ref.shape[0])
        ]
    else:
        out_ref, acc_ref, held, sems, rows_ref = refs
        copies = []
    for copy in copies:
        copy.start()
    mu, nu, _ = prev_ref.shape
    depth, group, _ = held.shape
    base, turn = where_from_ref[1], where_from_ref[2]
    acc_ref[...] = jnp.zeros_like(acc_ref)
    pivots = piv_ref[...]
    order = lax.broadcasted_iota(jnp.int32, pivots.shape, 0) * pivots.shape[1]
    order += lax.broadcasted_iota(jnp.int32, pivots.shape, 1)
    many = 1 << (mu * nu - 1).bit_length()
    last = many * pivots.size
    keys = jnp.full_like(pivots, last)
    for m in range(mu):
        inside = pivots - base - m * NBAS
        keys = jnp.where((inside >= 0) & (inside < nu), order * many + inside + m * nu, keys)
    owned = jnp.sum((keys < last).astype(jnp.int32))
    skip = turn * depth
    total = jnp.clip(owned - skip, 0, depth)

    def fetch(row, i):
        m = jnp.int32(0)
        for step in range(1, mu):
            m += (row >= step * nu).astype(jnp.int32)
        start = pl.multiple_of((row - m * nu) // group * group, group)
        return pltpu.make_async_copy(prev_ref.at[m, pl.ds(start, group)], held.at[i], sems.at[i])

    def find(i, key):
        key = jnp.min(jnp.where(keys > key, keys, last))

        @pl.when(i >= skip)
        def _():
            row = key & (many - 1)
            rows_ref[i - skip] = row
            fetch(row, i - skip).start()

        return key

    lax.fori_loop(0, skip + total, find, jnp.int32(-1))

    def place(i, _):
        row = rows_ref[i]
        fetch(row, i).wait()
        rows = held[i].astype(F32)
        keep = lax.broadcasted_iota(jnp.int32, rows.shape, 0) == row % group
        acc_ref[pl.ds(i, 1), :] = jnp.sum(jnp.where(keep, rows, 0.0), axis=0, keepdims=True)
        return 0

    lax.fori_loop(0, total, place, 0)
    out_ref[...] = acc_ref[...].astype(BF16)
    for copy in copies:
        copy.wait()


def pick_rows(where_from, pivots, previous, columns=None):
    n = pivots.shape[0]
    k = previous.shape[2]
    lanes = 128
    vmem = pl.BlockSpec(memory_space=pltpu.VMEM)
    hbm = pl.BlockSpec(memory_space=pltpu.HBM)
    args = [where_from, pivots.reshape(n // lanes, lanes), previous]
    out_shape = [jax.ShapeDtypeStruct((DEPTH, k), BF16)]
    scratch = [
        pltpu.VMEM((DEPTH, k), F32),
        pltpu.VMEM((DEPTH, 16, k), BF16),
        pltpu.SemaphoreType.DMA((DEPTH,)),
        pltpu.SMEM((DEPTH,), jnp.int32),
    ]
    bring = columns is not None
    if bring:
        args.append(columns)
        out_shape.append(jax.ShapeDtypeStruct(columns.shape, columns.dtype))
        scratch.append(pltpu.SemaphoreType.DMA((columns.shape[0],)))
    return pl.pallas_call(
        functools.partial(pick_kernel, bring=bring),
        out_shape=out_shape,
        in_specs=[pl.BlockSpec(memory_space=pltpu.SMEM), vmem, hbm] + [hbm] * bring,
        out_specs=[vmem] * len(out_shape),
        scratch_shapes=scratch,
        compiler_params=pltpu.CompilerParams(vmem_limit_bytes=4 << 20),
        cost_estimate=pl.CostEstimate(flops=n * k, bytes_accessed=2 * n * k, transcendentals=0),
        name="pick_rows",
    )(*args)


def whole_part(x, by):
    return jnp.floor((x + 0.5) * (1.0 / by))


def select_kernel(round_ref, piv_ref, slots_ref, so_far_ref, out_ref, rounds_ref, *, per_line, nu, owners):
    total, _ = slots_ref.shape
    n = piv_ref.shape[1]
    pivot = piv_ref[...].astype(F32)
    line = whole_part(pivot, per_line)
    inside = pivot - line * per_line
    inside = inside - whole_part(inside, NBAS) * NBAS
    device = jnp.broadcast_to(line * owners + whole_part(inside, nu), (n, n))
    mine = device.T
    before = lax.broadcasted_iota(jnp.int32, (n, n), 1) < lax.broadcasted_iota(jnp.int32, (n, n), 0)
    rank = jnp.sum(jnp.where((device == mine) & before, 1.0, 0.0), axis=1, keepdims=True)
    turn = whole_part(rank, DEPTH)
    turns = jnp.broadcast_to(turn, (n, n))
    my_line = whole_part(mine, owners)
    ahead = (device >= my_line * owners) & (device < mine) & (turns.T == turns)
    place = jnp.sum(jnp.where(ahead, 1.0, 0.0), axis=1, keepdims=True) + rank - turn * DEPTH
    part = whole_part(place, SLOTS)
    when = turn * PARTS + part
    rounds_ref[0] = jnp.max(when).astype(jnp.int32) + 1
    index = my_line[:, :1] * SLOTS + place - part * SLOTS
    index = jnp.where(when == round_ref[0].astype(F32), index, -1.0).astype(jnp.int32)
    hot = index == lax.broadcasted_iota(jnp.int32, (n, total), 1)
    hot = jnp.where(hot, 1.0, 0.0).astype(BF16)
    picked = jnp.dot(hot, slots_ref[...], preferred_element_type=F32)
    out_ref[...] = (picked + so_far_ref[...].astype(F32)).astype(BF16)


def select_rows(round_index, pivots, slots, so_far, per_line, nu, owners):
    total, width = slots.shape
    n = pivots.shape[0]
    vmem = pl.BlockSpec(memory_space=pltpu.VMEM)
    return pl.pallas_call(
        functools.partial(select_kernel, per_line=per_line, nu=nu, owners=owners),
        out_shape=(
            jax.ShapeDtypeStruct((n, width), BF16),
            jax.ShapeDtypeStruct((1,), jnp.int32),
        ),
        in_specs=[pl.BlockSpec(memory_space=pltpu.SMEM), vmem, vmem, vmem],
        out_specs=(vmem, pl.BlockSpec(memory_space=pltpu.SMEM)),
        compiler_params=pltpu.CompilerParams(vmem_limit_bytes=8 << 20),
        cost_estimate=pl.CostEstimate(
            flops=2 * n * total * width, bytes_accessed=2 * total * width, transcendentals=0
        ),
        name="select_rows",
    )(round_index, pivots.reshape(1, n), slots, so_far)


def spread_kernel(where_from_ref, piv_ref, came_ref, out_ref, *, mu, nu):
    owners, depth, k = came_ref.shape
    n = piv_ref.shape[1]
    line, turn, part = (where_from_ref[i] for i in (0, 2, 3))
    offset = jnp.broadcast_to(piv_ref[...] - line, (owners, n))
    low = lax.broadcasted_iota(jnp.int32, (owners, n), 0) * nu
    count = jnp.zeros((owners, n), F32)
    for m in range(mu):
        inside = offset - m * NBAS - low
        count += jnp.where((inside >= 0) & (inside < nu), 1.0, 0.0)
    count = jnp.sum(count, axis=1, keepdims=True) - (turn * depth).astype(F32)
    count = jnp.clip(count, 0.0, depth)
    wide = (owners, owners * depth)
    slot = lax.broadcasted_iota(jnp.int32, wide, 1) - lax.broadcasted_iota(jnp.int32, wide, 0) * depth
    here = (slot >= 0) & (slot < depth)
    start = jnp.sum(jnp.where(slot >= depth, count, 0.0), axis=0, keepdims=True)
    used = jnp.sum(jnp.where(here & (slot.astype(F32) < count), 1.0, 0.0), axis=0, keepdims=True)
    place = start + jnp.sum(jnp.where(here, slot.astype(F32), 0.0), axis=0, keepdims=True)
    place = place - (part * SLOTS).astype(F32)
    packed = lax.broadcasted_iota(jnp.int32, (SLOTS, wide[1]), 0).astype(F32)
    hot = jnp.where((packed == place) & (used > 0.0), 1.0, 0.0).astype(BF16)
    rows = came_ref[...].astype(F32).reshape(wide[1], k).astype(BF16)
    rows = jnp.dot(hot, rows, preferred_element_type=F32).astype(BF16)
    half = out_ref.shape[2]
    for c in range(2):
        piece = rows[:, c * half : (c + 1) * half]

        @pl.loop(0, out_ref.shape[0] // 2)
        def _(chip):
            out_ref[2 * chip + c] = piece


def spread(where_from, pivots, came, n_rows, mu, nu):
    k = came.shape[2]
    n = pivots.shape[0]
    vmem = pl.BlockSpec(memory_space=pltpu.VMEM)
    return pl.pallas_call(
        functools.partial(spread_kernel, mu=mu, nu=nu),
        out_shape=jax.ShapeDtypeStruct((n_rows, SLOTS, k // 2), BF16),
        in_specs=[pl.BlockSpec(memory_space=pltpu.SMEM), vmem, vmem],
        out_specs=vmem,
        compiler_params=pltpu.CompilerParams(vmem_limit_bytes=4 << 20),
        cost_estimate=pl.CostEstimate(
            flops=came.size, bytes_accessed=n_rows * SLOTS * k, transcendentals=0
        ),
        name="spread",
    )(where_from, pivots.reshape(1, n), came)


def preload_kernel(prev_ref, after_ref, out_ref, sems):
    copies = [
        pltpu.make_async_copy(prev_ref.at[m], out_ref.at[m], sems.at[m])
        for m in range(out_ref.shape[0])
    ]
    for copy in copies:
        copy.start()
    for copy in copies:
        copy.wait()


def preload(previous, count, after):
    shape = (count,) + previous.shape[1:]
    return pl.pallas_call(
        preload_kernel,
        out_shape=jax.ShapeDtypeStruct(shape, previous.dtype),
        in_specs=[pl.BlockSpec(memory_space=pltpu.HBM), pl.BlockSpec(memory_space=pl.ANY)],
        out_specs=pl.BlockSpec(memory_space=pltpu.VMEM),
        scratch_shapes=[pltpu.SemaphoreType.DMA((count,))],
        compiler_params=pltpu.CompilerParams(vmem_limit_bytes=4 << 20),
        cost_estimate=pl.CostEstimate(
            flops=0, bytes_accessed=previous.size, transcendentals=0
        ),
        name="preload",
    )(previous, after)


def vectors_kernel(
    core_ref, me_ref, cols_ref, first_ref, prev_ref, mine_ref, other_ref, inv_ref, orb_ref,
    new_ref, turned_ref, far_ref, came, made, load, store, far_sem, *, owners
):
    early, mu = first_ref.shape[0], cols_ref.shape[0]
    width = far_ref.shape[1]
    column = pl.multiple_of(lax.rem(me_ref[0] + owners // 2, owners) * width, width)
    far = pltpu.make_async_copy(orb_ref.at[:, pl.ds(column, width)], far_ref, far_sem)

    def load_of(i):
        return pltpu.make_async_copy(prev_ref.at[early + i], came.at[i], load.at[i])

    def store_of(m):
        return pltpu.make_async_copy(made.at[m], new_ref.at[m], store.at[m])

    def step(m, prev):
        mine, other = mine_ref[...].astype(F32), other_ref[...].astype(F32)
        first = core_ref[0] == 0
        rows = jnp.concatenate(
            [jnp.where(first, mine, other), jnp.where(first, other, mine)], axis=1
        ).astype(BF16)
        contract = (((1,), (1,)), ((), ()))
        correction = lax.dot_general(prev, rows, contract, preferred_element_type=F32)
        residual = (cols_ref[m].astype(F32) - correction).astype(BF16)
        inv = inv_ref[...]
        row, column = (lax.broadcasted_iota(jnp.int32, inv.shape, d) for d in (0, 1))
        upper = jnp.where(row > column, 0.0, inv.astype(F32)).astype(BF16)
        new = jnp.dot(residual, upper, preferred_element_type=F32).astype(BF16)
        made[m] = new
        store_of(m).start()
        turned_ref[m] = new.T

    for i in range(mu - early):
        load_of(i).start()
    far.start()

    @pl.loop(0, early)
    def _(m):
        step(m, first_ref[m])

    @pl.loop(0, mu - early)
    def _(i):
        load_of(i).wait()
        step(early + i, came[i])

    far.wait()
    for m in range(mu):
        store_of(m).wait()


def vectors(core, me, pivot_columns, first, previous, mine, other, pivot_inverse, orbitals, owners):
    mu, nu, k = previous.shape
    n = pivot_columns.shape[2]
    width = orbitals.shape[1] // owners
    smem = pl.BlockSpec(memory_space=pltpu.SMEM)
    vmem = pl.BlockSpec(memory_space=pltpu.VMEM)
    hbm = pl.BlockSpec(memory_space=pltpu.HBM)
    return pl.pallas_call(
        functools.partial(vectors_kernel, owners=owners),
        out_shape=(
            jax.ShapeDtypeStruct((mu, nu, n), BF16),
            jax.ShapeDtypeStruct((mu, n, nu), BF16),
            jax.ShapeDtypeStruct((nu, width), BF16),
        ),
        in_specs=[smem, smem, vmem, vmem, hbm, vmem, vmem, vmem, hbm],
        out_specs=(pl.BlockSpec(memory_space=pl.ANY), vmem, vmem),
        scratch_shapes=[
            pltpu.VMEM((mu - first.shape[0], nu, k), BF16),
            pltpu.VMEM((mu, nu, n), BF16),
            pltpu.SemaphoreType.DMA((mu - first.shape[0],)),
            pltpu.SemaphoreType.DMA((mu,)),
            pltpu.SemaphoreType.DMA,
        ],
        compiler_params=pltpu.CompilerParams(vmem_limit_bytes=24 << 20),
        cost_estimate=pl.CostEstimate(
            flops=2 * mu * nu * n * (k + n),
            bytes_accessed=2 * mu * nu * (k + 3 * n),
            transcendentals=0,
        ),
        name="vectors",
    )(core, me, pivot_columns, first, previous, mine, other, pivot_inverse, orbitals)


def bring_kernel(orb_ref, after_ref, out_ref, sems):
    count = sems.shape[0]
    rows = out_ref.shape[0] // count
    copies = [
        pltpu.make_async_copy(
            orb_ref.at[pl.ds(i * rows, rows)], out_ref.at[pl.ds(i * rows, rows)], sems.at[i]
        )
        for i in range(count)
    ]
    for copy in copies:
        copy.start()
    for copy in copies:
        copy.wait()


def bring(orbitals, after):
    return pl.pallas_call(
        bring_kernel,
        out_shape=jax.ShapeDtypeStruct(orbitals.shape, orbitals.dtype),
        in_specs=[pl.BlockSpec(memory_space=pltpu.HBM), pl.BlockSpec(memory_space=pl.ANY)],
        out_specs=pl.BlockSpec(memory_space=pltpu.VMEM),
        scratch_shapes=[pltpu.SemaphoreType.DMA((4,))],
        compiler_params=pltpu.CompilerParams(vmem_limit_bytes=4 << 20),
        cost_estimate=pl.CostEstimate(
            flops=0, bytes_accessed=2 * orbitals.size, transcendentals=0
        ),
        name="bring",
    )(orbitals, after)


def parts_kernel(me_ref, turned_ref, orb_ref, *out_refs, ahead, owners):
    mu, n, nu = turned_ref.shape
    keep, width = out_refs[0].shape[-2:]
    columns = [orb_ref[...]] if len(out_refs) == 2 else []
    for a in ahead[: 0 if columns else None]:
        start = pl.multiple_of(lax.rem(me_ref[0] + a, owners) * width, width)
        columns.append(orb_ref[:, pl.ds(start, width)])
    columns = columns[0] if len(columns) == 1 else jnp.concatenate(columns, axis=1)
    for m in range(mu):
        part = jnp.dot(turned_ref[m], columns, preferred_element_type=F32)
        if len(out_refs) == 2:
            half = n // 2
            for h, out_ref in enumerate(out_refs):
                piece = part[h * half : (h + 1) * half].reshape(half // keep, keep, width)
                out_ref[:, m] = piece.astype(out_ref.dtype)
        else:
            for q in range(len(ahead)):
                piece = part[:, q * width : (q + 1) * width].reshape(n // keep, keep, width)
                out_refs[0][q, :, m] = piece


def parts(me, turned, orbitals, ahead, owners, dests, send=False):
    mu, n, nu = turned.shape
    width = orbitals.shape[1] // (1 if send else owners)
    if send:
        shape = (dests // 2, mu, n // dests, width)
        out_shape = (jax.ShapeDtypeStruct(shape, BF16),) * 2
    else:
        shape = (len(ahead), dests, mu, n // dests, width)
        out_shape = jax.ShapeDtypeStruct(shape, F32)
    vmem = pl.BlockSpec(memory_space=pltpu.VMEM)
    return pl.pallas_call(
        functools.partial(parts_kernel, ahead=ahead, owners=owners),
        out_shape=out_shape,
        in_specs=[pl.BlockSpec(memory_space=pltpu.SMEM), vmem, vmem],
        out_specs=(vmem, vmem) if send else vmem,
        compiler_params=pltpu.CompilerParams(vmem_limit_bytes=20 << 20),
        cost_estimate=pl.CostEstimate(
            flops=2 * mu * n * nu * width * len(ahead),
            bytes_accessed=2 * mu * n * nu,
            transcendentals=0,
        ),
        name="parts",
    )(me, turned, orbitals)


def join_kernel(own_ref, came_ref, out_ref, *, second):
    half = came_ref.shape[0]
    mine, other = (slice(half, None), slice(0, half)) if second else (slice(0, half), slice(half, None))
    out_ref[mine] = (own_ref[0, mine] + came_ref[...].astype(F32)).astype(BF16)
    out_ref[other] = own_ref[0, other].astype(BF16)


def join(part, which, came, second):
    shape = part.shape[1:]
    return pl.pallas_call(
        functools.partial(join_kernel, second=second),
        grid=(1,),
        out_shape=jax.ShapeDtypeStruct(shape, BF16),
        in_specs=[
            pl.BlockSpec((1,) + shape, lambda i: (which, 0, 0, 0, 0)),
            pl.BlockSpec(came.shape, lambda i: (0, 0, 0, 0)),
        ],
        out_specs=pl.BlockSpec(shape, lambda i: (0, 0, 0, 0)),
        compiler_params=pltpu.CompilerParams(vmem_limit_bytes=6 << 20),
        cost_estimate=pl.CostEstimate(
            flops=came.size, bytes_accessed=12 * came.size, transcendentals=0
        ),
        name="join",
    )(part, came)


def add_kernel(own_ref, came_ref, out_ref):
    out_ref[...] = (own_ref[0] + came_ref[...].astype(F32)).astype(BF16)


def add(part, which, came):
    shape = came.shape
    zeros = lambda i: (0, 0, 0, 0)
    return pl.pallas_call(
        add_kernel,
        grid=(1,),
        out_shape=jax.ShapeDtypeStruct(shape, BF16),
        in_specs=[
            pl.BlockSpec((1,) + shape, lambda i: (which, 0, 0, 0, 0)),
            pl.BlockSpec(shape, zeros),
        ],
        out_specs=pl.BlockSpec(shape, zeros),
        compiler_params=pltpu.CompilerParams(vmem_limit_bytes=6 << 20),
        cost_estimate=pl.CostEstimate(
            flops=came.size, bytes_accessed=8 * came.size, transcendentals=0
        ),
        name="add",
    )(part, came)


def reduce_to_owner(me, turned, columns, orbitals, owners, dests):
    far = owners // 2

    def hop(x, way):
        return lax.ppermute(x, "grp", [(i, (i + way) % owners) for i in range(owners)])

    right, left = parts(me, turned, columns, (far,), owners, dests, send=True)
    orbitals = bring(orbitals, right)
    right, left = hop(right, 1), hop(left, -1)

    def own(ahead):
        return parts(me, turned, orbitals, ahead, owners, dests)

    near = own((far - 1, far + 1))
    right, left = hop(join(near, 0, right, False), 1), hop(join(near, 1, left, True), -1)
    for ahead in range(far - 2, 0, -1):
        near = own((ahead, owners - ahead))
        right, left = (
            hop(add(near, q, x), way)
            for q, (x, way) in enumerate(((right, 1), (left, -1)))
        )
    return own((0,))[0] + right.astype(F32) + left.astype(F32)


def final_kernel(half_ref, slab_ref, out_ref):
    rows, width = half_ref.shape
    mu = slab_ref.shape[0]
    keep = rows // mu
    slab_t = slab_ref[...].T
    slab_t = jnp.concatenate([slab_t, slab_t], axis=1)
    for p in range(0, keep, 2):
        pair = jnp.concatenate(
            [half_ref[pl.ds(q, mu, stride=keep), :] for q in (p, p + 1)], axis=1
        )
        high = pair.astype(BF16)
        low = (pair - high.astype(F32)).astype(BF16)
        both = jnp.dot(slab_t, jnp.concatenate([high, low], axis=0), preferred_element_type=F32)
        out_ref[p] = both[:, :width].astype(BF16)
        out_ref[p + 1] = both[:, width:].astype(BF16)


def final(half, slab):
    mu, occ = slab.shape
    rows, width = half.shape
    keep = rows // mu
    return pl.pallas_call(
        final_kernel,
        out_shape=jax.ShapeDtypeStruct((keep, occ, width), BF16),
        compiler_params=pltpu.CompilerParams(vmem_limit_bytes=16 << 20),
        cost_estimate=pl.CostEstimate(
            flops=4 * rows * width * occ,
            bytes_accessed=2 * keep * width * (2 * mu + occ),
            transcendentals=0,
        ),
        name="final",
    )(half, slab)


def exchange(x, axis):
    return lax.all_to_all(x, axis, split_axis=0, concat_axis=0, tiled=True)


def pivot_halves(n_rows, n_grp, pivots, previous, columns):
    mu, nu, k = previous.shape
    n = pivots.shape[0]
    half = k // 2
    per_line = mu * NBAS
    line = lax.axis_index("rows") * per_line
    base = line + lax.axis_index("grp") * nu
    line, base = line.astype(jnp.int32), base.astype(jnp.int32)

    def one_round(index, so_far, columns=None):
        index = jnp.asarray(index, jnp.int32)
        turn, part = index // PARTS, index % PARTS
        where_from = jnp.stack([line, base, turn, part])
        picked, *close = pick_rows(where_from, pivots, previous, columns)
        came = exchange(jnp.broadcast_to(picked, (n_grp,) + picked.shape), "grp")
        messages = spread(where_from, pivots, came, n_rows, mu, nu)
        slots = exchange(messages, "rows").reshape(n_rows * SLOTS, half)
        rows, rounds = select_rows(index.reshape(1), pivots, slots, so_far, per_line, nu, n_grp)
        return rows, rounds, *close

    mine, rounds, close = one_round(0, jnp.zeros((n, half), BF16), columns)
    start, mine, rounds = lax.optimization_barrier((jnp.int32(1), mine, rounds))
    mine = lax.fori_loop(start, rounds[0], lambda i, rows: one_round(i, rows)[0], mine)
    other = lax.ppermute(mine, "rows", [(i, i ^ 1) for i in range(n_rows)])
    return mine, other, close


def per_device(n_rows, n_grp, pivot_columns, previous, pivots, pivot_inverse, orbitals, slab_orbitals):
    previous, pivot_columns, orbitals = (
        pltpu.with_memory_space_constraint(x, pltpu.HBM) for x in (previous, pivot_columns, orbitals)
    )
    mine, other, close = pivot_halves(n_rows, n_grp, pivots, previous, pivot_columns)
    core = (lax.axis_index("rows") % 2).reshape(1).astype(jnp.int32)
    me = lax.axis_index("grp").reshape(1).astype(jnp.int32)
    first = preload(previous, previous.shape[0] // 2, mine)
    new_vectors, turned, far = vectors(
        core, me, close, first, previous, mine, other, pivot_inverse, orbitals, n_grp
    )
    half = exchange(reduce_to_owner(me, turned, far, orbitals, n_grp, n_rows), "rows")
    return new_vectors, final(half.reshape(-1, half.shape[-1]), slab_orbitals)


def solution(mesh):
    in_specs = (P("rows", "grp", None), P("rows", "grp", None), P(), P(), P("grp", None), P())
    out_specs = (P("rows", "grp", None), P("rows", None, "grp"))
    body = functools.partial(per_device, mesh.shape["rows"], mesh.shape["grp"])
    return jax.shard_map(body, mesh=mesh, in_specs=in_specs, out_specs=out_specs, check_vma=False)
```

```python
import functools

import jax
import jax.numpy as jnp
from jax import lax
from jax.experimental import pallas as pl
from jax.experimental.pallas import tpu as pltpu
from jax.sharding import PartitionSpec as P

NBAS = 10240
F32 = jnp.float32
BF16 = jnp.bfloat16
DEPTH = 8
SLOTS = 24
PARTS = 3


def pick_kernel(where_from_ref, piv_ref, prev_ref, *refs, bring):
    if bring:
        cols_ref, out_ref, close_ref, acc_ref, held, sems, rows_ref, close_sems = refs
        copies = [
            pltpu.make_async_copy(cols_ref.at[m], close_ref.at[m], close_sems.at[m])
            for m in range(cols_ref.shape[0])
        ]
    else:
        out_ref, acc_ref, held, sems, rows_ref = refs
        copies = []
    for copy in copies:
        copy.start()
    mu, nu, _ = prev_ref.shape
    depth, group, _ = held.shape
    base, turn = where_from_ref[1], where_from_ref[2]
    acc_ref[...] = jnp.zeros_like(acc_ref)
    pivots = piv_ref[...]
    order = lax.broadcasted_iota(jnp.int32, pivots.shape, 0) * pivots.shape[1]
    order += lax.broadcasted_iota(jnp.int32, pivots.shape, 1)
    many = 1 << (mu * nu - 1).bit_length()
    last = many * pivots.size
    keys = jnp.full_like(pivots, last)
    for m in range(mu):
        inside = pivots - base - m * NBAS
        keys = jnp.where((inside >= 0) & (inside < nu), order * many + inside + m * nu, keys)
    owned = jnp.sum((keys < last).astype(jnp.int32))
    skip = turn * depth
    total = jnp.clip(owned - skip, 0, depth)

    def fetch(row, i):
        m = jnp.int32(0)
        for step in range(1, mu):
            m += (row >= step * nu).astype(jnp.int32)
        start = pl.multiple_of((row - m * nu) // group * group, group)
        return pltpu.make_async_copy(prev_ref.at[m, pl.ds(start, group)], held.at[i], sems.at[i])

    def find(i, key):
        key = jnp.min(jnp.where(keys > key, keys, last))

        @pl.when(i >= skip)
        def _():
            row = key & (many - 1)
            rows_ref[i - skip] = row
            fetch(row, i - skip).start()

        return key

    lax.fori_loop(0, skip + total, find, jnp.int32(-1))

    def place(i, _):
        row = rows_ref[i]
        fetch(row, i).wait()
        rows = held[i].astype(F32)
        keep = lax.broadcasted_iota(jnp.int32, rows.shape, 0) == row % group
        acc_ref[pl.ds(i, 1), :] = jnp.sum(jnp.where(keep, rows, 0.0), axis=0, keepdims=True)
        return 0

    lax.fori_loop(0, total, place, 0)
    out_ref[...] = acc_ref[...].astype(BF16)
    for copy in copies:
        copy.wait()


def pick_rows(where_from, pivots, previous, columns=None):
    n = pivots.shape[0]
    k = previous.shape[2]
    lanes = 128
    vmem = pl.BlockSpec(memory_space=pltpu.VMEM)
    hbm = pl.BlockSpec(memory_space=pltpu.HBM)
    args = [where_from, pivots.reshape(n // lanes, lanes), previous]
    out_shape = [jax.ShapeDtypeStruct((DEPTH, k), BF16)]
    scratch = [
        pltpu.VMEM((DEPTH, k), F32),
        pltpu.VMEM((DEPTH, 16, k), BF16),
        pltpu.SemaphoreType.DMA((DEPTH,)),
        pltpu.SMEM((DEPTH,), jnp.int32),
    ]
    bring = columns is not None
    if bring:
        args.append(columns)
        out_shape.append(jax.ShapeDtypeStruct(columns.shape, columns.dtype))
        scratch.append(pltpu.SemaphoreType.DMA((columns.shape[0],)))
    return pl.pallas_call(
        functools.partial(pick_kernel, bring=bring),
        out_shape=out_shape,
        in_specs=[pl.BlockSpec(memory_space=pltpu.SMEM), vmem, hbm] + [hbm] * bring,
        out_specs=[vmem] * len(out_shape),
        scratch_shapes=scratch,
        compiler_params=pltpu.CompilerParams(vmem_limit_bytes=4 << 20),
        cost_estimate=pl.CostEstimate(flops=n * k, bytes_accessed=2 * n * k, transcendentals=0),
        name="pick_rows",
    )(*args)


def whole_part(x, by):
    return jnp.floor((x + 0.5) * (1.0 / by))


def select_kernel(round_ref, piv_ref, slots_ref, so_far_ref, out_ref, rounds_ref, *, per_line, nu, owners):
    total, _ = slots_ref.shape
    n = piv_ref.shape[1]
    pivot = piv_ref[...].astype(F32)
    line = whole_part(pivot, per_line)
    inside = pivot - line * per_line
    inside = inside - whole_part(inside, NBAS) * NBAS
    device = jnp.broadcast_to(line * owners + whole_part(inside, nu), (n, n))
    mine = device.T
    before = lax.broadcasted_iota(jnp.int32, (n, n), 1) < lax.broadcasted_iota(jnp.int32, (n, n), 0)
    rank = jnp.sum(jnp.where((device == mine) & before, 1.0, 0.0), axis=1, keepdims=True)
    turn = whole_part(rank, DEPTH)
    turns = jnp.broadcast_to(turn, (n, n))
    my_line = whole_part(mine, owners)
    ahead = (device >= my_line * owners) & (device < mine) & (turns.T == turns)
    place = jnp.sum(jnp.where(ahead, 1.0, 0.0), axis=1, keepdims=True) + rank - turn * DEPTH
    part = whole_part(place, SLOTS)
    when = turn * PARTS + part
    rounds_ref[0] = jnp.max(when).astype(jnp.int32) + 1
    index = my_line[:, :1] * SLOTS + place - part * SLOTS
    index = jnp.where(when == round_ref[0].astype(F32), index, -1.0).astype(jnp.int32)
    hot = index == lax.broadcasted_iota(jnp.int32, (n, total), 1)
    hot = jnp.where(hot, 1.0, 0.0).astype(BF16)
    picked = jnp.dot(hot, slots_ref[...], preferred_element_type=F32)
    out_ref[...] = (picked + so_far_ref[...].astype(F32)).astype(BF16)


def select_rows(round_index, pivots, slots, so_far, per_line, nu, owners):
    total, width = slots.shape
    n = pivots.shape[0]
    vmem = pl.BlockSpec(memory_space=pltpu.VMEM)
    return pl.pallas_call(
        functools.partial(select_kernel, per_line=per_line, nu=nu, owners=owners),
        out_shape=(
            jax.ShapeDtypeStruct((n, width), BF16),
            jax.ShapeDtypeStruct((1,), jnp.int32),
        ),
        in_specs=[pl.BlockSpec(memory_space=pltpu.SMEM), vmem, vmem, vmem],
        out_specs=(vmem, pl.BlockSpec(memory_space=pltpu.SMEM)),
        compiler_params=pltpu.CompilerParams(vmem_limit_bytes=8 << 20),
        cost_estimate=pl.CostEstimate(
            flops=2 * n * total * width, bytes_accessed=2 * total * width, transcendentals=0
        ),
        name="select_rows",
    )(round_index, pivots.reshape(1, n), slots, so_far)


def spread_kernel(where_from_ref, piv_ref, came_ref, out_ref, *, mu, nu):
    owners, depth, k = came_ref.shape
    n = piv_ref.shape[1]
    line, turn, part = (where_from_ref[i] for i in (0, 2, 3))
    offset = jnp.broadcast_to(piv_ref[...] - line, (owners, n))
    low = lax.broadcasted_iota(jnp.int32, (owners, n), 0) * nu
    count = jnp.zeros((owners, n), F32)
    for m in range(mu):
        inside = offset - m * NBAS - low
        count += jnp.where((inside >= 0) & (inside < nu), 1.0, 0.0)
    count = jnp.sum(count, axis=1, keepdims=True) - (turn * depth).astype(F32)
    count = jnp.clip(count, 0.0, depth)
    wide = (owners, owners * depth)
    slot = lax.broadcasted_iota(jnp.int32, wide, 1) - lax.broadcasted_iota(jnp.int32, wide, 0) * depth
    here = (slot >= 0) & (slot < depth)
    start = jnp.sum(jnp.where(slot >= depth, count, 0.0), axis=0, keepdims=True)
    used = jnp.sum(jnp.where(here & (slot.astype(F32) < count), 1.0, 0.0), axis=0, keepdims=True)
    place = start + jnp.sum(jnp.where(here, slot.astype(F32), 0.0), axis=0, keepdims=True)
    place = place - (part * SLOTS).astype(F32)
    packed = lax.broadcasted_iota(jnp.int32, (SLOTS, wide[1]), 0).astype(F32)
    hot = jnp.where((packed == place) & (used > 0.0), 1.0, 0.0).astype(BF16)
    rows = came_ref[...].astype(F32).reshape(wide[1], k).astype(BF16)
    rows = jnp.dot(hot, rows, preferred_element_type=F32).astype(BF16)
    half = out_ref.shape[2]
    for c in range(2):
        piece = rows[:, c * half : (c + 1) * half]

        @pl.loop(0, out_ref.shape[0] // 2)
        def _(chip):
            out_ref[2 * chip + c] = piece


def spread(where_from, pivots, came, n_rows, mu, nu):
    k = came.shape[2]
    n = pivots.shape[0]
    vmem = pl.BlockSpec(memory_space=pltpu.VMEM)
    return pl.pallas_call(
        functools.partial(spread_kernel, mu=mu, nu=nu),
        out_shape=jax.ShapeDtypeStruct((n_rows, SLOTS, k // 2), BF16),
        in_specs=[pl.BlockSpec(memory_space=pltpu.SMEM), vmem, vmem],
        out_specs=vmem,
        compiler_params=pltpu.CompilerParams(vmem_limit_bytes=4 << 20),
        cost_estimate=pl.CostEstimate(
            flops=came.size, bytes_accessed=n_rows * SLOTS * k, transcendentals=0
        ),
        name="spread",
    )(where_from, pivots.reshape(1, n), came)


def preload_kernel(prev_ref, after_ref, out_ref, sems):
    copies = [
        pltpu.make_async_copy(prev_ref.at[m], out_ref.at[m], sems.at[m])
        for m in range(out_ref.shape[0])
    ]
    for copy in copies:
        copy.start()
    for copy in copies:
        copy.wait()


def preload(previous, count, after):
    shape = (count,) + previous.shape[1:]
    return pl.pallas_call(
        preload_kernel,
        out_shape=jax.ShapeDtypeStruct(shape, previous.dtype),
        in_specs=[pl.BlockSpec(memory_space=pltpu.HBM), pl.BlockSpec(memory_space=pl.ANY)],
        out_specs=pl.BlockSpec(memory_space=pltpu.VMEM),
        scratch_shapes=[pltpu.SemaphoreType.DMA((count,))],
        compiler_params=pltpu.CompilerParams(vmem_limit_bytes=4 << 20),
        cost_estimate=pl.CostEstimate(
            flops=0, bytes_accessed=previous.size, transcendentals=0
        ),
        name="preload",
    )(previous, after)


def vectors_kernel(
    core_ref, me_ref, cols_ref, first_ref, prev_ref, mine_ref, other_ref, inv_ref, orb_ref,
    new_ref, turned_ref, far_ref, came, made, load, store, far_sem, rows_ref, upper_ref, *, owners
):
    early, mu = first_ref.shape[0], cols_ref.shape[0]
    width = far_ref.shape[1]
    column = pl.multiple_of(lax.rem(me_ref[0] + owners // 2, owners) * width, width)
    far = pltpu.make_async_copy(orb_ref.at[:, pl.ds(column, width)], far_ref, far_sem)

    def load_of(i):
        return pltpu.make_async_copy(prev_ref.at[early + i], came.at[i], load.at[i])

    def store_of(m):
        return pltpu.make_async_copy(made.at[m], new_ref.at[m], store.at[m])

    def step(m, prev):
        contract = (((1,), (1,)), ((), ()))
        correction = lax.dot_general(prev, rows_ref[...], contract, preferred_element_type=F32)
        residual = (cols_ref[m].astype(F32) - correction).astype(BF16)
        new = jnp.dot(residual, upper_ref[...], preferred_element_type=F32).astype(BF16)
        made[m] = new
        store_of(m).start()
        turned_ref[m] = new.T

    for i in range(mu - early):
        load_of(i).start()
    far.start()
    mine, other = mine_ref[...].astype(F32), other_ref[...].astype(F32)
    first, half = core_ref[0] == 0, mine.shape[1]
    rows_ref[:, :half] = jnp.where(first, mine, other).astype(BF16)
    rows_ref[:, half:] = jnp.where(first, other, mine).astype(BF16)
    inv = inv_ref[...]
    row, column = (lax.broadcasted_iota(jnp.int32, inv.shape, d) for d in (0, 1))
    upper_ref[...] = jnp.where(row > column, 0.0, inv.astype(F32)).astype(BF16)

    @pl.loop(0, early)
    def _(m):
        step(m, first_ref[m])

    @pl.loop(0, mu - early)
    def _(i):
        load_of(i).wait()
        step(early + i, came[i])

    far.wait()
    for m in range(mu):
        store_of(m).wait()


def vectors(core, me, pivot_columns, first, previous, mine, other, pivot_inverse, orbitals, owners):
    mu, nu, k = previous.shape
    n = pivot_columns.shape[2]
    width = orbitals.shape[1] // owners
    smem = pl.BlockSpec(memory_space=pltpu.SMEM)
    vmem = pl.BlockSpec(memory_space=pltpu.VMEM)
    hbm = pl.BlockSpec(memory_space=pltpu.HBM)
    return pl.pallas_call(
        functools.partial(vectors_kernel, owners=owners),
        out_shape=(
            jax.ShapeDtypeStruct((mu, nu, n), BF16),
            jax.ShapeDtypeStruct((mu, n, nu), BF16),
            jax.ShapeDtypeStruct((nu, width), BF16),
        ),
        in_specs=[smem, smem, vmem, vmem, hbm, vmem, vmem, vmem, hbm],
        out_specs=(pl.BlockSpec(memory_space=pl.ANY), vmem, vmem),
        scratch_shapes=[
            pltpu.VMEM((mu - first.shape[0], nu, k), BF16),
            pltpu.VMEM((mu, nu, n), BF16),
            pltpu.SemaphoreType.DMA((mu - first.shape[0],)),
            pltpu.SemaphoreType.DMA((mu,)),
            pltpu.SemaphoreType.DMA,
            pltpu.VMEM((n, k), BF16),
            pltpu.VMEM((n, n), BF16),
        ],
        compiler_params=pltpu.CompilerParams(vmem_limit_bytes=24 << 20),
        cost_estimate=pl.CostEstimate(
            flops=2 * mu * nu * n * (k + n),
            bytes_accessed=2 * mu * nu * (k + 3 * n),
            transcendentals=0,
        ),
        name="vectors",
    )(core, me, pivot_columns, first, previous, mine, other, pivot_inverse, orbitals)


def bring_kernel(orb_ref, after_ref, out_ref, sems):
    count = sems.shape[0]
    rows = out_ref.shape[0] // count
    copies = [
        pltpu.make_async_copy(
            orb_ref.at[pl.ds(i * rows, rows)], out_ref.at[pl.ds(i * rows, rows)], sems.at[i]
        )
        for i in range(count)
    ]
    for copy in copies:
        copy.start()
    for copy in copies:
        copy.wait()


def bring(orbitals, after):
    return pl.pallas_call(
        bring_kernel,
        out_shape=jax.ShapeDtypeStruct(orbitals.shape, orbitals.dtype),
        in_specs=[pl.BlockSpec(memory_space=pltpu.HBM), pl.BlockSpec(memory_space=pl.ANY)],
        out_specs=pl.BlockSpec(memory_space=pltpu.VMEM),
        scratch_shapes=[pltpu.SemaphoreType.DMA((4,))],
        compiler_params=pltpu.CompilerParams(vmem_limit_bytes=4 << 20),
        cost_estimate=pl.CostEstimate(
            flops=0, bytes_accessed=2 * orbitals.size, transcendentals=0
        ),
        name="bring",
    )(orbitals, after)


def parts_kernel(me_ref, turned_ref, orb_ref, *out_refs, ahead, owners):
    mu, n, nu = turned_ref.shape
    keep, width = out_refs[0].shape[-2:]
    columns = [orb_ref[...]] if len(out_refs) == 2 else []
    for a in ahead[: 0 if columns else None]:
        start = pl.multiple_of(lax.rem(me_ref[0] + a, owners) * width, width)
        columns.append(orb_ref[:, pl.ds(start, width)])
    columns = columns[0] if len(columns) == 1 else jnp.concatenate(columns, axis=1)
    for m in range(mu):
        part = jnp.dot(turned_ref[m], columns, preferred_element_type=F32)
        if len(out_refs) == 2:
            half = n // 2
            for h, out_ref in enumerate(out_refs):
                piece = part[h * half : (h + 1) * half].reshape(half // keep, keep, width)
                out_ref[:, m] = piece.astype(out_ref.dtype)
        else:
            for q in range(len(ahead)):
                piece = part[:, q * width : (q + 1) * width].reshape(n // keep, keep, width)
                out_refs[0][q, :, m] = piece


def parts(me, turned, orbitals, ahead, owners, dests, send=False):
    mu, n, nu = turned.shape
    width = orbitals.shape[1] // (1 if send else owners)
    if send:
        shape = (dests // 2, mu, n // dests, width)
        out_shape = (jax.ShapeDtypeStruct(shape, BF16),) * 2
    else:
        shape = (len(ahead), dests, mu, n // dests, width)
        out_shape = jax.ShapeDtypeStruct(shape, F32)
    vmem = pl.BlockSpec(memory_space=pltpu.VMEM)
    return pl.pallas_call(
        functools.partial(parts_kernel, ahead=ahead, owners=owners),
        out_shape=out_shape,
        in_specs=[pl.BlockSpec(memory_space=pltpu.SMEM), vmem, vmem],
        out_specs=(vmem, vmem) if send else vmem,
        compiler_params=pltpu.CompilerParams(vmem_limit_bytes=20 << 20),
        cost_estimate=pl.CostEstimate(
            flops=2 * mu * n * nu * width * len(ahead),
            bytes_accessed=2 * mu * n * nu,
            transcendentals=0,
        ),
        name="parts",
    )(me, turned, orbitals)


def join_kernel(own_ref, came_ref, out_ref, *, second):
    half = came_ref.shape[0]
    mine, other = (slice(half, None), slice(0, half)) if second else (slice(0, half), slice(half, None))
    out_ref[mine] = (own_ref[0, mine] + came_ref[...].astype(F32)).astype(BF16)
    out_ref[other] = own_ref[0, other].astype(BF16)


def join(part, which, came, second):
    shape = part.shape[1:]
    return pl.pallas_call(
        functools.partial(join_kernel, second=second),
        grid=(1,),
        out_shape=jax.ShapeDtypeStruct(shape, BF16),
        in_specs=[
            pl.BlockSpec((1,) + shape, lambda i: (which, 0, 0, 0, 0)),
            pl.BlockSpec(came.shape, lambda i: (0, 0, 0, 0)),
        ],
        out_specs=pl.BlockSpec(shape, lambda i: (0, 0, 0, 0)),
        compiler_params=pltpu.CompilerParams(vmem_limit_bytes=6 << 20),
        cost_estimate=pl.CostEstimate(
            flops=came.size, bytes_accessed=12 * came.size, transcendentals=0
        ),
        name="join",
    )(part, came)


def add_kernel(own_ref, came_ref, out_ref):
    out_ref[...] = (own_ref[0] + came_ref[...].astype(F32)).astype(BF16)


def add(part, which, came):
    shape = came.shape
    zeros = lambda i: (0, 0, 0, 0)
    return pl.pallas_call(
        add_kernel,
        grid=(1,),
        out_shape=jax.ShapeDtypeStruct(shape, BF16),
        in_specs=[
            pl.BlockSpec((1,) + shape, lambda i: (which, 0, 0, 0, 0)),
            pl.BlockSpec(shape, zeros),
        ],
        out_specs=pl.BlockSpec(shape, zeros),
        compiler_params=pltpu.CompilerParams(vmem_limit_bytes=6 << 20),
        cost_estimate=pl.CostEstimate(
            flops=came.size, bytes_accessed=8 * came.size, transcendentals=0
        ),
        name="add",
    )(part, came)


def reduce_to_owner(me, turned, columns, orbitals, owners, dests):
    far = owners // 2

    def hop(x, way):
        return lax.ppermute(x, "grp", [(i, (i + way) % owners) for i in range(owners)])

    right, left = parts(me, turned, columns, (far,), owners, dests, send=True)
    orbitals = bring(orbitals, right)
    right, left = hop(right, 1), hop(left, -1)

    def own(ahead):
        return parts(me, turned, orbitals, ahead, owners, dests)

    near = own((far - 1, far + 1))
    right, left = hop(join(near, 0, right, False), 1), hop(join(near, 1, left, True), -1)
    for ahead in range(far - 2, 0, -1):
        near = own((ahead, owners - ahead))
        right, left = (
            hop(add(near, q, x), way)
            for q, (x, way) in enumerate(((right, 1), (left, -1)))
        )
    return own((0,))[0] + right.astype(F32) + left.astype(F32)


def final_kernel(half_ref, slab_ref, out_ref, made, store):
    rows, width = half_ref.shape
    mu = slab_ref.shape[0]
    keep = rows // mu
    slab_t = slab_ref[...].T
    slab_t = jnp.concatenate([slab_t, slab_t], axis=1)

    def store_of(p):
        return pltpu.make_async_copy(made.at[pl.ds(p, 2)], out_ref.at[pl.ds(p, 2)], store.at[p // 2])

    for p in range(0, keep, 2):
        pair = jnp.concatenate(
            [half_ref[pl.ds(q, mu, stride=keep), :] for q in (p, p + 1)], axis=1
        )
        high = pair.astype(BF16)
        low = (pair - high.astype(F32)).astype(BF16)
        both = jnp.dot(slab_t, jnp.concatenate([high, low], axis=0), preferred_element_type=F32)
        made[p] = both[:, :width].astype(BF16)
        made[p + 1] = both[:, width:].astype(BF16)
        store_of(p).start()
    for p in range(0, keep, 2):
        store_of(p).wait()


def final(half, slab):
    mu, occ = slab.shape
    rows, width = half.shape
    keep = rows // mu
    vmem = pl.BlockSpec(memory_space=pltpu.VMEM)
    return pl.pallas_call(
        final_kernel,
        out_shape=jax.ShapeDtypeStruct((keep, occ, width), BF16),
        in_specs=[vmem, vmem],
        out_specs=pl.BlockSpec(memory_space=pl.ANY),
        scratch_shapes=[
            pltpu.VMEM((keep, occ, width), BF16),
            pltpu.SemaphoreType.DMA((keep // 2,)),
        ],
        compiler_params=pltpu.CompilerParams(vmem_limit_bytes=16 << 20),
        cost_estimate=pl.CostEstimate(
            flops=4 * rows * width * occ,
            bytes_accessed=2 * keep * width * (2 * mu + occ),
            transcendentals=0,
        ),
        name="final",
    )(half, slab)


def exchange(x, axis):
    return lax.all_to_all(x, axis, split_axis=0, concat_axis=0, tiled=True)


def pivot_halves(n_rows, n_grp, pivots, previous, columns):
    mu, nu, k = previous.shape
    n = pivots.shape[0]
    half = k // 2
    per_line = mu * NBAS
    line = lax.axis_index("rows") * per_line
    base = line + lax.axis_index("grp") * nu
    line, base = line.astype(jnp.int32), base.astype(jnp.int32)

    def one_round(index, so_far, columns=None):
        index = jnp.asarray(index, jnp.int32)
        turn, part = index // PARTS, index % PARTS
        where_from = jnp.stack([line, base, turn, part])
        picked, *close = pick_rows(where_from, pivots, previous, columns)
        came = exchange(jnp.broadcast_to(picked, (n_grp,) + picked.shape), "grp")
        messages = spread(where_from, pivots, came, n_rows, mu, nu)
        slots = exchange(messages, "rows").reshape(n_rows * SLOTS, half)
        rows, rounds = select_rows(index.reshape(1), pivots, slots, so_far, per_line, nu, n_grp)
        return rows, rounds, *close

    mine, rounds, close = one_round(0, jnp.zeros((n, half), BF16), columns)
    start, mine, rounds = lax.optimization_barrier((jnp.int32(1), mine, rounds))
    mine = lax.fori_loop(start, rounds[0], lambda i, rows: one_round(i, rows)[0], mine)
    other = lax.ppermute(mine, "rows", [(i, i ^ 1) for i in range(n_rows)])
    return mine, other, close


def per_device(n_rows, n_grp, pivot_columns, previous, pivots, pivot_inverse, orbitals, slab_orbitals):
    previous, pivot_columns, orbitals = (
        pltpu.with_memory_space_constraint(x, pltpu.HBM) for x in (previous, pivot_columns, orbitals)
    )
    mine, other, close = pivot_halves(n_rows, n_grp, pivots, previous, pivot_columns)
    core = (lax.axis_index("rows") % 2).reshape(1).astype(jnp.int32)
    me = lax.axis_index("grp").reshape(1).astype(jnp.int32)
    first = preload(previous, previous.shape[0] // 2, mine)
    new_vectors, turned, far = vectors(
        core, me, close, first, previous, mine, other, pivot_inverse, orbitals, n_grp
    )
    half = exchange(reduce_to_owner(me, turned, far, orbitals, n_grp, n_rows), "rows")
    return new_vectors, final(half.reshape(-1, half.shape[-1]), slab_orbitals)


def solution(mesh):
    in_specs = (P("rows", "grp", None), P("rows", "grp", None), P(), P(), P("grp", None), P())
    out_specs = (P("rows", "grp", None), P("rows", None, "grp"))
    body = functools.partial(per_device, mesh.shape["rows"], mesh.shape["grp"])
    return jax.shard_map(body, mesh=mesh, in_specs=in_specs, out_specs=out_specs, check_vma=False)
```

```python
import functools

import jax
import jax.numpy as jnp
from jax import lax
from jax.experimental import pallas as pl
from jax.experimental.pallas import tpu as pltpu
from jax.sharding import PartitionSpec as P

NBAS = 10240
F32 = jnp.float32
BF16 = jnp.bfloat16
DEPTH = 8
SLOTS = 24
PARTS = 3


def pick_kernel(where_from_ref, piv_ref, prev_ref, *refs, bring):
    if bring:
        cols_ref, out_ref, close_ref, acc_ref, held, sems, rows_ref, close_sems = refs
        copies = [
            pltpu.make_async_copy(cols_ref.at[m], close_ref.at[m], close_sems.at[m])
            for m in range(cols_ref.shape[0])
        ]
    else:
        out_ref, acc_ref, held, sems, rows_ref = refs
        copies = []
    for copy in copies:
        copy.start()
    mu, nu, _ = prev_ref.shape
    depth, group, _ = held.shape
    base, turn = where_from_ref[1], where_from_ref[2]
    acc_ref[...] = jnp.zeros_like(acc_ref)
    pivots = piv_ref[...]
    order = lax.broadcasted_iota(jnp.int32, pivots.shape, 0) * pivots.shape[1]
    order += lax.broadcasted_iota(jnp.int32, pivots.shape, 1)
    many = 1 << (mu * nu - 1).bit_length()
    last = many * pivots.size
    keys = jnp.full_like(pivots, last)
    for m in range(mu):
        inside = pivots - base - m * NBAS
        keys = jnp.where((inside >= 0) & (inside < nu), order * many + inside + m * nu, keys)
    owned = jnp.sum((keys < last).astype(jnp.int32))
    skip = turn * depth
    total = jnp.clip(owned - skip, 0, depth)

    def fetch(row, i):
        m = jnp.int32(0)
        for step in range(1, mu):
            m += (row >= step * nu).astype(jnp.int32)
        start = pl.multiple_of((row - m * nu) // group * group, group)
        return pltpu.make_async_copy(prev_ref.at[m, pl.ds(start, group)], held.at[i], sems.at[i])

    def find(i, key):
        key = jnp.min(jnp.where(keys > key, keys, last))

        @pl.when(i >= skip)
        def _():
            row = key & (many - 1)
            rows_ref[i - skip] = row
            fetch(row, i - skip).start()

        return key

    lax.fori_loop(0, skip + total, find, jnp.int32(-1))

    def place(i, _):
        row = rows_ref[i]
        fetch(row, i).wait()
        rows = held[i].astype(F32)
        keep = lax.broadcasted_iota(jnp.int32, rows.shape, 0) == row % group
        acc_ref[pl.ds(i, 1), :] = jnp.sum(jnp.where(keep, rows, 0.0), axis=0, keepdims=True)
        return 0

    lax.fori_loop(0, total, place, 0)
    out_ref[...] = acc_ref[...].astype(BF16)
    for copy in copies:
        copy.wait()


def pick_rows(where_from, pivots, previous, columns=None):
    n = pivots.shape[0]
    k = previous.shape[2]
    lanes = 128
    vmem = pl.BlockSpec(memory_space=pltpu.VMEM)
    hbm = pl.BlockSpec(memory_space=pltpu.HBM)
    args = [where_from, pivots.reshape(n // lanes, lanes), previous]
    out_shape = [jax.ShapeDtypeStruct((DEPTH, k), BF16)]
    scratch = [
        pltpu.VMEM((DEPTH, k), F32),
        pltpu.VMEM((DEPTH, 16, k), BF16),
        pltpu.SemaphoreType.DMA((DEPTH,)),
        pltpu.SMEM((DEPTH,), jnp.int32),
    ]
    bring = columns is not None
    if bring:
        args.append(columns)
        out_shape.append(jax.ShapeDtypeStruct(columns.shape, columns.dtype))
        scratch.append(pltpu.SemaphoreType.DMA((columns.shape[0],)))
    return pl.pallas_call(
        functools.partial(pick_kernel, bring=bring),
        out_shape=out_shape,
        in_specs=[pl.BlockSpec(memory_space=pltpu.SMEM), vmem, hbm] + [hbm] * bring,
        out_specs=[vmem] * len(out_shape),
        scratch_shapes=scratch,
        compiler_params=pltpu.CompilerParams(vmem_limit_bytes=4 << 20),
        cost_estimate=pl.CostEstimate(flops=n * k, bytes_accessed=2 * n * k, transcendentals=0),
        name="pick_rows",
    )(*args)


def whole_part(x, by):
    return jnp.floor((x + 0.5) * (1.0 / by))


def select_kernel(round_ref, piv_ref, slots_ref, so_far_ref, out_ref, rounds_ref, *, per_line, nu, owners):
    total, _ = slots_ref.shape
    n = piv_ref.shape[1]
    pivot = piv_ref[...].astype(F32)
    line = whole_part(pivot, per_line)
    inside = pivot - line * per_line
    inside = inside - whole_part(inside, NBAS) * NBAS
    device = jnp.broadcast_to(line * owners + whole_part(inside, nu), (n, n))
    mine = device.T
    before = lax.broadcasted_iota(jnp.int32, (n, n), 1) < lax.broadcasted_iota(jnp.int32, (n, n), 0)
    rank = jnp.sum(jnp.where((device == mine) & before, 1.0, 0.0), axis=1, keepdims=True)
    turn = whole_part(rank, DEPTH)
    turns = jnp.broadcast_to(turn, (n, n))
    my_line = whole_part(mine, owners)
    ahead = (device >= my_line * owners) & (device < mine) & (turns.T == turns)
    place = jnp.sum(jnp.where(ahead, 1.0, 0.0), axis=1, keepdims=True) + rank - turn * DEPTH
    part = whole_part(place, SLOTS)
    when = turn * PARTS + part
    rounds_ref[0] = jnp.max(when).astype(jnp.int32) + 1
    index = my_line[:, :1] * SLOTS + place - part * SLOTS
    index = jnp.where(when == round_ref[0].astype(F32), index, -1.0).astype(jnp.int32)
    hot = index == lax.broadcasted_iota(jnp.int32, (n, total), 1)
    hot = jnp.where(hot, 1.0, 0.0).astype(BF16)
    picked = jnp.dot(hot, slots_ref[...], preferred_element_type=F32)
    out_ref[...] = (picked + so_far_ref[...].astype(F32)).astype(BF16)


def select_rows(round_index, pivots, slots, so_far, per_line, nu, owners):
    total, width = slots.shape
    n = pivots.shape[0]
    vmem = pl.BlockSpec(memory_space=pltpu.VMEM)
    return pl.pallas_call(
        functools.partial(select_kernel, per_line=per_line, nu=nu, owners=owners),
        out_shape=(
            jax.ShapeDtypeStruct((n, width), BF16),
            jax.ShapeDtypeStruct((1,), jnp.int32),
        ),
        in_specs=[pl.BlockSpec(memory_space=pltpu.SMEM), vmem, vmem, vmem],
        out_specs=(vmem, pl.BlockSpec(memory_space=pltpu.SMEM)),
        compiler_params=pltpu.CompilerParams(vmem_limit_bytes=8 << 20),
        cost_estimate=pl.CostEstimate(
            flops=2 * n * total * width, bytes_accessed=2 * total * width, transcendentals=0
        ),
        name="select_rows",
    )(round_index, pivots.reshape(1, n), slots, so_far)


def spread_kernel(where_from_ref, piv_ref, came_ref, out_ref, *, mu, nu):
    owners, depth, k = came_ref.shape
    n = piv_ref.shape[1]
    line, turn, part = (where_from_ref[i] for i in (0, 2, 3))
    offset = jnp.broadcast_to(piv_ref[...] - line, (owners, n))
    low = lax.broadcasted_iota(jnp.int32, (owners, n), 0) * nu
    count = jnp.zeros((owners, n), F32)
    for m in range(mu):
        inside = offset - m * NBAS - low
        count += jnp.where((inside >= 0) & (inside < nu), 1.0, 0.0)
    count = jnp.sum(count, axis=1, keepdims=True) - (turn * depth).astype(F32)
    count = jnp.clip(count, 0.0, depth)
    wide = (owners, owners * depth)
    slot = lax.broadcasted_iota(jnp.int32, wide, 1) - lax.broadcasted_iota(jnp.int32, wide, 0) * depth
    here = (slot >= 0) & (slot < depth)
    start = jnp.sum(jnp.where(slot >= depth, count, 0.0), axis=0, keepdims=True)
    used = jnp.sum(jnp.where(here & (slot.astype(F32) < count), 1.0, 0.0), axis=0, keepdims=True)
    place = start + jnp.sum(jnp.where(here, slot.astype(F32), 0.0), axis=0, keepdims=True)
    place = place - (part * SLOTS).astype(F32)
    packed = lax.broadcasted_iota(jnp.int32, (SLOTS, wide[1]), 0).astype(F32)
    hot = jnp.where((packed == place) & (used > 0.0), 1.0, 0.0).astype(BF16)
    rows = came_ref[...].astype(F32).reshape(wide[1], k).astype(BF16)
    rows = jnp.dot(hot, rows, preferred_element_type=F32).astype(BF16)
    half = out_ref.shape[2]
    for c in range(2):
        piece = rows[:, c * half : (c + 1) * half]

        @pl.loop(0, out_ref.shape[0] // 2)
        def _(chip):
            out_ref[2 * chip + c] = piece


def spread(where_from, pivots, came, n_rows, mu, nu):
    k = came.shape[2]
    n = pivots.shape[0]
    vmem = pl.BlockSpec(memory_space=pltpu.VMEM)
    return pl.pallas_call(
        functools.partial(spread_kernel, mu=mu, nu=nu),
        out_shape=jax.ShapeDtypeStruct((n_rows, SLOTS, k // 2), BF16),
        in_specs=[pl.BlockSpec(memory_space=pltpu.SMEM), vmem, vmem],
        out_specs=vmem,
        compiler_params=pltpu.CompilerParams(vmem_limit_bytes=4 << 20),
        cost_estimate=pl.CostEstimate(
            flops=came.size, bytes_accessed=n_rows * SLOTS * k, transcendentals=0
        ),
        name="spread",
    )(where_from, pivots.reshape(1, n), came)


def preload_kernel(prev_ref, after_ref, out_ref, sems):
    copies = [
        pltpu.make_async_copy(prev_ref.at[m], out_ref.at[m], sems.at[m])
        for m in range(out_ref.shape[0])
    ]
    for copy in copies:
        copy.start()
    for copy in copies:
        copy.wait()


def preload(previous, count, after):
    shape = (count,) + previous.shape[1:]
    return pl.pallas_call(
        preload_kernel,
        out_shape=jax.ShapeDtypeStruct(shape, previous.dtype),
        in_specs=[pl.BlockSpec(memory_space=pltpu.HBM), pl.BlockSpec(memory_space=pl.ANY)],
        out_specs=pl.BlockSpec(memory_space=pltpu.VMEM),
        scratch_shapes=[pltpu.SemaphoreType.DMA((count,))],
        compiler_params=pltpu.CompilerParams(vmem_limit_bytes=4 << 20),
        cost_estimate=pl.CostEstimate(
            flops=0, bytes_accessed=previous.size, transcendentals=0
        ),
        name="preload",
    )(previous, after)


def vectors_kernel(
    core_ref, me_ref, cols_ref, first_ref, prev_ref, mine_ref, other_ref, inv_ref, orb_ref,
    new_ref, turned_ref, far_ref, came, made, load, store, far_sem, rows_ref, upper_ref, *, owners
):
    early, mu = first_ref.shape[0], cols_ref.shape[0]
    width = far_ref.shape[1]
    column = pl.multiple_of(lax.rem(me_ref[0] + owners // 2, owners) * width, width)
    far = pltpu.make_async_copy(orb_ref.at[:, pl.ds(column, width)], far_ref, far_sem)

    def load_of(i):
        return pltpu.make_async_copy(prev_ref.at[early + i], came.at[i], load.at[i])

    def store_of(m):
        return pltpu.make_async_copy(made.at[m], new_ref.at[m], store.at[m])

    def step(m, prev):
        contract = (((1,), (1,)), ((), ()))
        correction = lax.dot_general(prev, rows_ref[...], contract, preferred_element_type=F32)
        residual = (cols_ref[m].astype(F32) - correction).astype(BF16)
        new = jnp.dot(residual, upper_ref[...], preferred_element_type=F32).astype(BF16)
        made[m] = new
        store_of(m).start()
        turned_ref[m] = new.T

    for i in range(mu - early):
        load_of(i).start()
    far.start()
    mine, other = mine_ref[...].astype(F32), other_ref[...].astype(F32)
    first, half = core_ref[0] == 0, mine.shape[1]
    rows_ref[:, :half] = jnp.where(first, mine, other).astype(BF16)
    rows_ref[:, half:] = jnp.where(first, other, mine).astype(BF16)
    inv = inv_ref[...]
    row, column = (lax.broadcasted_iota(jnp.int32, inv.shape, d) for d in (0, 1))
    upper_ref[...] = jnp.where(row > column, 0.0, inv.astype(F32)).astype(BF16)

    @pl.loop(0, early)
    def _(m):
        step(m, first_ref[m])

    @pl.loop(0, mu - early)
    def _(i):
        load_of(i).wait()
        step(early + i, came[i])

    far.wait()
    for m in range(mu):
        store_of(m).wait()


def vectors(core, me, pivot_columns, first, previous, mine, other, pivot_inverse, orbitals, owners):
    mu, nu, k = previous.shape
    n = pivot_columns.shape[2]
    width = orbitals.shape[1] // owners
    smem = pl.BlockSpec(memory_space=pltpu.SMEM)
    vmem = pl.BlockSpec(memory_space=pltpu.VMEM)
    hbm = pl.BlockSpec(memory_space=pltpu.HBM)
    return pl.pallas_call(
        functools.partial(vectors_kernel, owners=owners),
        out_shape=(
            jax.ShapeDtypeStruct((mu, nu, n), BF16),
            jax.ShapeDtypeStruct((mu, n, nu), BF16),
            jax.ShapeDtypeStruct((nu, width), BF16),
        ),
        in_specs=[smem, smem, vmem, vmem, hbm, vmem, vmem, vmem, hbm],
        out_specs=(pl.BlockSpec(memory_space=pl.ANY), vmem, vmem),
        scratch_shapes=[
            pltpu.VMEM((mu - first.shape[0], nu, k), BF16),
            pltpu.VMEM((mu, nu, n), BF16),
            pltpu.SemaphoreType.DMA((mu - first.shape[0],)),
            pltpu.SemaphoreType.DMA((mu,)),
            pltpu.SemaphoreType.DMA,
            pltpu.VMEM((n, k), BF16),
            pltpu.VMEM((n, n), BF16),
        ],
        compiler_params=pltpu.CompilerParams(vmem_limit_bytes=24 << 20),
        cost_estimate=pl.CostEstimate(
            flops=2 * mu * nu * n * (k + n),
            bytes_accessed=2 * mu * nu * (k + 3 * n),
            transcendentals=0,
        ),
        name="vectors",
    )(core, me, pivot_columns, first, previous, mine, other, pivot_inverse, orbitals)


def bring_kernel(orb_ref, after_ref, out_ref, sems):
    count = sems.shape[0]
    rows = out_ref.shape[0] // count
    copies = [
        pltpu.make_async_copy(
            orb_ref.at[pl.ds(i * rows, rows)], out_ref.at[pl.ds(i * rows, rows)], sems.at[i]
        )
        for i in range(count)
    ]
    for copy in copies:
        copy.start()
    for copy in copies:
        copy.wait()


def bring(orbitals, after):
    return pl.pallas_call(
        bring_kernel,
        out_shape=jax.ShapeDtypeStruct(orbitals.shape, orbitals.dtype),
        in_specs=[pl.BlockSpec(memory_space=pltpu.HBM), pl.BlockSpec(memory_space=pl.ANY)],
        out_specs=pl.BlockSpec(memory_space=pltpu.VMEM),
        scratch_shapes=[pltpu.SemaphoreType.DMA((4,))],
        compiler_params=pltpu.CompilerParams(vmem_limit_bytes=4 << 20),
        cost_estimate=pl.CostEstimate(
            flops=0, bytes_accessed=2 * orbitals.size, transcendentals=0
        ),
        name="bring",
    )(orbitals, after)


def parts_kernel(me_ref, turned_ref, orb_ref, *out_refs, ahead, owners):
    mu, n, nu = turned_ref.shape
    keep, width = out_refs[0].shape[-2:]
    columns = [orb_ref[...]] if len(out_refs) == 2 else []
    for a in ahead[: 0 if columns else None]:
        start = pl.multiple_of(lax.rem(me_ref[0] + me_ref[1] * a + owners, owners) * width, width)
        columns.append(orb_ref[:, pl.ds(start, width)])
    columns = columns[0] if len(columns) == 1 else jnp.concatenate(columns, axis=1)
    for m in range(mu):
        part = jnp.dot(turned_ref[m], columns, preferred_element_type=F32)
        if len(out_refs) == 2:
            half = n // 2
            for h, out_ref in enumerate(out_refs):
                piece = part[h * half : (h + 1) * half].reshape(half // keep, keep, width)
                out_ref[:, m] = piece.astype(out_ref.dtype)
        else:
            for q in range(len(ahead)):
                piece = part[:, q * width : (q + 1) * width].reshape(n // keep, keep, width)
                out_refs[0][q, :, m] = piece


def parts(me, turned, orbitals, ahead, owners, dests, send=False):
    mu, n, nu = turned.shape
    width = orbitals.shape[1] // (1 if send else owners)
    if send:
        shape = (dests // 2, mu, n // dests, width)
        out_shape = (jax.ShapeDtypeStruct(shape, BF16),) * 2
    else:
        shape = (len(ahead), dests, mu, n // dests, width)
        out_shape = jax.ShapeDtypeStruct(shape, F32)
    vmem = pl.BlockSpec(memory_space=pltpu.VMEM)
    return pl.pallas_call(
        functools.partial(parts_kernel, ahead=ahead, owners=owners),
        out_shape=out_shape,
        in_specs=[pl.BlockSpec(memory_space=pltpu.SMEM), vmem, vmem],
        out_specs=(vmem, vmem) if send else vmem,
        compiler_params=pltpu.CompilerParams(vmem_limit_bytes=20 << 20),
        cost_estimate=pl.CostEstimate(
            flops=2 * mu * n * nu * width * len(ahead),
            bytes_accessed=2 * mu * n * nu,
            transcendentals=0,
        ),
        name="parts",
    )(me, turned, orbitals)


def join_kernel(own_ref, came_ref, out_ref, *, second):
    half = came_ref.shape[0]
    mine, other = (slice(half, None), slice(0, half)) if second else (slice(0, half), slice(half, None))
    out_ref[mine] = (own_ref[0, mine] + came_ref[...].astype(F32)).astype(BF16)
    out_ref[other] = own_ref[0, other].astype(BF16)


def join(part, which, came, second):
    shape = part.shape[1:]
    return pl.pallas_call(
        functools.partial(join_kernel, second=second),
        grid=(1,),
        out_shape=jax.ShapeDtypeStruct(shape, BF16),
        in_specs=[
            pl.BlockSpec((1,) + shape, lambda i: (which, 0, 0, 0, 0)),
            pl.BlockSpec(came.shape, lambda i: (0, 0, 0, 0)),
        ],
        out_specs=pl.BlockSpec(shape, lambda i: (0, 0, 0, 0)),
        compiler_params=pltpu.CompilerParams(vmem_limit_bytes=6 << 20),
        cost_estimate=pl.CostEstimate(
            flops=came.size, bytes_accessed=12 * came.size, transcendentals=0
        ),
        name="join",
    )(part, came)


def add_kernel(own_ref, came_ref, out_ref):
    out_ref[...] = (own_ref[0] + came_ref[...].astype(F32)).astype(BF16)


def add(part, which, came):
    shape = came.shape
    zeros = lambda i: (0, 0, 0, 0)
    return pl.pallas_call(
        add_kernel,
        grid=(1,),
        out_shape=jax.ShapeDtypeStruct(shape, BF16),
        in_specs=[
            pl.BlockSpec((1,) + shape, lambda i: (which, 0, 0, 0, 0)),
            pl.BlockSpec(shape, zeros),
        ],
        out_specs=pl.BlockSpec(shape, zeros),
        compiler_params=pltpu.CompilerParams(vmem_limit_bytes=6 << 20),
        cost_estimate=pl.CostEstimate(
            flops=came.size, bytes_accessed=8 * came.size, transcendentals=0
        ),
        name="add",
    )(part, came)


def reduce_to_owner(me, turned, columns, orbitals, owners, dests):
    far = owners // 2

    def hop(x, way):
        pairs = [
            (r * owners + g, r * owners + (g + (way if r % 2 == 0 else -way)) % owners)
            for r in range(dests)
            for g in range(owners)
        ]
        return lax.ppermute(x, ("rows", "grp"), pairs)

    right, left = parts(me, turned, columns, (far,), owners, dests, send=True)
    orbitals = bring(orbitals, right)
    right, left = hop(right, 1), hop(left, -1)

    def own(ahead):
        return parts(me, turned, orbitals, ahead, owners, dests)

    near = own((far - 1, far + 1))
    right, left = hop(join(near, 0, right, False), 1), hop(join(near, 1, left, True), -1)
    for ahead in range(far - 2, 0, -1):
        near = own((ahead, owners - ahead))
        right, left = (
            hop(add(near, q, x), way)
            for q, (x, way) in enumerate(((right, 1), (left, -1)))
        )
    return own((0,))[0] + right.astype(F32) + left.astype(F32)


def final_kernel(half_ref, slab_ref, out_ref, made, store):
    rows, width = half_ref.shape
    mu = slab_ref.shape[0]
    keep = rows // mu
    slab_t = slab_ref[...].T
    slab_t = jnp.concatenate([slab_t, slab_t], axis=1)

    def store_of(p):
        return pltpu.make_async_copy(made.at[pl.ds(p, 2)], out_ref.at[pl.ds(p, 2)], store.at[p // 2])

    for p in range(0, keep, 2):
        pair = jnp.concatenate(
            [half_ref[pl.ds(q, mu, stride=keep), :] for q in (p, p + 1)], axis=1
        )
        high = pair.astype(BF16)
        low = (pair - high.astype(F32)).astype(BF16)
        both = jnp.dot(slab_t, jnp.concatenate([high, low], axis=0), preferred_element_type=F32)
        made[p] = both[:, :width].astype(BF16)
        made[p + 1] = both[:, width:].astype(BF16)
        store_of(p).start()
    for p in range(0, keep, 2):
        store_of(p).wait()


def final(half, slab):
    mu, occ = slab.shape
    rows, width = half.shape
    keep = rows // mu
    vmem = pl.BlockSpec(memory_space=pltpu.VMEM)
    return pl.pallas_call(
        final_kernel,
        out_shape=jax.ShapeDtypeStruct((keep, occ, width), BF16),
        in_specs=[vmem, vmem],
        out_specs=pl.BlockSpec(memory_space=pl.ANY),
        scratch_shapes=[
            pltpu.VMEM((keep, occ, width), BF16),
            pltpu.SemaphoreType.DMA((keep // 2,)),
        ],
        compiler_params=pltpu.CompilerParams(vmem_limit_bytes=16 << 20),
        cost_estimate=pl.CostEstimate(
            flops=4 * rows * width * occ,
            bytes_accessed=2 * keep * width * (2 * mu + occ),
            transcendentals=0,
        ),
        name="final",
    )(half, slab)


def exchange(x, axis):
    return lax.all_to_all(x, axis, split_axis=0, concat_axis=0, tiled=True)


def pivot_halves(n_rows, n_grp, pivots, previous, columns):
    mu, nu, k = previous.shape
    n = pivots.shape[0]
    half = k // 2
    per_line = mu * NBAS
    line = lax.axis_index("rows") * per_line
    base = line + lax.axis_index("grp") * nu
    line, base = line.astype(jnp.int32), base.astype(jnp.int32)

    def one_round(index, so_far, columns=None):
        index = jnp.asarray(index, jnp.int32)
        turn, part = index // PARTS, index % PARTS
        where_from = jnp.stack([line, base, turn, part])
        picked, *close = pick_rows(where_from, pivots, previous, columns)
        came = exchange(jnp.broadcast_to(picked, (n_grp,) + picked.shape), "grp")
        messages = spread(where_from, pivots, came, n_rows, mu, nu)
        slots = exchange(messages, "rows").reshape(n_rows * SLOTS, half)
        rows, rounds = select_rows(index.reshape(1), pivots, slots, so_far, per_line, nu, n_grp)
        return rows, rounds, *close

    mine, rounds, close = one_round(0, jnp.zeros((n, half), BF16), columns)
    start, mine, rounds = lax.optimization_barrier((jnp.int32(1), mine, rounds))
    mine = lax.fori_loop(start, rounds[0], lambda i, rows: one_round(i, rows)[0], mine)
    other = lax.ppermute(mine, "rows", [(i, i ^ 1) for i in range(n_rows)])
    return mine, other, close


def per_device(n_rows, n_grp, pivot_columns, previous, pivots, pivot_inverse, orbitals, slab_orbitals):
    previous, pivot_columns, orbitals = (
        pltpu.with_memory_space_constraint(x, pltpu.HBM) for x in (previous, pivot_columns, orbitals)
    )
    mine, other, close = pivot_halves(n_rows, n_grp, pivots, previous, pivot_columns)
    core = (lax.axis_index("rows") % 2).reshape(1).astype(jnp.int32)
    way = 1 - 2 * (lax.axis_index("rows") % 2)
    me = jnp.stack([lax.axis_index("grp"), way]).astype(jnp.int32)
    first = preload(previous, previous.shape[0] // 2, mine)
    new_vectors, turned, far = vectors(
        core, me, close, first, previous, mine, other, pivot_inverse, orbitals, n_grp
    )
    half = exchange(reduce_to_owner(me, turned, far, orbitals, n_grp, n_rows), "rows")
    return new_vectors, final(half.reshape(-1, half.shape[-1]), slab_orbitals)


def solution(mesh):
    in_specs = (P("rows", "grp", None), P("rows", "grp", None), P(), P(), P("grp", None), P())
    out_specs = (P("rows", "grp", None), P("rows", None, "grp"))
    body = functools.partial(per_device, mesh.shape["rows"], mesh.shape["grp"])
    return jax.shard_map(body, mesh=mesh, in_specs=in_specs, out_specs=out_specs, check_vma=False)
```

```python
import functools

import jax
import jax.numpy as jnp
from jax import lax
from jax.experimental import pallas as pl
from jax.experimental.pallas import tpu as pltpu
from jax.sharding import PartitionSpec as P

NBAS = 10240
F32 = jnp.float32
BF16 = jnp.bfloat16
DEPTH = 8
SLOTS = 24
PARTS = 3


def pick_kernel(where_from_ref, piv_ref, prev_ref, *refs, bring):
    if bring:
        cols_ref, out_ref, close_ref, acc_ref, held, sems, rows_ref, close_sems = refs
        copies = [
            pltpu.make_async_copy(
                cols_ref.at[m, pl.ds(h * rows, rows)], close_ref.at[m, pl.ds(h * rows, rows)], close_sems.at[m, h]
            )
            for rows in (cols_ref.shape[1] // 2,)
            for m in range(cols_ref.shape[0])
            for h in range(2)
        ]
    else:
        out_ref, acc_ref, held, sems, rows_ref = refs
        copies = []
    for copy in copies:
        copy.start()
    mu, nu, _ = prev_ref.shape
    depth, group, _ = held.shape
    base, turn = where_from_ref[1], where_from_ref[2]
    acc_ref[...] = jnp.zeros_like(acc_ref)
    pivots = piv_ref[...]
    order = lax.broadcasted_iota(jnp.int32, pivots.shape, 0) * pivots.shape[1]
    order += lax.broadcasted_iota(jnp.int32, pivots.shape, 1)
    many = 1 << (mu * nu - 1).bit_length()
    last = many * pivots.size
    keys = jnp.full_like(pivots, last)
    for m in range(mu):
        inside = pivots - base - m * NBAS
        keys = jnp.where((inside >= 0) & (inside < nu), order * many + inside + m * nu, keys)
    owned = jnp.sum((keys < last).astype(jnp.int32))
    skip = turn * depth
    total = jnp.clip(owned - skip, 0, depth)

    def fetch(row, i):
        m = jnp.int32(0)
        for step in range(1, mu):
            m += (row >= step * nu).astype(jnp.int32)
        start = pl.multiple_of((row - m * nu) // group * group, group)
        return pltpu.make_async_copy(prev_ref.at[m, pl.ds(start, group)], held.at[i], sems.at[i])

    def find(i, key):
        key = jnp.min(jnp.where(keys > key, keys, last))

        @pl.when(i >= skip)
        def _():
            row = key & (many - 1)
            rows_ref[i - skip] = row
            fetch(row, i - skip).start()

        return key

    lax.fori_loop(0, skip + total, find, jnp.int32(-1))

    def place(i, _):
        row = rows_ref[i]
        fetch(row, i).wait()
        rows = held[i].astype(F32)
        keep = lax.broadcasted_iota(jnp.int32, rows.shape, 0) == row % group
        acc_ref[pl.ds(i, 1), :] = jnp.sum(jnp.where(keep, rows, 0.0), axis=0, keepdims=True)
        return 0

    lax.fori_loop(0, total, place, 0)
    out_ref[...] = acc_ref[...].astype(BF16)
    for copy in copies:
        copy.wait()


def pick_rows(where_from, pivots, previous, columns=None):
    n = pivots.shape[0]
    k = previous.shape[2]
    lanes = 128
    vmem = pl.BlockSpec(memory_space=pltpu.VMEM)
    hbm = pl.BlockSpec(memory_space=pltpu.HBM)
    args = [where_from, pivots.reshape(n // lanes, lanes), previous]
    out_shape = [jax.ShapeDtypeStruct((DEPTH, k), BF16)]
    scratch = [
        pltpu.VMEM((DEPTH, k), F32),
        pltpu.VMEM((DEPTH, 16, k), BF16),
        pltpu.SemaphoreType.DMA((DEPTH,)),
        pltpu.SMEM((DEPTH,), jnp.int32),
    ]
    bring = columns is not None
    if bring:
        args.append(columns)
        out_shape.append(jax.ShapeDtypeStruct(columns.shape, columns.dtype))
        scratch.append(pltpu.SemaphoreType.DMA((columns.shape[0], 2)))
    return pl.pallas_call(
        functools.partial(pick_kernel, bring=bring),
        out_shape=out_shape,
        in_specs=[pl.BlockSpec(memory_space=pltpu.SMEM), vmem, hbm] + [hbm] * bring,
        out_specs=[vmem] * len(out_shape),
        scratch_shapes=scratch,
        compiler_params=pltpu.CompilerParams(vmem_limit_bytes=4 << 20),
        cost_estimate=pl.CostEstimate(flops=n * k, bytes_accessed=2 * n * k, transcendentals=0),
        name="pick_rows",
    )(*args)


def whole_part(x, by):
    return jnp.floor((x + 0.5) * (1.0 / by))


def select_kernel(round_ref, piv_ref, slots_ref, so_far_ref, out_ref, rounds_ref, *, per_line, nu, owners):
    total, _ = slots_ref.shape
    n = piv_ref.shape[1]
    pivot = piv_ref[...].astype(F32)
    line = whole_part(pivot, per_line)
    inside = pivot - line * per_line
    inside = inside - whole_part(inside, NBAS) * NBAS
    device = jnp.broadcast_to(line * owners + whole_part(inside, nu), (n, n))
    mine = device.T
    before = lax.broadcasted_iota(jnp.int32, (n, n), 1) < lax.broadcasted_iota(jnp.int32, (n, n), 0)
    rank = jnp.sum(jnp.where((device == mine) & before, 1.0, 0.0), axis=1, keepdims=True)
    turn = whole_part(rank, DEPTH)
    turns = jnp.broadcast_to(turn, (n, n))
    my_line = whole_part(mine, owners)
    ahead = (device >= my_line * owners) & (device < mine) & (turns.T == turns)
    place = jnp.sum(jnp.where(ahead, 1.0, 0.0), axis=1, keepdims=True) + rank - turn * DEPTH
    part = whole_part(place, SLOTS)
    when = turn * PARTS + part
    rounds_ref[0] = jnp.max(when).astype(jnp.int32) + 1
    index = my_line[:, :1] * SLOTS + place - part * SLOTS
    index = jnp.where(when == round_ref[0].astype(F32), index, -1.0).astype(jnp.int32)
    hot = index == lax.broadcasted_iota(jnp.int32, (n, total), 1)
    hot = jnp.where(hot, 1.0, 0.0).astype(BF16)
    picked = jnp.dot(hot, slots_ref[...], preferred_element_type=F32)
    out_ref[...] = (picked + so_far_ref[...].astype(F32)).astype(BF16)


def select_rows(round_index, pivots, slots, so_far, per_line, nu, owners):
    total, width = slots.shape
    n = pivots.shape[0]
    vmem = pl.BlockSpec(memory_space=pltpu.VMEM)
    return pl.pallas_call(
        functools.partial(select_kernel, per_line=per_line, nu=nu, owners=owners),
        out_shape=(
            jax.ShapeDtypeStruct((n, width), BF16),
            jax.ShapeDtypeStruct((1,), jnp.int32),
        ),
        in_specs=[pl.BlockSpec(memory_space=pltpu.SMEM), vmem, vmem, vmem],
        out_specs=(vmem, pl.BlockSpec(memory_space=pltpu.SMEM)),
        compiler_params=pltpu.CompilerParams(vmem_limit_bytes=8 << 20),
        cost_estimate=pl.CostEstimate(
            flops=2 * n * total * width, bytes_accessed=2 * total * width, transcendentals=0
        ),
        name="select_rows",
    )(round_index, pivots.reshape(1, n), slots, so_far)


def spread_kernel(where_from_ref, piv_ref, came_ref, out_ref, *, mu, nu):
    owners, depth, k = came_ref.shape
    n = piv_ref.shape[1]
    line, turn, part = (where_from_ref[i] for i in (0, 2, 3))
    offset = jnp.broadcast_to(piv_ref[...] - line, (owners, n))
    low = lax.broadcasted_iota(jnp.int32, (owners, n), 0) * nu
    count = jnp.zeros((owners, n), F32)
    for m in range(mu):
        inside = offset - m * NBAS - low
        count += jnp.where((inside >= 0) & (inside < nu), 1.0, 0.0)
    count = jnp.sum(count, axis=1, keepdims=True) - (turn * depth).astype(F32)
    count = jnp.clip(count, 0.0, depth)
    wide = (owners, owners * depth)
    slot = lax.broadcasted_iota(jnp.int32, wide, 1) - lax.broadcasted_iota(jnp.int32, wide, 0) * depth
    here = (slot >= 0) & (slot < depth)
    start = jnp.sum(jnp.where(slot >= depth, count, 0.0), axis=0, keepdims=True)
    used = jnp.sum(jnp.where(here & (slot.astype(F32) < count), 1.0, 0.0), axis=0, keepdims=True)
    place = start + jnp.sum(jnp.where(here, slot.astype(F32), 0.0), axis=0, keepdims=True)
    place = place - (part * SLOTS).astype(F32)
    packed = lax.broadcasted_iota(jnp.int32, (SLOTS, wide[1]), 0).astype(F32)
    hot = jnp.where((packed == place) & (used > 0.0), 1.0, 0.0).astype(BF16)
    rows = came_ref[...].astype(F32).reshape(wide[1], k).astype(BF16)
    rows = jnp.dot(hot, rows, preferred_element_type=F32).astype(BF16)
    half = out_ref.shape[2]
    for c in range(2):
        piece = rows[:, c * half : (c + 1) * half]

        @pl.loop(0, out_ref.shape[0] // 2)
        def _(chip):
            out_ref[2 * chip + c] = piece


def spread(where_from, pivots, came, n_rows, mu, nu):
    k = came.shape[2]
    n = pivots.shape[0]
    vmem = pl.BlockSpec(memory_space=pltpu.VMEM)
    return pl.pallas_call(
        functools.partial(spread_kernel, mu=mu, nu=nu),
        out_shape=jax.ShapeDtypeStruct((n_rows, SLOTS, k // 2), BF16),
        in_specs=[pl.BlockSpec(memory_space=pltpu.SMEM), vmem, vmem],
        out_specs=vmem,
        compiler_params=pltpu.CompilerParams(vmem_limit_bytes=4 << 20),
        cost_estimate=pl.CostEstimate(
            flops=came.size, bytes_accessed=n_rows * SLOTS * k, transcendentals=0
        ),
        name="spread",
    )(where_from, pivots.reshape(1, n), came)


def preload_kernel(prev_ref, after_ref, out_ref, sems):
    copies = [
        pltpu.make_async_copy(prev_ref.at[m], out_ref.at[m], sems.at[m])
        for m in range(out_ref.shape[0])
    ]
    for copy in copies:
        copy.start()
    for copy in copies:
        copy.wait()


def preload(previous, count, after):
    shape = (count,) + previous.shape[1:]
    return pl.pallas_call(
        preload_kernel,
        out_shape=jax.ShapeDtypeStruct(shape, previous.dtype),
        in_specs=[pl.BlockSpec(memory_space=pltpu.HBM), pl.BlockSpec(memory_space=pl.ANY)],
        out_specs=pl.BlockSpec(memory_space=pltpu.VMEM),
        scratch_shapes=[pltpu.SemaphoreType.DMA((count,))],
        compiler_params=pltpu.CompilerParams(vmem_limit_bytes=4 << 20),
        cost_estimate=pl.CostEstimate(
            flops=0, bytes_accessed=previous.size, transcendentals=0
        ),
        name="preload",
    )(previous, after)


def vectors_kernel(
    core_ref, me_ref, cols_ref, first_ref, prev_ref, mine_ref, other_ref, inv_ref, orb_ref,
    new_ref, turned_ref, far_ref, came, made, load, store, far_sem, rows_ref, upper_ref, *, owners
):
    early, mu = first_ref.shape[0], cols_ref.shape[0]
    width = far_ref.shape[1]
    column = pl.multiple_of(lax.rem(me_ref[0] + owners // 2, owners) * width, width)
    far = pltpu.make_async_copy(orb_ref.at[:, pl.ds(column, width)], far_ref, far_sem)

    def load_of(i):
        return pltpu.make_async_copy(prev_ref.at[early + i], came.at[i], load.at[i])

    def store_of(m):
        return pltpu.make_async_copy(made.at[m], new_ref.at[m], store.at[m])

    def step(m, prev):
        contract = (((1,), (1,)), ((), ()))
        correction = lax.dot_general(prev, rows_ref[...], contract, preferred_element_type=F32)
        residual = (cols_ref[m].astype(F32) - correction).astype(BF16)
        new = jnp.dot(residual, upper_ref[...], preferred_element_type=F32).astype(BF16)
        made[m] = new
        store_of(m).start()
        turned_ref[m] = new.T

    for i in range(mu - early):
        load_of(i).start()
    far.start()
    mine, other = mine_ref[...].astype(F32), other_ref[...].astype(F32)
    first, half = core_ref[0] == 0, mine.shape[1]
    rows_ref[:, :half] = jnp.where(first, mine, other).astype(BF16)
    rows_ref[:, half:] = jnp.where(first, other, mine).astype(BF16)
    inv = inv_ref[...]
    row, column = (lax.broadcasted_iota(jnp.int32, inv.shape, d) for d in (0, 1))
    upper_ref[...] = jnp.where(row > column, 0.0, inv.astype(F32)).astype(BF16)

    @pl.loop(0, early)
    def _(m):
        step(m, first_ref[m])

    @pl.loop(0, mu - early)
    def _(i):
        load_of(i).wait()
        step(early + i, came[i])

    far.wait()
    for m in range(mu):
        store_of(m).wait()


def vectors(core, me, pivot_columns, first, previous, mine, other, pivot_inverse, orbitals, owners):
    mu, nu, k = previous.shape
    n = pivot_columns.shape[2]
    width = orbitals.shape[1] // owners
    smem = pl.BlockSpec(memory_space=pltpu.SMEM)
    vmem = pl.BlockSpec(memory_space=pltpu.VMEM)
    hbm = pl.BlockSpec(memory_space=pltpu.HBM)
    return pl.pallas_call(
        functools.partial(vectors_kernel, owners=owners),
        out_shape=(
            jax.ShapeDtypeStruct((mu, nu, n), BF16),
            jax.ShapeDtypeStruct((mu, n, nu), BF16),
            jax.ShapeDtypeStruct((nu, width), BF16),
        ),
        in_specs=[smem, smem, vmem, vmem, hbm, vmem, vmem, vmem, hbm],
        out_specs=(pl.BlockSpec(memory_space=pl.ANY), vmem, vmem),
        scratch_shapes=[
            pltpu.VMEM((mu - first.shape[0], nu, k), BF16),
            pltpu.VMEM((mu, nu, n), BF16),
            pltpu.SemaphoreType.DMA((mu - first.shape[0],)),
            pltpu.SemaphoreType.DMA((mu,)),
            pltpu.SemaphoreType.DMA,
            pltpu.VMEM((n, k), BF16),
            pltpu.VMEM((n, n), BF16),
        ],
        compiler_params=pltpu.CompilerParams(vmem_limit_bytes=24 << 20),
        cost_estimate=pl.CostEstimate(
            flops=2 * mu * nu * n * (k + n),
            bytes_accessed=2 * mu * nu * (k + 3 * n),
            transcendentals=0,
        ),
        name="vectors",
    )(core, me, pivot_columns, first, previous, mine, other, pivot_inverse, orbitals)


def bring_kernel(orb_ref, after_ref, out_ref, sems):
    count = sems.shape[0]
    rows = out_ref.shape[0] // count
    copies = [
        pltpu.make_async_copy(
            orb_ref.at[pl.ds(i * rows, rows)], out_ref.at[pl.ds(i * rows, rows)], sems.at[i]
        )
        for i in range(count)
    ]
    for copy in copies:
        copy.start()
    for copy in copies:
        copy.wait()


def bring(orbitals, after):
    return pl.pallas_call(
        bring_kernel,
        out_shape=jax.ShapeDtypeStruct(orbitals.shape, orbitals.dtype),
        in_specs=[pl.BlockSpec(memory_space=pltpu.HBM), pl.BlockSpec(memory_space=pl.ANY)],
        out_specs=pl.BlockSpec(memory_space=pltpu.VMEM),
        scratch_shapes=[pltpu.SemaphoreType.DMA((4,))],
        compiler_params=pltpu.CompilerParams(vmem_limit_bytes=4 << 20),
        cost_estimate=pl.CostEstimate(
            flops=0, bytes_accessed=2 * orbitals.size, transcendentals=0
        ),
        name="bring",
    )(orbitals, after)


def parts_kernel(me_ref, turned_ref, orb_ref, *out_refs, ahead, owners):
    mu, n, nu = turned_ref.shape
    keep, width = out_refs[0].shape[-2:]
    columns = [orb_ref[...]] if len(out_refs) == 2 else []
    for a in ahead[: 0 if columns else None]:
        start = pl.multiple_of(lax.rem(me_ref[0] + a, owners) * width, width)
        columns.append(orb_ref[:, pl.ds(start, width)])
    columns = columns[0] if len(columns) == 1 else jnp.concatenate(columns, axis=1)
    for m in range(mu):
        part = jnp.dot(turned_ref[m], columns, preferred_element_type=F32)
        if len(out_refs) == 2:
            half = n // 2
            for h, out_ref in enumerate(out_refs):
                piece = part[h * half : (h + 1) * half].reshape(half // keep, keep, width)
                out_ref[:, m] = piece.astype(out_ref.dtype)
        else:
            for q in range(len(ahead)):
                piece = part[:, q * width : (q + 1) * width].reshape(n // keep, keep, width)
                out_refs[0][q, :, m] = piece


def parts(me, turned, orbitals, ahead, owners, dests, send=False):
    mu, n, nu = turned.shape
    width = orbitals.shape[1] // (1 if send else owners)
    if send:
        shape = (dests // 2, mu, n // dests, width)
        out_shape = (jax.ShapeDtypeStruct(shape, BF16),) * 2
    else:
        shape = (len(ahead), dests, mu, n // dests, width)
        out_shape = jax.ShapeDtypeStruct(shape, F32)
    vmem = pl.BlockSpec(memory_space=pltpu.VMEM)
    return pl.pallas_call(
        functools.partial(parts_kernel, ahead=ahead, owners=owners),
        out_shape=out_shape,
        in_specs=[pl.BlockSpec(memory_space=pltpu.SMEM), vmem, vmem],
        out_specs=(vmem, vmem) if send else vmem,
        compiler_params=pltpu.CompilerParams(vmem_limit_bytes=20 << 20),
        cost_estimate=pl.CostEstimate(
            flops=2 * mu * n * nu * width * len(ahead),
            bytes_accessed=2 * mu * n * nu,
            transcendentals=0,
        ),
        name="parts",
    )(me, turned, orbitals)


def join_kernel(own_ref, came_ref, out_ref, *, second):
    half = came_ref.shape[0]
    mine, other = (slice(half, None), slice(0, half)) if second else (slice(0, half), slice(half, None))
    out_ref[mine] = (own_ref[0, mine] + came_ref[...].astype(F32)).astype(BF16)
    out_ref[other] = own_ref[0, other].astype(BF16)


def join(part, which, came, second):
    shape = part.shape[1:]
    return pl.pallas_call(
        functools.partial(join_kernel, second=second),
        grid=(1,),
        out_shape=jax.ShapeDtypeStruct(shape, BF16),
        in_specs=[
            pl.BlockSpec((1,) + shape, lambda i: (which, 0, 0, 0, 0)),
            pl.BlockSpec(came.shape, lambda i: (0, 0, 0, 0)),
        ],
        out_specs=pl.BlockSpec(shape, lambda i: (0, 0, 0, 0)),
        compiler_params=pltpu.CompilerParams(vmem_limit_bytes=6 << 20),
        cost_estimate=pl.CostEstimate(
            flops=came.size, bytes_accessed=12 * came.size, transcendentals=0
        ),
        name="join",
    )(part, came)


def add_kernel(own_ref, came_ref, out_ref):
    out_ref[...] = (own_ref[0] + came_ref[...].astype(F32)).astype(BF16)


def add(part, which, came):
    shape = came.shape
    zeros = lambda i: (0, 0, 0, 0)
    return pl.pallas_call(
        add_kernel,
        grid=(1,),
        out_shape=jax.ShapeDtypeStruct(shape, BF16),
        in_specs=[
            pl.BlockSpec((1,) + shape, lambda i: (which, 0, 0, 0, 0)),
            pl.BlockSpec(shape, zeros),
        ],
        out_specs=pl.BlockSpec(shape, zeros),
        compiler_params=pltpu.CompilerParams(vmem_limit_bytes=6 << 20),
        cost_estimate=pl.CostEstimate(
            flops=came.size, bytes_accessed=8 * came.size, transcendentals=0
        ),
        name="add",
    )(part, came)


def reduce_to_owner(me, turned, columns, orbitals, owners, dests):
    far = owners // 2

    def hop(x, way):
        return lax.ppermute(x, "grp", [(i, (i + way) % owners) for i in range(owners)])

    right, left = parts(me, turned, columns, (far,), owners, dests, send=True)
    orbitals = bring(orbitals, right)
    right, left = hop(right, 1), hop(left, -1)

    def own(ahead):
        return parts(me, turned, orbitals, ahead, owners, dests)

    near = own((far - 1, far + 1))
    right, left = hop(join(near, 0, right, False), 1), hop(join(near, 1, left, True), -1)
    for ahead in range(far - 2, 0, -1):
        near = own((ahead, owners - ahead))
        right, left = (
            hop(add(near, q, x), way)
            for q, (x, way) in enumerate(((right, 1), (left, -1)))
        )
    return own((0,))[0] + right.astype(F32) + left.astype(F32)


def final_kernel(half_ref, slab_ref, out_ref, made, store):
    rows, width = half_ref.shape
    mu = slab_ref.shape[0]
    keep = rows // mu
    slab_t = slab_ref[...].T
    slab_t = jnp.concatenate([slab_t, slab_t], axis=1)

    def store_of(p):
        return pltpu.make_async_copy(made.at[pl.ds(p, 2)], out_ref.at[pl.ds(p, 2)], store.at[p // 2])

    for p in range(0, keep, 2):
        pair = jnp.concatenate(
            [half_ref[pl.ds(q, mu, stride=keep), :] for q in (p, p + 1)], axis=1
        )
        high = pair.astype(BF16)
        low = (pair - high.astype(F32)).astype(BF16)
        both = jnp.dot(slab_t, jnp.concatenate([high, low], axis=0), preferred_element_type=F32)
        made[p] = both[:, :width].astype(BF16)
        made[p + 1] = both[:, width:].astype(BF16)
        store_of(p).start()
    for p in range(0, keep, 2):
        store_of(p).wait()


def final(half, slab):
    mu, occ = slab.shape
    rows, width = half.shape
    keep = rows // mu
    vmem = pl.BlockSpec(memory_space=pltpu.VMEM)
    return pl.pallas_call(
        final_kernel,
        out_shape=jax.ShapeDtypeStruct((keep, occ, width), BF16),
        in_specs=[vmem, vmem],
        out_specs=pl.BlockSpec(memory_space=pl.ANY),
        scratch_shapes=[
            pltpu.VMEM((keep, occ, width), BF16),
            pltpu.SemaphoreType.DMA((keep // 2,)),
        ],
        compiler_params=pltpu.CompilerParams(vmem_limit_bytes=16 << 20),
        cost_estimate=pl.CostEstimate(
            flops=4 * rows * width * occ,
            bytes_accessed=2 * keep * width * (2 * mu + occ),
            transcendentals=0,
        ),
        name="final",
    )(half, slab)


def exchange(x, axis):
    return lax.all_to_all(x, axis, split_axis=0, concat_axis=0, tiled=True)


def pivot_halves(n_rows, n_grp, pivots, previous, columns):
    mu, nu, k = previous.shape
    n = pivots.shape[0]
    half = k // 2
    per_line = mu * NBAS
    line = lax.axis_index("rows") * per_line
    base = line + lax.axis_index("grp") * nu
    line, base = line.astype(jnp.int32), base.astype(jnp.int32)

    def one_round(index, so_far, columns=None):
        index = jnp.asarray(index, jnp.int32)
        turn, part = index // PARTS, index % PARTS
        where_from = jnp.stack([line, base, turn, part])
        picked, *close = pick_rows(where_from, pivots, previous, columns)
        came = exchange(jnp.broadcast_to(picked, (n_grp,) + picked.shape), "grp")
        messages = spread(where_from, pivots, came, n_rows, mu, nu)
        slots = exchange(messages, "rows").reshape(n_rows * SLOTS, half)
        rows, rounds = select_rows(index.reshape(1), pivots, slots, so_far, per_line, nu, n_grp)
        return rows, rounds, *close

    mine, rounds, close = one_round(0, jnp.zeros((n, half), BF16), columns)
    start, mine, rounds = lax.optimization_barrier((jnp.int32(1), mine, rounds))
    mine = lax.fori_loop(start, rounds[0], lambda i, rows: one_round(i, rows)[0], mine)
    other = lax.ppermute(mine, "rows", [(i, i ^ 1) for i in range(n_rows)])
    return mine, other, close


def per_device(n_rows, n_grp, pivot_columns, previous, pivots, pivot_inverse, orbitals, slab_orbitals):
    previous, pivot_columns, orbitals = (
        pltpu.with_memory_space_constraint(x, pltpu.HBM) for x in (previous, pivot_columns, orbitals)
    )
    mine, other, close = pivot_halves(n_rows, n_grp, pivots, previous, pivot_columns)
    core = (lax.axis_index("rows") % 2).reshape(1).astype(jnp.int32)
    me = lax.axis_index("grp").reshape(1).astype(jnp.int32)
    first = preload(previous, previous.shape[0] // 2, mine)
    new_vectors, turned, far = vectors(
        core, me, close, first, previous, mine, other, pivot_inverse, orbitals, n_grp
    )
    half = exchange(reduce_to_owner(me, turned, far, orbitals, n_grp, n_rows), "rows")
    return new_vectors, final(half.reshape(-1, half.shape[-1]), slab_orbitals)


def solution(mesh):
    in_specs = (P("rows", "grp", None), P("rows", "grp", None), P(), P(), P("grp", None), P())
    out_specs = (P("rows", "grp", None), P("rows", None, "grp"))
    body = functools.partial(per_device, mesh.shape["rows"], mesh.shape["grp"])
    return jax.shard_map(body, mesh=mesh, in_specs=in_specs, out_specs=out_specs, check_vma=False)
```
